32 devices in a mesh: dp: 16 (over z, x, core), seq: 2 (over y).
Axes of the slice: x: 2, y: 2, z: 4, core: 2. Of those that a mesh axis runs over, the one named last changes fastest.
Arguments:
- tokens: bfloat16 [24576, 768], P(('dp', 'seq')), may hold values from -7 to 7
- entity_flags: int32 [24576], P(('dp', 'seq')), may hold values 0 or 1
- query_weight: bfloat16 [4, 768, 768], P(None, 'dp'), may hold values from -0.21875 to 0.21875
- key_weight: bfloat16 [768, 768], P('dp'), may hold values from -0.21875 to 0.21875
- value_weight: bfloat16 [768, 768], P('dp'), may hold values from -0.21875 to 0.21875
- mixing_weight: bfloat16 [768, 768], P('dp'), may hold values from -4 to 4
- mixing_bias: bfloat16 [768], P('dp'), may hold values from -4 to 4
- first_gain: bfloat16 [768], P('dp'), may hold values from 0.5 to 1.5
- first_bias: bfloat16 [768], P('dp'), may hold values from -4 to 4
- up_weight: bfloat16 [768, 3072], P('dp'), may hold values from -0.21875 to 0.21875
- up_bias: bfloat16 [3072], P('dp'), may hold values from -4 to 4
- down_weight: bfloat16 [3072, 768], P('dp'), may hold values from -0.109375 to 0.109375
- down_bias: bfloat16 [768], P('dp'), may hold values from -4 to 4
- second_gain: bfloat16 [768], P('dp'), may hold values from 0.5 to 1.5
- second_bias: bfloat16 [768], P('dp'), may hold values from -4 to 4
- cotangent: bfloat16 [24576, 768], P(('dp', 'seq')), may hold values from -6 to 6
Outputs:
- layer_out: bfloat16 [24576, 768], P(('dp', 'seq'))
- tokens_grad: bfloat16 [24576, 768], P(('dp', 'seq'))
- query_grad: float32 [4, 768, 768], P(None, 'dp')
- key_grad: float32 [768, 768], P('dp')
- value_grad: float32 [768, 768], P('dp')
- mixing_grad: float32 [768, 768], P('dp')
- mixing_bias_grad: float32 [768], P('dp')
- first_gain_grad: float32 [768], P('dp')
- first_bias_grad: float32 [768], P('dp')
- up_grad: float32 [768, 3072], P('dp')
- up_bias_grad: float32 [3072], P('dp')
- down_grad: float32 [3072, 768], P('dp')
- down_bias_grad: float32 [768], P('dp')
- second_gain_grad: float32 [768], P('dp')
- second_bias_grad: float32 [768], P('dp')
- stream_rms: float32 [3], replicated
The draws below stay inside these ranges and needn't reach their ends.
All inputs are finite; a program needn't handle non-finite values. No bound on the sum of `entity_flags` on one device may be relied on, other than what follows from the above.
Results may differ from the reference program's by a relative error of at most 0.015.
Values may be sent and summed in bfloat16 or wider, within the bound.
No kernel may reach another device: no remote copies, remote signals or barrier semaphores. Data moves between devices by JAX's collectives and lax.ppermute only.
A program may use at most 192 MiB of HBM per device.

```python
import jax
import jax.numpy as jnp
from jax import lax

D = 768
HEADS = 12
HD = 64
FF = 3072
SEQ_LEN = 1536
TOKENS = 24576


def draw_tokens(key, part):
    sequence_ids = jnp.arange(TOKENS) // SEQ_LEN
    seq_count = TOKENS // SEQ_LEN
    level = sequence_ids.astype(jnp.float32) / max(seq_count - 1, 1)
    factor = jnp.sqrt(1.0 + 2.0 * level)[:, None]
    base = jnp.clip(jax.random.normal(key, (TOKENS, D), jnp.float32), -4.0, 4.0)
    return (base * factor).astype(jnp.bfloat16)


def set_ends(values, key, low, high):
    index_at = [jax.random.randint(jax.random.fold_in(key, axis), (), 0, length) for axis, length in enumerate(values.shape)]
    widest = values.shape.index(max(values.shape))
    next_to = index_at[:widest] + [(index_at[widest] + 1) % values.shape[widest]] + index_at[widest + 1:]
    return values.at[tuple(index_at)].set(low).at[tuple(next_to)].set(high)


def levels(key, dims, split, low, high):
    def one(dim, blocks):
        heights = jax.random.uniform(jax.random.fold_in(jax.random.fold_in(key, 6), dim), (blocks,), jnp.float32, low / len(split), high / len(split))
        return jnp.repeat(jnp.exp(heights), dims[dim] // blocks).reshape((-1,) + (1,) * (len(dims) - dim - 1))

    level = one(*split[0])
    for cut in split[1:]:
        level = level * one(*cut)
    return level


def gaussian(stream_key, dims, scale, limit, pieces=(), kind=jnp.bfloat16):
    factor_of = levels(stream_key, dims, pieces, -0.22, 0.18) if pieces else 1.0
    drawn = jax.random.normal(stream_key, dims, jnp.float32) * scale * factor_of
    return jnp.minimum(jnp.maximum(drawn, -limit), limit).astype(kind)


def setup_inputs(seed: int = 0) -> dict:
    key_of = jax.random.split(jax.random.key(seed), 17)
    return {
        "tokens": draw_tokens(jax.random.fold_in(key_of[16], 71), 0),
        "entity_flags": set_ends((jax.random.randint(key_of[1], (TOKENS,), 0, 4) < 1).astype(jnp.int32), jax.random.fold_in(key_of[1], 1), 0, 1),
        "query_weight": gaussian(key_of[2], (4, D, D), D ** -0.5, 0.21875, ((1, 16),)),
        "key_weight": gaussian(key_of[3], (D, D), D ** -0.5, 0.21875, ((0, 16),)),
        "value_weight": gaussian(key_of[4], (D, D), D ** -0.5, 0.21875, ((0, 16),)),
        "mixing_weight": gaussian(key_of[5], (D, D), (max(D // 384, 1)) ** -0.5, 4.0, ((0, 16),)),
        "mixing_bias": gaussian(key_of[6], (D,), 0.3, 4.0, ((0, 16),)),
        "first_gain": jnp.clip(1.0 + 0.1 * jax.random.normal(key_of[7], (D,), jnp.float32), 0.5, 1.5).astype(jnp.bfloat16),
        "first_bias": gaussian(key_of[8], (D,), 0.3, 4.0, ((0, 16),)),
        "up_weight": gaussian(key_of[9], (D, FF), D ** -0.5, 0.21875, ((0, 16),)),
        "up_bias": gaussian(key_of[10], (FF,), 0.3, 4.0, ((0, 16),)),
        "down_weight": gaussian(key_of[11], (FF, D), FF ** -0.5, 0.109375, ((0, 16),)),
        "down_bias": gaussian(key_of[12], (D,), 0.3, 4.0, ((0, 16),)),
        "second_gain": jnp.clip(1.0 + 0.1 * jax.random.normal(key_of[13], (D,), jnp.float32), 0.5, 1.5).astype(jnp.bfloat16),
        "second_bias": gaussian(key_of[14], (D,), 0.3, 4.0, ((0, 16),)),
        "cotangent": gaussian(key_of[15], (TOKENS, D), 1.0, 6.0, ((0, 32),)),
    }


@jax.custom_vjp
def low(v):
    return lax.optimization_barrier(v.astype(jnp.bfloat16)).astype(jnp.float32)

@jax.custom_vjp
def low_back(v):
    return v

def low_keep(v):
    return (low(v), None)

def low_pass(kept, grad):
    return (grad,)

def back_keep(v):
    return (v, None)

def back_low(kept, grad):
    return (low(grad),)
low.defvjp(low_keep, low_pass)
low_back.defvjp(back_keep, back_low)
epsilon = 1e-05

def rounded_both(value):
    return low_back(low(value))

def matmul(left, right):
    return jnp.dot(left, right, precision=lax.Precision.HIGHEST)

def layer_norm(value, gain, shift):
    center = value - lax.optimization_barrier(jnp.mean(value, axis=-1, keepdims=True))
    spread = lax.optimization_barrier(jnp.mean(center * center, axis=-1, keepdims=True))
    return center * lax.rsqrt(spread + epsilon) * gain + shift

def gelu_exact(value):
    return 0.5 * value * (1.0 + lax.erf(value * 0.7071067811865476))

def sequence_layer(params, tokens, entity_flags):
    query_weight, key_weight, value_weight, mixing_weight, mixing_bias, first_gain, first_bias, up_weight, up_bias, down_weight, down_bias, second_gain, second_bias = params
    length = tokens.shape[0]
    entity = entity_flags.astype(jnp.float32)[:, None]
    wordly = 1.0 - entity
    projected = [matmul(tokens, query_weight[matrix_index]) for matrix_index in range(4)]
    to_word = wordly * projected[0] + entity * projected[2]
    to_entity = wordly * projected[1] + entity * projected[3]
    key_rows = matmul(tokens, key_weight)
    queries = rounded_both(jnp.concatenate([to_word.reshape(length, HEADS, HD), to_entity.reshape(length, HEADS, HD)], axis=2))
    keys_masked = rounded_both(jnp.concatenate([(wordly * key_rows).reshape(length, HEADS, HD), (entity * key_rows).reshape(length, HEADS, HD)], axis=2))
    values = rounded_both(matmul(tokens, value_weight)).reshape(length, HEADS, HD)
    scores = low_back(HD ** (-0.5) * jnp.einsum('qhc,khc->hqk', queries, keys_masked, precision=lax.Precision.HIGHEST))
    highest = lax.optimization_barrier(jnp.max(scores, axis=-1, keepdims=True))
    weights = jnp.exp(scores - highest)
    attention = weights / lax.optimization_barrier(jnp.sum(weights, axis=-1, keepdims=True))
    mixture = rounded_both(jnp.einsum('hqk,khc->qhc', low(attention), values, precision=lax.Precision.HIGHEST)).reshape(length, D)
    attention_out = low_back(matmul(mixture, mixing_weight) + mixing_bias)
    stream = tokens + attention_out
    hidden = layer_norm(stream, first_gain, first_bias)
    before = low_back(matmul(low(hidden), up_weight) + up_bias)
    active = low(gelu_exact(before))
    forward_out = low_back(matmul(active, down_weight) + down_bias)
    output = layer_norm(hidden + forward_out, second_gain, second_bias)
    squares = jnp.stack([jnp.sum(stream * stream), jnp.sum(attention_out * attention_out), jnp.sum(forward_out * forward_out)])
    return (output, squares)

def reference(tokens, entity_flags, query_weight, key_weight, value_weight, mixing_weight, mixing_bias, first_gain, first_bias, up_weight, up_bias, down_weight, down_bias, second_gain, second_bias, cotangent):
    params = tuple((weight.astype(jnp.float32) for weight in (query_weight, key_weight, value_weight, mixing_weight, mixing_bias, first_gain, first_bias, up_weight, up_bias, down_weight, down_bias, second_gain, second_bias)))
    seq_count = TOKENS // SEQ_LEN
    token_rows = tokens.astype(jnp.float32).reshape(seq_count, SEQ_LEN, D)
    flag_rows = entity_flags.reshape(seq_count, SEQ_LEN)

    def forward(params_in, rows_in):

        def one_sequence(member):
            return sequence_layer(params_in, member[0], member[1])
        return lax.map(jax.checkpoint(one_sequence), (rows_in, flag_rows))
    (outputs, squares), pullback = jax.vjp(forward, params, token_rows)
    param_grads, token_grads = pullback((cotangent.astype(jnp.float32).reshape(seq_count, SEQ_LEN, D), jnp.zeros_like(squares)))
    totals = lax.optimization_barrier(jnp.sum(squares, axis=0))
    stream_rms = jnp.sqrt(totals / (TOKENS * D))
    return (outputs.reshape(TOKENS, D).astype(jnp.bfloat16), token_grads.reshape(TOKENS, D).astype(jnp.bfloat16), param_grads[0], param_grads[1], param_grads[2], param_grads[3], param_grads[4], param_grads[5], param_grads[6], param_grads[7], param_grads[8], param_grads[9], param_grads[10], param_grads[11], param_grads[12], stream_rms)
```

```python
import functools

import jax
import jax.numpy as jnp
from jax import lax
from jax.experimental import pallas as pl
from jax.experimental.pallas import tpu as pltpu
from jax.sharding import PartitionSpec as P

D = 768
HEADS = 12
HD = 64
PAIRS = HEADS // 2
LANES = 2 * HD
F32 = jnp.float32
BF = jnp.bfloat16
EPSILON = 1e-05
LN2 = 0.6931471805599453
QUERY_SCALE = HD**-0.5 / LN2
FORWARD_GROUPS = (1, 1, 2, 2)
VMEM_LIMIT = 58 * 1024 * 1024


def dot(left, right):
    return jnp.dot(left, right, preferred_element_type=F32)


def dot_rt(left, right):
    return lax.dot_general(left, right, (((1,), (1,)), ((), ())), preferred_element_type=F32)


def dot_lt(left, right):
    return lax.dot_general(left, right, (((0,), (0,)), ((), ())), preferred_element_type=F32)


def call(kernel, **kwargs):
    return pl.pallas_call(
        kernel, compiler_params=pltpu.CompilerParams(vmem_limit_bytes=VMEM_LIMIT), **kwargs
    )


def whole_block(shape):
    return pl.BlockSpec(shape, lambda step: (0,) * len(shape))


def pair_block(shape):
    return pl.BlockSpec((1,) + shape, lambda step: (step,) + (0,) * len(shape))


def weight_rows(pieces, columns=slice(None)):
    rows = [piece[0, :, :, columns].reshape(-1, piece[0, :, :, columns].shape[-1]) for piece in pieces]
    return rows[0] if len(rows) == 1 else jnp.concatenate(rows, axis=0)


def attention_forward_kernel(piece_count, own, other, own_entity, other_entity, *refs):
    pieces = refs[:piece_count]
    mixed, queries, keys, values, weights, totals, key_masked, value_ones, packed = refs[piece_count:]
    rows = own.shape[0]
    block = rows // 2
    lane = lax.broadcasted_iota(jnp.int32, (rows, LANES), 1)
    low = lane < HD
    at = 0
    for piece in pieces:
        part = piece[0].reshape(-1, D)
        packed[at : at + part.shape[0], :] = part
        at += part.shape[0]
    is_own = own_entity[...]
    is_other = other_entity[...]
    projected = dot(own[...], packed[...])
    entity_row = is_own > 0.5
    to_word = jnp.where(entity_row, projected[:, 256:384], projected[:, 0:128]) * QUERY_SCALE
    to_entity = jnp.where(entity_row, projected[:, 384:512], projected[:, 128:256]) * QUERY_SCALE
    queries[0, :, 0:LANES] = jnp.where(low, to_word, pltpu.roll(to_entity, HD, 1)).astype(BF)
    queries[0, :, LANES:] = jnp.where(low, pltpu.roll(to_word, HD, 1), to_entity).astype(BF)
    projected_other = dot(other[...], packed[:, 512:768])
    halves = (
        (projected[:, 512:640], projected[:, 640:768], is_own),
        (projected_other[:, 0:128], projected_other[:, 128:256], is_other),
    )
    for half, (key, value, entity) in enumerate(halves):
        at = pl.ds(half * rows, rows)
        keys[0, at, :] = key.astype(BF)
        values[0, at, :] = value.astype(BF)
        mask = jnp.where(low, 1.0 - entity, entity)
        turned = pltpu.roll(key, HD, 1)
        key_masked[at, 0:LANES] = (jnp.where(low, key, turned) * mask).astype(BF)
        key_masked[at, LANES:] = (jnp.where(low, turned, key) * mask).astype(BF)
        ones = jnp.ones_like(value)
        value_ones[at, 0:LANES] = jnp.where(low, value, ones).astype(BF)
        value_ones[at, LANES:] = jnp.where(low, ones, value).astype(BF)
    for index in range(rows // block):
        at = pl.ds(index * block, block)
        sums = []
        for head in range(2):
            columns = pl.ds(head * LANES, LANES)
            scores = dot_rt(queries[0, at, columns], key_masked[:, columns])
            highest = jnp.max(scores, axis=-1, keepdims=True)
            weight = jnp.exp2(scores - highest).astype(BF)
            weights[0, head, at, :] = weight
            sums.append(dot(weight, value_ones[:, columns]))
        upper = jnp.where(low[:block], sums[0], sums[1])
        total = pltpu.roll(jnp.where(low[:block], sums[1], sums[0]), HD, 1)
        mixed[at, :] = (upper / total).astype(BF)
        totals[0, at, :] = total


def piece_blocks(pieces):
    return [pair_block(piece.shape[1:]) for piece in pieces]


def attention_forward(own, other, own_entity, other_entity, pieces):
    count = pieces[0].shape[0]
    rows = own.shape[0]
    length = 2 * rows
    return call(
        functools.partial(attention_forward_kernel, len(pieces)),
        grid=(count,),
        in_specs=[whole_block((rows, D))] * 2 + [whole_block((rows, LANES))] * 2 + piece_blocks(pieces),
        out_specs=[
            pl.BlockSpec((rows, LANES), lambda step: (0, step)),
            pair_block((rows, 2 * LANES)),
            pair_block((length, LANES)),
            pair_block((length, LANES)),
            pair_block((2, rows, length)),
            pair_block((rows, LANES)),
        ],
        out_shape=[
            jax.ShapeDtypeStruct((rows, LANES * count), BF),
            jax.ShapeDtypeStruct((count, rows, 2 * LANES), BF),
            jax.ShapeDtypeStruct((count, length, LANES), BF),
            jax.ShapeDtypeStruct((count, length, LANES), BF),
            jax.ShapeDtypeStruct((count, 2, rows, length), BF),
            jax.ShapeDtypeStruct((count, rows, LANES), F32),
        ],
        scratch_shapes=[
            pltpu.VMEM((length, 2 * LANES), BF),
            pltpu.VMEM((length, 2 * LANES), BF),
            pltpu.VMEM((D, D), BF),
        ],
        name="attention_forward",
        cost_estimate=pl.CostEstimate(
            flops=count * 7_000_000_000, transcendentals=count * 2400000, bytes_accessed=count * 8_000_000
        ),
    )(own, other, own_entity, other_entity, *pieces)


def attention_backward_kernel(piece_count, first, own, other, own_entity, other_entity, *refs):
    pieces = refs[:piece_count]
    refs = refs[piece_count:]
    queries, keys, values, weights, totals, mixed, grad = refs[:7]
    refs = refs[7:]
    if not first:
        own_before, other_before = refs[:2]
        refs = refs[2:]
    near, far, own_grad, other_grad = refs[:4]
    key_masked, value_ones, grad_wide, query_grad, key_grad, value_grad, joined, packed = refs[4:]
    rows = own.shape[0]
    block = rows // 3
    lane = lax.broadcasted_iota(jnp.int32, (rows, LANES), 1)
    low = lane < HD
    at = 0
    for piece in pieces:
        part = piece[0].reshape(-1, D)
        packed[at : at + part.shape[0], :] = part
        at += part.shape[0]
    is_own = own_entity[...]
    is_other = other_entity[...]
    for half, entity in enumerate((is_own, is_other)):
        at = pl.ds(half * rows, rows)
        key = keys[0, at, :].astype(F32)
        turned = pltpu.roll(key, HD, 1)
        mask = jnp.where(low, 1.0 - entity, entity)
        key_masked[at, 0:LANES] = (jnp.where(low, key, turned) * mask).astype(BF)
        key_masked[at, LANES:] = (jnp.where(low, turned, key) * mask).astype(BF)
        value = values[0, at, :].astype(F32)
        ones = jnp.where(lane % HD < 2, 1.0, 0.0)
        value_ones[at, 0:LANES] = jnp.where(low, value, ones).astype(BF)
        value_ones[at, LANES:] = jnp.where(low, ones, value).astype(BF)
    scaled = grad[...].astype(F32) / totals[0]
    inner = scaled * mixed[...].astype(F32)

    def correction(inner_sum):
        upper = inner_sum.astype(BF).astype(F32)
        return jnp.where(
            lane % HD == 0, -upper, jnp.where(lane % HD == 1, upper - inner_sum, 0.0)
        )

    first_inner = jnp.sum(jnp.where(low, inner, 0.0), axis=-1, keepdims=True)
    second_inner = jnp.sum(jnp.where(low, 0.0, inner), axis=-1, keepdims=True)
    grad_wide[:, 0:LANES] = jnp.where(low, scaled, correction(first_inner)).astype(BF)
    grad_wide[:, LANES:] = jnp.where(low, correction(second_inner), scaled).astype(BF)
    for head in range(2):
        columns = pl.ds(head * LANES, LANES)
        for index in range(rows // block):
            at = pl.ds(index * block, block)
            grad_block = grad_wide[at, columns]
            weight = weights[0, head, at, :]
            score_grad = (weight.astype(F32) * dot_rt(grad_block, value_ones[:, columns])).astype(BF)
            query_grad[at, columns] = dot(score_grad, key_masked[:, columns]) * HD**-0.5
            query_turned = queries[0, at, columns].astype(F32).T.astype(BF)
            grad_turned = grad_block.astype(F32).T[head * HD : (head + 1) * HD].astype(BF)
            key_part = dot(query_turned, score_grad)
            value_part = dot(grad_turned, weight)
            key_at = pl.ds(head * LANES, LANES)
            value_at = pl.ds(head * HD, HD)
            if index == 0:
                key_grad[key_at, :] = key_part
                value_grad[value_at, :] = value_part
            else:
                key_grad[key_at, :] += key_part
                value_grad[value_at, :] += value_part
    query_a = query_grad[:, 0:LANES]
    query_b = query_grad[:, LANES:]
    word_grad = jnp.where(low, query_a, pltpu.roll(query_b, HD, 1))
    entity_grad = jnp.where(low, pltpu.roll(query_a, HD, 1), query_b)
    is_word = 1.0 - is_own
    joined[0:rows, 0:128] = (is_word * word_grad).astype(BF)
    joined[0:rows, 128:256] = (is_word * entity_grad).astype(BF)
    joined[0:rows, 256:384] = (is_own * word_grad).astype(BF)
    joined[0:rows, 384:512] = (is_own * entity_grad).astype(BF)
    key_back = key_grad[...].T
    value_back = value_grad[...].T
    for half, entity in enumerate((is_own, is_other)):
        at = slice(half * rows, half * rows + rows)
        key_a = key_back[at, 0:LANES]
        key_b = key_back[at, LANES:]
        key_word = jnp.where(low, key_a, pltpu.roll(key_b, HD, 1))
        key_entity = jnp.where(low, pltpu.roll(key_a, HD, 1), key_b)
        joined[at, 512:640] = (jnp.where(entity > 0.5, key_entity, key_word) * LN2).astype(BF)
        joined[at, 640:768] = value_back[at].astype(BF)
    here = dot_lt(own[...], joined[0:rows, :])
    there = dot_lt(other[...], joined[rows:, 512:768])
    for target, at in ((near, slice(0, D // 2)), (far, slice(D // 2, D))):
        target[0, :, 0:512] = here[at, 0:512].astype(BF)
        target[0, :, 512:768] = (here[at, 512:768] + there[at]).astype(BF)
    own_part = dot_rt(joined[0:rows, :], packed[...])
    other_part = dot_rt(joined[rows:, 512:768], packed[:, 512:768])
    step = pl.program_id(0)

    @pl.when(step == 0)
    def _():
        if first:
            own_grad[...] = own_part
            other_grad[...] = other_part
        else:
            own_grad[...] = own_before[...] + own_part
            other_grad[...] = other_before[...] + other_part

    @pl.when(step > 0)
    def _():
        own_grad[...] += own_part
        other_grad[...] += other_part


def attention_backward(own, other, own_entity, other_entity, pieces, saved, grad, before):
    count = pieces[0].shape[0]
    rows = own.shape[0]
    length = 2 * rows
    first = before is None
    column = pl.BlockSpec((rows, LANES), lambda step: (0, step))
    mixed, queries, keys, values, weights, totals = saved
    return call(
        functools.partial(attention_backward_kernel, len(pieces), first),
        grid=(count,),
        in_specs=[whole_block((rows, D))] * 2
        + [whole_block((rows, LANES))] * 2
        + piece_blocks(pieces)
        + [
            pair_block((rows, 2 * LANES)),
            pair_block((length, LANES)),
            pair_block((length, LANES)),
            pair_block((2, rows, length)),
            pair_block((rows, LANES)),
            column,
            column,
        ]
        + [whole_block((rows, D))] * (0 if first else 2),
        out_specs=[pair_block((D // 2, D))] * 2 + [whole_block((rows, D))] * 2,
        out_shape=[jax.ShapeDtypeStruct((count, D // 2, D), BF)] * 2
        + [jax.ShapeDtypeStruct((rows, D), F32)] * 2,
        scratch_shapes=[
            pltpu.VMEM((length, 2 * LANES), BF),
            pltpu.VMEM((length, 2 * LANES), BF),
            pltpu.VMEM((rows, 2 * LANES), BF),
            pltpu.VMEM((rows, 2 * LANES), F32),
            pltpu.VMEM((2 * LANES, length), F32),
            pltpu.VMEM((LANES, length), F32),
            pltpu.VMEM((length, D), BF),
            pltpu.VMEM((D, D), BF),
        ],
        name="attention_backward",
        cost_estimate=pl.CostEstimate(
            flops=count * 12_000_000_000, transcendentals=0, bytes_accessed=count * 12_000_000
        ),
    )(
        own, other, own_entity, other_entity, *pieces,
        queries, keys, values, weights, totals, mixed, grad, *(() if first else before),
    )


def error_function(value):
    value = jnp.clip(value, -3.7439211627767994, 3.7439211627767994)
    square = value * value
    upper = jnp.float32(0.00022905065861350646)
    for term in (
        0.0034082910107109506, 0.050955695062380861, 0.18520832239976145, 1.128379143519084,
    ):
        upper = upper * square + term
    lower = jnp.float32(-1.1791602954361697e-7)
    for term in (
        0.000023547966471313185, 0.0010179625278914885, 0.014070470171167667,
        0.11098505178285362, 0.49746925110067538, 1.0,
    ):
        lower = lower * square + term
    return value * upper / lower


def load_weights(copies):
    for copy in copies:
        copy.start()


def wait_all(copies):
    for copy in copies:
        copy.wait()


def feed_forward_kernel(
    group_count, piece_offsets, parts, position, vectors, tokens, cotangent, *refs
):
    piece_count = len(piece_offsets)
    mixed_groups = refs[:group_count]
    refs = refs[group_count:]
    mixing_pieces, up_pieces, down_pieces = (
        refs[k * piece_count : (k + 1) * piece_count] for k in range(3)
    )
    refs = refs[3 * piece_count :]
    (
        layer_out, near, far, hidden_low, slopes, normed_out, inverse_out, residual_grad, sums,
        mixing, up, down, active, total, hidden, low_grad, down_grad, in_sems, out_sems,
    ) = refs
    rows = tokens.shape[0]
    block = rows // 3
    me = position[0]

    def copies(source_pieces, target, index):
        made = []
        for k, offsets in enumerate(piece_offsets):
            for j, offset in enumerate(offsets):
                made.append((source_pieces[k].at[j], me ^ offset, len(made)))
        return made

    mixing_copies = [
        pltpu.make_async_copy(src, mixing.at[at], in_sems.at[0, n]) for src, at, n in copies(mixing_pieces, mixing, 0)
    ]
    up_copies = [
        pltpu.make_async_copy(src, up.at[:, at], in_sems.at[1, n]) for src, at, n in copies(up_pieces, up, 1)
    ]
    down_copies = [
        pltpu.make_async_copy(src, down.at[at], in_sems.at[2, n]) for src, at, n in copies(down_pieces, down, 2)
    ]
    load_weights(mixing_copies + up_copies + down_copies)
    chunk = parts // 4

    def vector(index):
        return vectors[index : index + 1, :]

    def add_sum(index, value, start):
        part = jnp.sum(value, axis=0, keepdims=True)
        if start:
            sums[index : index + 1, :] = part
        else:
            sums[index : index + 1, :] += part

    sums[6:8, :] = jnp.zeros((2, D), F32)
    wait_all(mixing_copies)
    for index in range(3):
        at = pl.ds(index * block, block)
        mixed = jnp.concatenate([group[at, :] for group in mixed_groups], axis=1)
        attended = dot(mixed, mixing[...].reshape(D, D)) + vector(0)
        stream = tokens[at, :].astype(F32) + attended
        add_sum(0, stream * stream, index == 0)
        add_sum(1, attended * attended, index == 0)
        center = stream - jnp.mean(stream, axis=-1, keepdims=True)
        inverse = lax.rsqrt(jnp.mean(center * center, axis=-1, keepdims=True) + EPSILON)
        normed = center * inverse
        normed_out[at, :] = normed
        inverse_out[at, :] = jnp.broadcast_to(inverse, (block, LANES))
        value = normed * vector(1) + vector(2)
        hidden[at, :] = value
        hidden_low[at, :] = value.astype(BF)
    wait_all(up_copies)
    wait_all(down_copies)
    for quarter in range(4):
        up_part = up[quarter].reshape(D, D)
        down_part = down[quarter * chunk : (quarter + 1) * chunk].reshape(D, D)
        for index in range(3):
            at = pl.ds(index * block, block)
            before = dot(hidden_low[at, :], up_part) + vector(6 + quarter)
            half = 0.5 * (1.0 + error_function(before * 0.7071067811865476))
            act = (before * half).astype(BF)
            active[quarter, at, :] = act
            slope = half + before * jnp.exp(-0.5 * before * before) * 0.3989422804014327
            slopes[at, quarter * D : (quarter + 1) * D] = slope.astype(BF)
            part = dot(act, down_part)
            if quarter == 0:
                total[at, :] = part
            else:
                total[at, :] += part
    for index in range(3):
        at = pl.ds(index * block, block)
        forward_out = total[at, :] + vector(3)
        add_sum(2, forward_out * forward_out, index == 0)
        value = hidden[at, :] + forward_out
        center = value - jnp.mean(value, axis=-1, keepdims=True)
        inverse = lax.rsqrt(jnp.mean(center * center, axis=-1, keepdims=True) + EPSILON)
        normed = center * inverse
        layer_out[at, :] = (normed * vector(4) + vector(5)).astype(BF)
        upstream = cotangent[at, :].astype(F32)
        scaled = upstream * vector(4)
        inner = (
            scaled
            - jnp.mean(scaled, axis=-1, keepdims=True)
            - normed * jnp.mean(scaled * normed, axis=-1, keepdims=True)
        ) * inverse
        residual_grad[at, :] = inner
        rounded = inner.astype(BF)
        low_grad[at, :] = rounded
        add_sum(3, upstream * normed, index == 0)
        add_sum(4, upstream, index == 0)
        add_sum(5, rounded.astype(F32), index == 0)
    for quarter in range(4):
        grad = dot_lt(active[quarter], low_grad[...])
        down_grad[quarter * chunk : (quarter + 1) * chunk] = grad.astype(BF).reshape(chunk, -1, D)
    store_relative(down_grad, near, far, me, piece_offsets, out_sems, lambda ref, at: ref.at[at])


def store_relative(source, near, far, me, piece_offsets, sems, pick):
    offsets = [offset for part in piece_offsets for offset in part]
    made = []
    for j, offset in enumerate(offsets):
        half = len(offsets) // 2
        target = near if j < half else far
        made.append(
            pltpu.make_async_copy(pick(source, me ^ offset), target.at[j % half], sems.at[j])
        )
    for copy in made:
        copy.start()
    for copy in made:
        copy.wait()


def feed_forward(position, vectors, tokens, cotangent, groups, weights, piece_offsets, parts):
    rows = tokens.shape[0]
    share = D // parts
    anywhere = pl.BlockSpec(memory_space=pl.ANY)
    vmem = pl.BlockSpec(memory_space=pltpu.VMEM)
    mixing_pieces, up_pieces, down_pieces = weights
    return call(
        functools.partial(feed_forward_kernel, len(groups), piece_offsets, parts),
        in_specs=[pl.BlockSpec(memory_space=pltpu.SMEM), vmem, vmem, vmem]
        + [vmem] * len(groups)
        + [anywhere] * (3 * len(piece_offsets)),
        out_specs=[vmem, anywhere, anywhere] + [vmem] * 6,
        out_shape=[
            jax.ShapeDtypeStruct((rows, D), BF),
            jax.ShapeDtypeStruct((parts // 2, 4 * share, D), BF),
            jax.ShapeDtypeStruct((parts // 2, 4 * share, D), BF),
            jax.ShapeDtypeStruct((rows, D), BF),
            jax.ShapeDtypeStruct((rows, 4 * D), BF),
            jax.ShapeDtypeStruct((rows, D), F32),
            jax.ShapeDtypeStruct((rows, LANES), F32),
            jax.ShapeDtypeStruct((rows, D), F32),
            jax.ShapeDtypeStruct((8, D), F32),
        ],
        scratch_shapes=[
            pltpu.VMEM((parts, share, D), BF),
            pltpu.VMEM((4, parts, share, D), BF),
            pltpu.VMEM((parts, 4 * share, D), BF),
            pltpu.VMEM((4, rows, D), BF),
            pltpu.VMEM((rows, D), F32),
            pltpu.VMEM((rows, D), F32),
            pltpu.VMEM((rows, D), BF),
            pltpu.VMEM((parts, 4 * share, D), BF),
            pltpu.SemaphoreType.DMA((3, parts)),
            pltpu.SemaphoreType.DMA((parts,)),
        ],
        name="feed_forward",
        cost_estimate=pl.CostEstimate(
            flops=12_000_000_000, transcendentals=4800000, bytes_accessed=40_000_000
        ),
    )(position, vectors, tokens, cotangent, *groups, *mixing_pieces, *up_pieces, *down_pieces)


def feed_back_kernel(
    group_count, piece_offsets, parts, position, vectors, hidden_low, slopes, normed, inverse,
    residual_grad, *refs
):
    piece_count = len(piece_offsets)
    mixed_groups = refs[:group_count]
    refs = refs[group_count:]
    mixing_pieces, up_pieces, down_pieces = (
        refs[k * piece_count : (k + 1) * piece_count] for k in range(3)
    )
    refs = refs[3 * piece_count :]
    up_near, up_far, mixing_near, mixing_far, stream_grad, sums = refs[:6]
    grad_groups = refs[6 : 6 + group_count]
    mixing, up, down, pre_grad, low_grad, back, up_grad, mixing_grad, in_sems, out_sems = refs[6 + group_count :]
    rows = hidden_low.shape[0]
    block = rows // 3
    me = position[0]
    chunk = parts // 4

    def copies(source_pieces):
        made = []
        for k, offsets in enumerate(piece_offsets):
            for j, offset in enumerate(offsets):
                made.append((source_pieces[k].at[j], me ^ offset, len(made)))
        return made

    down_copies = [
        pltpu.make_async_copy(src, down.at[at], in_sems.at[2, n]) for src, at, n in copies(down_pieces)
    ]
    up_copies = [
        pltpu.make_async_copy(src, up.at[:, at], in_sems.at[1, n]) for src, at, n in copies(up_pieces)
    ]
    mixing_copies = [
        pltpu.make_async_copy(src, mixing.at[at], in_sems.at[0, n]) for src, at, n in copies(mixing_pieces)
    ]
    load_weights(down_copies + up_copies + mixing_copies)

    def vector(index):
        return vectors[index : index + 1, :]

    def add_sum(index, value, start):
        part = jnp.sum(value, axis=0, keepdims=True)
        if start:
            sums[index : index + 1, :] = part
        else:
            sums[index : index + 1, :] += part

    sums[7:8, :] = jnp.zeros((1, D), F32)
    low_grad[...] = residual_grad[...].astype(BF)
    wait_all(down_copies)
    wait_all(up_copies)
    for quarter in range(4):
        up_part = up[quarter].reshape(D, D)
        down_part = down[quarter * chunk : (quarter + 1) * chunk].reshape(D, D)
        for index in range(3):
            at = pl.ds(index * block, block)
            slope = slopes[at, quarter * D : (quarter + 1) * D].astype(F32)
            part = (dot_rt(low_grad[at, :], down_part) * slope).astype(BF)
            pre_grad[at, :] = part
            add_sum(3 + quarter, part.astype(F32), index == 0)
            back_part = dot_rt(part, up_part)
            if quarter == 0:
                back[at, :] = back_part
            else:
                back[at, :] += back_part
        grad = dot_lt(hidden_low[...], pre_grad[...])
        up_grad[quarter] = grad.astype(BF).reshape(parts, -1, D)
    wait_all(mixing_copies)
    for index in range(3):
        at = pl.ds(index * block, block)
        hidden_grad = residual_grad[at, :] + back[at, :]
        norm = normed[at, :]
        scaled = hidden_grad * vector(1)
        inner = (
            scaled
            - jnp.mean(scaled, axis=-1, keepdims=True)
            - norm * jnp.mean(scaled * norm, axis=-1, keepdims=True)
        ) * inverse[at, 0:1]
        stream_grad[at, :] = inner
        rounded = inner.astype(BF)
        low_grad[at, :] = rounded
        add_sum(0, hidden_grad * norm, index == 0)
        add_sum(1, hidden_grad, index == 0)
        add_sum(2, rounded.astype(F32), index == 0)
        mixed_grad = dot_rt(rounded, mixing[...].reshape(D, D)).astype(BF)
        start = 0
        for group in grad_groups:
            width = group.shape[1]
            group[at, :] = mixed_grad[:, start : start + width]
            start += width
    start = 0
    for group in mixed_groups:
        width = group.shape[1]
        back[start : start + width, :] = dot_lt(group[...], low_grad[...])
        start += width
    mixing_grad[...] = back[...].astype(BF).reshape(parts, -1, D)
    store_relative(up_grad, up_near, up_far, me, piece_offsets, out_sems.at[0], lambda ref, at: ref.at[:, at])
    store_relative(mixing_grad, mixing_near, mixing_far, me, piece_offsets, out_sems.at[1], lambda ref, at: ref.at[at])


def feed_back(position, vectors, saved, groups, weights, piece_offsets, parts):
    hidden_low, slopes, normed, inverse, residual_grad = saved
    rows = hidden_low.shape[0]
    share = D // parts
    half = parts // 2
    anywhere = pl.BlockSpec(memory_space=pl.ANY)
    vmem = pl.BlockSpec(memory_space=pltpu.VMEM)
    mixing_pieces, up_pieces, down_pieces = weights
    return call(
        functools.partial(feed_back_kernel, len(groups), piece_offsets, parts),
        in_specs=[pl.BlockSpec(memory_space=pltpu.SMEM)]
        + [vmem] * (6 + len(groups))
        + [anywhere] * (3 * len(piece_offsets)),
        out_specs=[anywhere] * 4 + [vmem] * (2 + len(groups)),
        out_shape=[jax.ShapeDtypeStruct((half, 4, share, D), BF)] * 2
        + [jax.ShapeDtypeStruct((half, share, D), BF)] * 2
        + [jax.ShapeDtypeStruct((rows, D), F32), jax.ShapeDtypeStruct((8, D), F32)]
        + [jax.ShapeDtypeStruct(group.shape, BF) for group in groups],
        scratch_shapes=[
            pltpu.VMEM((parts, share, D), BF),
            pltpu.VMEM((4, parts, share, D), BF),
            pltpu.VMEM((parts, 4 * share, D), BF),
            pltpu.VMEM((rows, D), BF),
            pltpu.VMEM((rows, D), BF),
            pltpu.VMEM((rows, D), F32),
            pltpu.VMEM((4, parts, share, D), BF),
            pltpu.VMEM((parts, share, D), BF),
            pltpu.SemaphoreType.DMA((3, parts)),
            pltpu.SemaphoreType.DMA((2, parts)),
        ],
        name="feed_back",
        cost_estimate=pl.CostEstimate(
            flops=13_000_000_000, transcendentals=0, bytes_accessed=40_000_000
        ),
    )(position, vectors, hidden_low, slopes, normed, inverse, residual_grad, *groups,
      *mixing_pieces, *up_pieces, *down_pieces)


def swap(value, bit, axis="dp"):
    size = lax.axis_size(axis)
    return lax.ppermute(value, axis, [(index, index ^ bit) for index in range(size)])


def relative_offsets(size):
    offsets = [0]
    bit = size // 2
    while bit:
        offsets += [offset ^ bit for offset in offsets]
        bit //= 2
    return offsets


def gather_pieces(shard, axis):
    size = lax.axis_size("dp")
    held = jnp.expand_dims(shard, axis)
    bit = size // 2
    while bit > 2:
        held = jnp.concatenate([held, swap(held, bit)], axis=axis)
        bit //= 2
    beside = swap(held, 2)
    return [held, beside, swap(held, 1), swap(beside, 1)]


def scatter_sum(near, far, axis):
    kept, received = near, swap(far, 1)
    bit = 2
    while bit < lax.axis_size("dp"):
        half = kept.shape[axis] // 2
        first = lax.slice_in_dim(kept, 0, half, axis=axis) + lax.slice_in_dim(received, 0, half, axis=axis)
        second = lax.slice_in_dim(kept, half, 2 * half, axis=axis) + lax.slice_in_dim(received, half, 2 * half, axis=axis)
        kept, received = first, swap(second, bit)
        bit *= 2
    mine = kept + received
    mine = lax.squeeze(mine, (axis,))
    return mine.astype(F32) + swap(mine, 1, "seq").astype(F32)


def sum_everywhere(value, axes):
    for axis in axes:
        bit = 1
        while bit < lax.axis_size(axis):
            value = value + swap(value, bit, axis)
            bit *= 2
    return value


def local(
    tokens,
    entity_flags,
    query_weight,
    key_weight,
    value_weight,
    mixing_weight,
    mixing_bias,
    first_gain,
    first_bias,
    up_weight,
    up_bias,
    down_weight,
    down_bias,
    second_gain,
    second_bias,
    cotangent,
):
    parts = lax.axis_size("dp")
    me = lax.axis_index("dp")
    share = D // parts
    rows = tokens.shape[0]
    by_swaps = share % 16 == 0 and parts & (parts - 1) == 0 and parts > 4

    six = jnp.concatenate([query_weight, key_weight[None], value_weight[None]], axis=0)
    pairs = jnp.transpose(six.reshape(6, share, PAIRS, LANES), (2, 1, 0, 3)).reshape(PAIRS, share, D)
    up_shard = jnp.transpose(up_weight.reshape(share, 4, D), (1, 0, 2))

    offsets = relative_offsets(parts) if by_swaps else list(range(parts))
    order = me ^ jnp.array(offsets, jnp.int32) if by_swaps else jnp.array(offsets, jnp.int32)
    column_of = (order[:, None] * share + jnp.arange(share, dtype=jnp.int32)[None, :]).reshape(D)
    choose = (lax.broadcasted_iota(jnp.int32, (D, D), 0) == column_of[None, :]).astype(BF)
    own = dot(tokens, choose).astype(BF)
    other = swap(own, 1, "seq")
    entity = entity_flags.astype(F32)
    own_entity = jnp.broadcast_to(entity[:, None], (rows, LANES))
    other_entity = jnp.broadcast_to(swap(entity, 1, "seq")[:, None], (rows, LANES))

    blank = jnp.zeros((D,), BF)
    vectors = jnp.stack(
        [
            lax.dynamic_update_slice(blank, vector, (me * share,))
            for vector in (mixing_bias, first_gain, first_bias, down_bias, second_gain, second_bias)
        ]
    )
    up_vector = lax.dynamic_update_slice(jnp.zeros((4 * D,), BF), up_bias, (me * 4 * share,)).reshape(4, D)
    vectors = jnp.concatenate([vectors, up_vector, jnp.zeros((6, D), BF)], axis=0)

    groups = []
    start = 0
    if by_swaps:
        for count in FORWARD_GROUPS:
            groups.append(gather_pieces(pairs[start : start + count], 1))
            start += count
        middle = (
            gather_pieces(mixing_weight, 0),
            gather_pieces(up_shard, 0),
            gather_pieces(down_weight, 0),
        )
        vectors = sum_everywhere(vectors, ("dp",))
        middle_offsets = [offsets[k * parts // 4 : (k + 1) * parts // 4] for k in range(4)]
        position, middle_parts = me, parts
    else:
        for count in FORWARD_GROUPS:
            gathered = lax.all_gather(pairs[start : start + count], "dp", axis=1, tiled=True)
            groups.append([gathered.reshape(count, 1, D, D)])
            start += count
        joined = [
            lax.all_gather(weight, "dp", axis=0, tiled=True)
            for weight in (mixing_weight, up_weight, down_weight)
        ]
        vectors = lax.psum(vectors, "dp")
        middle_parts = 4
        middle = (
            [joined[0].reshape(4, D // 4, D)],
            [jnp.transpose(joined[1].reshape(4, D // 4, 4, D), (0, 2, 1, 3))],
            [joined[2].reshape(4, D, D)],
        )
        middle_offsets = [[0, 1, 2, 3]]
        position = jnp.int32(0)
    vectors = vectors.astype(F32)
    position = position.astype(jnp.int32).reshape(1)

    saved = [attention_forward(own, other, own_entity, other_entity, pieces) for pieces in groups]
    mixed = [item[0] for item in saved]
    (
        layer_out, down_near, down_far, hidden_low, slopes, normed, inverse, residual_grad, sums_one,
    ) = feed_forward(position, vectors, tokens, cotangent, mixed, middle, middle_offsets, middle_parts)
    up_near, up_far, mixing_near, mixing_far, stream_grad, sums_two, *mixed_grads = feed_back(
        position, vectors, (hidden_low, slopes, normed, inverse, residual_grad), mixed, middle,
        middle_offsets, middle_parts,
    )

    before = None
    parts_of = [None] * len(groups)
    for index in reversed(range(len(groups))):
        near, far, *before = attention_backward(
            own, other, own_entity, other_entity, groups[index], saved[index], mixed_grads[index], before
        )
        parts_of[index] = (near, far)
    own_grad, other_grad = before
    attended = own_grad + swap(other_grad.astype(BF), 1, "seq").astype(F32)
    upper = attended.astype(BF)
    lower = (attended - upper.astype(F32)).astype(BF)
    tokens_grad = (stream_grad + dot_rt(upper, choose) + dot_rt(lower, choose)).astype(BF)

    sums = jnp.concatenate([sums_one, sums_two], axis=0)
    if by_swaps:
        down_sum = scatter_sum(down_near, down_far, 0)
        up_sum = scatter_sum(up_near, up_far, 0)
        mixing_sum = scatter_sum(mixing_near, mixing_far, 0)
        pair_sums = []
        for near, far in parts_of:
            shape = (near.shape[0], parts // 2, share, D)
            pair_sums.append(scatter_sum(near.reshape(shape), far.reshape(shape), 1))
        pair_sum = jnp.concatenate(pair_sums, axis=0)
        sums = sum_everywhere(sums, ("dp", "seq"))
    else:

        def reduced(near, far, axis):
            value = jnp.concatenate([near, far], axis=axis)
            piece = lax.psum_scatter(value.reshape(value.shape), "dp", scatter_dimension=axis, tiled=True)
            return lax.psum(piece, "seq").astype(F32)

        down_sum = reduced(down_near.reshape(-1, D), down_far.reshape(-1, D), 0)
        up_all = jnp.concatenate([up_near, up_far], axis=0)
        up_sum = reduced(
            *jnp.split(jnp.transpose(up_all, (1, 0, 2, 3)).reshape(4, D, D), 2, axis=1), 1
        )
        mixing_sum = reduced(mixing_near.reshape(-1, D), mixing_far.reshape(-1, D), 0)
        pair_sum = jnp.concatenate([reduced(near, far, 1) for near, far in parts_of], axis=0)
        sums = lax.psum(sums, ("dp", "seq"))

    six_sum = jnp.transpose(pair_sum.reshape(PAIRS, share, 6, LANES), (2, 1, 0, 3)).reshape(6, share, D)
    up_out = jnp.transpose(up_sum, (1, 0, 2)).reshape(share, 4 * D)

    def shard(row, width=1):
        return lax.dynamic_slice(sums[row : row + width].reshape(-1), (me * share * width,), (share * width,))

    token_count = rows * parts * lax.axis_size("seq")
    stream_rms = jnp.sqrt(jnp.sum(sums[0:3], axis=1) / (token_count * D))
    return (
        layer_out,
        tokens_grad,
        six_sum[0:4],
        six_sum[4],
        six_sum[5],
        mixing_sum,
        shard(10),
        shard(8),
        shard(9),
        up_out,
        shard(11, 4),
        down_sum,
        shard(5),
        shard(3),
        shard(4),
        stream_rms,
    )


def solution(mesh):
    rows = P(("dp", "seq"), None)
    vector = P("dp")
    matrix = P("dp", None)
    stacked = P(None, "dp", None)
    in_specs = (
        rows, P(("dp", "seq")), stacked, matrix, matrix, matrix, vector, vector, vector, matrix,
        vector, matrix, vector, vector, vector, rows,
    )
    out_specs = (
        rows, rows, stacked, matrix, matrix, matrix, vector, vector, vector, matrix, vector,
        matrix, vector, vector, vector, P(),
    )
    return jax.shard_map(local, mesh=mesh, in_specs=in_specs, out_specs=out_specs, check_vma=False)
```

```python
import functools

import jax
import jax.numpy as jnp
from jax import lax
from jax.experimental import pallas as pl
from jax.experimental.pallas import tpu as pltpu
from jax.sharding import PartitionSpec as P

D = 768
HEADS = 12
HD = 64
PAIRS = HEADS // 2
LANES = 2 * HD
F32 = jnp.float32
BF = jnp.bfloat16
EPSILON = 1e-05
LN2 = 0.6931471805599453
QUERY_SCALE = HD**-0.5 / LN2
FORWARD_GROUPS = (1, 2, 3)
SUM_ROWS = 16
MIDDLE_STEP = 0
MIB = 1024 * 1024


def dot(left, right):
    return jnp.dot(left, right, preferred_element_type=F32)


def dot_rt(left, right):
    return lax.dot_general(left, right, (((1,), (1,)), ((), ())), preferred_element_type=F32)


def dot_lt(left, right):
    return lax.dot_general(left, right, (((0,), (0,)), ((), ())), preferred_element_type=F32)


def call(kernel, mebibytes, **kwargs):
    return pl.pallas_call(
        kernel, compiler_params=pltpu.CompilerParams(vmem_limit_bytes=mebibytes * MIB), **kwargs
    )


def whole_block(shape):
    return pl.BlockSpec(shape, lambda step: (0,) * len(shape))


def pair_block(shape):
    return pl.BlockSpec((1,) + shape, lambda step: (step,) + (0,) * len(shape))


def attention_forward_kernel(piece_count, own, other, own_entity, other_entity, *refs):
    pieces = refs[:piece_count]
    mixed, queries, keys, values, weights, totals, key_masked, value_ones, packed = refs[piece_count:]
    rows = own.shape[0]
    block = rows // 2
    lane = lax.broadcasted_iota(jnp.int32, (rows, LANES), 1)
    low = lane < HD
    at = 0
    for piece in pieces:
        part = piece[0].reshape(-1, D)
        packed[at : at + part.shape[0], :] = part
        at += part.shape[0]
    is_own = own_entity[...]
    is_other = other_entity[...]
    projected = dot(own[...], packed[...])
    entity_row = is_own > 0.5
    to_word = jnp.where(entity_row, projected[:, 256:384], projected[:, 0:128]) * QUERY_SCALE
    to_entity = jnp.where(entity_row, projected[:, 384:512], projected[:, 128:256]) * QUERY_SCALE
    queries[0, :, 0:LANES] = jnp.where(low, to_word, pltpu.roll(to_entity, HD, 1)).astype(BF)
    queries[0, :, LANES:] = jnp.where(low, pltpu.roll(to_word, HD, 1), to_entity).astype(BF)
    projected_other = dot(other[...], packed[:, 512:768])
    halves = (
        (projected[:, 512:640], projected[:, 640:768], is_own),
        (projected_other[:, 0:128], projected_other[:, 128:256], is_other),
    )
    for half, (key, value, entity) in enumerate(halves):
        at = pl.ds(half * rows, rows)
        keys[0, at, :] = key.astype(BF)
        values[0, at, :] = value.astype(BF)
        mask = jnp.where(low, 1.0 - entity, entity)
        turned = pltpu.roll(key, HD, 1)
        key_masked[at, 0:LANES] = (jnp.where(low, key, turned) * mask).astype(BF)
        key_masked[at, LANES:] = (jnp.where(low, turned, key) * mask).astype(BF)
        ones = jnp.ones_like(value)
        value_ones[at, 0:LANES] = jnp.where(low, value, ones).astype(BF)
        value_ones[at, LANES:] = jnp.where(low, ones, value).astype(BF)
    items = [(index, head) for index in range(rows // block) for head in range(2)]

    def scores_of(item):
        index, head = item
        columns = pl.ds(head * LANES, LANES)
        return dot_rt(queries[0, pl.ds(index * block, block), columns], key_masked[:, columns])

    ahead = scores_of(items[0])
    sums = []
    for number, (index, head) in enumerate(items):
        scores = ahead
        if number + 1 < len(items):
            ahead = scores_of(items[number + 1])
        at = pl.ds(index * block, block)
        highest = jnp.max(scores, axis=-1, keepdims=True)
        weight = jnp.exp2(scores - highest).astype(BF)
        weights[0, head, at, :] = weight
        sums.append(dot(weight, value_ones[:, pl.ds(head * LANES, LANES)]))
        if head:
            upper = jnp.where(low[:block], sums[0], sums[1])
            total = pltpu.roll(jnp.where(low[:block], sums[1], sums[0]), HD, 1)
            mixed[at, :] = (upper / total).astype(BF)
            totals[0, at, :] = total
            sums = []


def piece_blocks(pieces):
    return [pair_block(piece.shape[1:]) for piece in pieces]


def attention_forward(own, other, own_entity, other_entity, pieces):
    count = pieces[0].shape[0]
    rows = own.shape[0]
    length = 2 * rows
    return call(
        functools.partial(attention_forward_kernel, len(pieces)),
        30,
        grid=(count,),
        in_specs=[whole_block((rows, D))] * 2 + [whole_block((rows, LANES))] * 2 + piece_blocks(pieces),
        out_specs=[
            pl.BlockSpec((rows, LANES), lambda step: (0, step)),
            pair_block((rows, 2 * LANES)),
            pair_block((length, LANES)),
            pair_block((length, LANES)),
            pair_block((2, rows, length)),
            pair_block((rows, LANES)),
        ],
        out_shape=[
            jax.ShapeDtypeStruct((rows, LANES * count), BF),
            jax.ShapeDtypeStruct((count, rows, 2 * LANES), BF),
            jax.ShapeDtypeStruct((count, length, LANES), BF),
            jax.ShapeDtypeStruct((count, length, LANES), BF),
            jax.ShapeDtypeStruct((count, 2, rows, length), BF),
            jax.ShapeDtypeStruct((count, rows, LANES), F32),
        ],
        scratch_shapes=[
            pltpu.VMEM((length, 2 * LANES), BF),
            pltpu.VMEM((length, 2 * LANES), BF),
            pltpu.VMEM((D, D), BF),
        ],
        name="attention_forward",
        cost_estimate=pl.CostEstimate(
            flops=count * 7_000_000_000, transcendentals=count * 2400000, bytes_accessed=count * 8_000_000
        ),
    )(own, other, own_entity, other_entity, *pieces)


def attention_backward_kernel(own, other, own_entity, other_entity, *refs):
    queries, keys, values, weights, totals, mixed, grad = refs[:7]
    near, far, joined, joined_other = refs[7:11]
    key_masked, value_ones, grad_wide, query_grad, key_grad, value_grad = refs[11:]
    rows = own.shape[0]
    block = rows // 3
    lane = lax.broadcasted_iota(jnp.int32, (rows, LANES), 1)
    low = lane < HD
    is_own = own_entity[...]
    is_other = other_entity[...]
    for half, entity in enumerate((is_own, is_other)):
        at = pl.ds(half * rows, rows)
        key = keys[0, at, :].astype(F32)
        turned = pltpu.roll(key, HD, 1)
        mask = jnp.where(low, 1.0 - entity, entity)
        key_masked[at, 0:LANES] = (jnp.where(low, key, turned) * mask).astype(BF)
        key_masked[at, LANES:] = (jnp.where(low, turned, key) * mask).astype(BF)
        value = values[0, at, :].astype(F32)
        ones = jnp.where(lane % HD < 2, 1.0, 0.0)
        value_ones[at, 0:LANES] = jnp.where(low, value, ones).astype(BF)
        value_ones[at, LANES:] = jnp.where(low, ones, value).astype(BF)
    scaled = grad[...].astype(F32) / totals[0]
    inner = scaled * mixed[...].astype(F32)

    def correction(inner_sum):
        upper = inner_sum.astype(BF).astype(F32)
        return jnp.where(
            lane % HD == 0, -upper, jnp.where(lane % HD == 1, upper - inner_sum, 0.0)
        )

    first_inner = jnp.sum(jnp.where(low, inner, 0.0), axis=-1, keepdims=True)
    second_inner = jnp.sum(jnp.where(low, 0.0, inner), axis=-1, keepdims=True)
    grad_wide[:, 0:LANES] = jnp.where(low, scaled, correction(first_inner)).astype(BF)
    grad_wide[:, LANES:] = jnp.where(low, correction(second_inner), scaled).astype(BF)
    for head in range(2):
        columns = pl.ds(head * LANES, LANES)
        for index in range(rows // block):
            at = pl.ds(index * block, block)
            grad_block = grad_wide[at, columns]
            weight = weights[0, head, at, :]
            score_grad = (weight.astype(F32) * dot_rt(grad_block, value_ones[:, columns])).astype(BF)
            query_grad[at, columns] = dot(score_grad, key_masked[:, columns]) * HD**-0.5
            query_turned = queries[0, at, columns].astype(F32).T.astype(BF)
            grad_turned = grad_block.astype(F32).T[head * HD : (head + 1) * HD].astype(BF)
            key_part = dot(query_turned, score_grad)
            value_part = dot(grad_turned, weight)
            key_at = pl.ds(head * LANES, LANES)
            value_at = pl.ds(head * HD, HD)
            if index == 0:
                key_grad[key_at, :] = key_part
                value_grad[value_at, :] = value_part
            else:
                key_grad[key_at, :] += key_part
                value_grad[value_at, :] += value_part
    query_a = query_grad[:, 0:LANES]
    query_b = query_grad[:, LANES:]
    word_grad = jnp.where(low, query_a, pltpu.roll(query_b, HD, 1))
    entity_grad = jnp.where(low, pltpu.roll(query_a, HD, 1), query_b)
    is_word = 1.0 - is_own
    joined[0, :, 0:128] = (is_word * word_grad).astype(BF)
    joined[0, :, 128:256] = (is_word * entity_grad).astype(BF)
    joined[0, :, 256:384] = (is_own * word_grad).astype(BF)
    joined[0, :, 384:512] = (is_own * entity_grad).astype(BF)
    key_back = key_grad[...].T
    value_back = value_grad[...].T
    for half, entity in enumerate((is_own, is_other)):
        at = slice(half * rows, half * rows + rows)
        key_a = key_back[at, 0:LANES]
        key_b = key_back[at, LANES:]
        key_word = jnp.where(low, key_a, pltpu.roll(key_b, HD, 1))
        key_entity = jnp.where(low, pltpu.roll(key_a, HD, 1), key_b)
        key_part = (jnp.where(entity > 0.5, key_entity, key_word) * LN2).astype(BF)
        value_part = value_back[at].astype(BF)
        if half == 0:
            joined[0, :, 512:640] = key_part
            joined[0, :, 640:768] = value_part
        else:
            joined_other[0, :, 0:128] = key_part
            joined_other[0, :, 128:256] = value_part
    here = dot_lt(own[...], joined[0])
    there = dot_lt(other[...], joined_other[0])
    for target, at in ((near, slice(0, D // 2)), (far, slice(D // 2, D))):
        target[0, :, 0:512] = here[at, 0:512].astype(BF)
        target[0, :, 512:768] = (here[at, 512:768] + there[at]).astype(BF)


def attention_backward(own, other, own_entity, other_entity, saved, grad):
    mixed, queries, keys, values, weights, totals = saved
    count = queries.shape[0]
    rows = own.shape[0]
    length = 2 * rows
    column = pl.BlockSpec((rows, LANES), lambda step: (0, step))
    return call(
        attention_backward_kernel,
        34,
        grid=(count,),
        in_specs=[whole_block((rows, D))] * 2
        + [whole_block((rows, LANES))] * 2
        + [
            pair_block((rows, 2 * LANES)),
            pair_block((length, LANES)),
            pair_block((length, LANES)),
            pair_block((2, rows, length)),
            pair_block((rows, LANES)),
            column,
            column,
        ],
        out_specs=[pair_block((D // 2, D))] * 2 + [pair_block((rows, D)), pair_block((rows, 2 * LANES))],
        out_shape=[jax.ShapeDtypeStruct((count, D // 2, D), BF)] * 2
        + [
            jax.ShapeDtypeStruct((count, rows, D), BF),
            jax.ShapeDtypeStruct((count, rows, 2 * LANES), BF),
        ],
        scratch_shapes=[
            pltpu.VMEM((length, 2 * LANES), BF),
            pltpu.VMEM((length, 2 * LANES), BF),
            pltpu.VMEM((rows, 2 * LANES), BF),
            pltpu.VMEM((rows, 2 * LANES), F32),
            pltpu.VMEM((2 * LANES, length), F32),
            pltpu.VMEM((LANES, length), F32),
        ],
        name="attention_backward",
        cost_estimate=pl.CostEstimate(
            flops=count * 10_000_000_000, transcendentals=0, bytes_accessed=count * 12_000_000
        ),
    )(own, other, own_entity, other_entity, queries, keys, values, weights, totals, mixed, grad)


def token_gradient_kernel(piece_count, first, last, *refs):
    pieces = refs[:piece_count]
    refs = refs[piece_count:]
    joined, received = refs[:2]
    refs = refs[2:]
    if not first:
        before, refs = refs[0], refs[1:]
    if last:
        choose, stream_grad = refs[:2]
        refs = refs[2:]
        out, total, packed, wide = refs
    else:
        out, packed, wide = refs
        total = out
    at = 0
    for piece in pieces:
        part = piece[0].reshape(-1, D)
        packed[at : at + part.shape[0], :] = part
        at += part.shape[0]
    wide[:, 0:512] = joined[0, :, 0:512]
    wide[:, 512:768] = (joined[0, :, 512:768].astype(F32) + received[0].astype(F32)).astype(BF)
    part = dot_rt(wide[...], packed[...])
    step = pl.program_id(0)

    @pl.when(step == 0)
    def _():
        total[...] = part if first else before[...] + part

    @pl.when(step > 0)
    def _():
        total[...] += part

    if last:
        @pl.when(step == pl.num_programs(0) - 1)
        def _():
            value = total[...]
            upper = value.astype(BF)
            lower = (value - upper.astype(F32)).astype(BF)
            out[...] = (
                stream_grad[...] + dot_rt(upper, choose[...]) + dot_rt(lower, choose[...])
            ).astype(BF)


def token_gradient(pieces, joined, received, before, finish=None):
    count, rows, _ = joined.shape
    first, last = before is None, finish is not None
    return call(
        functools.partial(token_gradient_kernel, len(pieces), first, last),
        16,
        grid=(count,),
        in_specs=piece_blocks(pieces)
        + [pair_block((rows, D)), pair_block((rows, 2 * LANES))]
        + [whole_block((rows, D))] * (0 if first else 1)
        + ([whole_block((D, D)), whole_block((rows, D))] if last else []),
        out_specs=whole_block((rows, D)),
        out_shape=jax.ShapeDtypeStruct((rows, D), BF if last else F32),
        scratch_shapes=([pltpu.VMEM((rows, D), F32)] if last else [])
        + [pltpu.VMEM((D, D), BF), pltpu.VMEM((rows, D), BF)],
        name="token_gradient",
        cost_estimate=pl.CostEstimate(
            flops=count * 1_000_000_000, transcendentals=0, bytes_accessed=count * 4_000_000
        ),
    )(*pieces, joined, received, *(() if first else (before,)), *(finish or ()))


def error_function(value):
    value = jnp.clip(value, -3.7439211627767994, 3.7439211627767994)
    square = value * value
    upper = jnp.float32(0.00022905065861350646)
    for term in (
        0.0034082910107109506, 0.050955695062380861, 0.18520832239976145, 1.128379143519084,
    ):
        upper = upper * square + term
    lower = jnp.float32(-1.1791602954361697e-7)
    for term in (
        0.000023547966471313185, 0.0010179625278914885, 0.014070470171167667,
        0.11098505178285362, 0.49746925110067538, 1.0,
    ):
        lower = lower * square + term
    return value * upper / lower


def wait_all(copies):
    for copy in copies:
        copy.wait()


def weight_copies(share, starts, mixing_up, down_shards, mixing, up, down, sems):
    return (
        pltpu.make_async_copy(mixing_up.at[:, pl.ds(0, share)], mixing, sems.at[0]),
        [
            pltpu.make_async_copy(
                mixing_up.at[:, pl.ds(starts[0] + quarter * share, share)], up.at[quarter], sems.at[1 + quarter]
            )
            for quarter in range(4)
        ],
        pltpu.make_async_copy(down_shards.at[:, pl.ds(starts[1], 4 * share)], down, sems.at[5]),
    )


def make_adder(sums):
    def add_sum(index, value, start):
        part = jnp.sum(value, axis=0, keepdims=True)
        if start:
            sums[index : index + 1, :] = part
        else:
            sums[index : index + 1, :] += part

    return add_sum


def relative_place(block, me, parts, relative):
    if not relative:
        return jnp.int32(block)
    offset = me ^ block
    place = 0
    for bit in range(parts.bit_length() - 1):
        place += ((offset >> bit) & 1) << (parts.bit_length() - 2 - bit)
    return place


def feed_forward_kernel(group_count, share, up_at, relative, position, vectors, tokens, cotangent, *refs):
    mixed_groups = refs[:group_count]
    (
        mixing_up, down_shards, layer_out, near, far, hidden_low, slopes_out, normed_out, inverse_out,
        residual_grad, sums, mixing, up, down, active, slopes, total, hidden, low_grad, down_grad,
        in_sems, out_sems, slope_sems,
    ) = refs[group_count:]
    rows = tokens.shape[0]
    block = rows // 3
    chunk = down.shape[0] // 4
    mixing_copy, up_copies, down_copy = weight_copies(
        share, up_at, mixing_up, down_shards, mixing, up, down, in_sems
    )
    mixing_copy.start()
    for copy in up_copies:
        copy.start()
    down_copy.start()
    add_sum = make_adder(sums)

    def vector(index):
        return vectors[index : index + 1, :]

    sums[6:8, :] = jnp.zeros((2, D), F32)
    mixing_copy.wait()
    for index in range(3):
        at = pl.ds(index * block, block)
        mixed = jnp.concatenate([group[at, :] for group in mixed_groups], axis=1)
        attended = dot(mixed, mixing[...].reshape(D, D)) + vector(0)
        stream = tokens[at, :].astype(F32) + attended
        add_sum(0, stream * stream, index == 0)
        add_sum(1, attended * attended, index == 0)
        center = stream - jnp.mean(stream, axis=-1, keepdims=True)
        inverse = lax.rsqrt(jnp.mean(center * center, axis=-1, keepdims=True) + EPSILON)
        normed = center * inverse
        normed_out[at, :] = normed
        inverse_out[at, :] = jnp.broadcast_to(inverse, (block, LANES))
        value = normed * vector(1) + vector(2)
        hidden[at, :] = value
        hidden_low[at, :] = value.astype(BF)
    down_copy.wait()
    slope_copies = []
    for quarter in range(4):
        up_copies[quarter].wait()
        up_part = up[quarter].reshape(D, D)
        down_part = down[quarter * chunk : (quarter + 1) * chunk].reshape(D, D)
        for index in range(3):
            at = pl.ds(index * block, block)
            before = dot(hidden_low[at, :], up_part) + vector(6 + quarter)
            half = 0.5 * (1.0 + error_function(before * 0.7071067811865476))
            act = (before * half).astype(BF)
            active[quarter, at, :] = act
            slope = half + before * jnp.exp(-0.5 * before * before) * 0.3989422804014327
            slopes[quarter, at, :] = slope.astype(BF)
            part = dot(act, down_part)
            if quarter == 0:
                total[at, :] = part
            else:
                total[at, :] += part
        slope_copies.append(
            pltpu.make_async_copy(slopes.at[quarter], slopes_out.at[quarter], slope_sems.at[quarter])
        )
        slope_copies[-1].start()
    for index in range(3):
        at = pl.ds(index * block, block)
        forward_out = total[at, :] + vector(3)
        add_sum(2, forward_out * forward_out, index == 0)
        value = hidden[at, :] + forward_out
        center = value - jnp.mean(value, axis=-1, keepdims=True)
        inverse = lax.rsqrt(jnp.mean(center * center, axis=-1, keepdims=True) + EPSILON)
        normed = center * inverse
        layer_out[at, :] = (normed * vector(4) + vector(5)).astype(BF)
        upstream = cotangent[at, :].astype(F32)
        scaled = upstream * vector(4)
        inner = (
            scaled
            - jnp.mean(scaled, axis=-1, keepdims=True)
            - normed * jnp.mean(scaled * normed, axis=-1, keepdims=True)
        ) * inverse
        residual_grad[at, :] = inner
        rounded = inner.astype(BF)
        low_grad[at, :] = rounded
        add_sum(3, upstream * normed, index == 0)
        add_sum(4, upstream, index == 0)
        add_sum(5, rounded.astype(F32), index == 0)
    parts = down.shape[0]
    half_parts = parts // 2
    for quarter in range(4):
        grad = dot_lt(active[quarter], low_grad[...])
        at = pl.ds(quarter * chunk, chunk)
        down_grad[at] = grad.astype(BF).reshape(chunk, -1, D)
        for block in range(quarter * chunk, (quarter + 1) * chunk):
            place = relative_place(block, position[0], parts, relative)

            @pl.when(place < half_parts)
            def _():
                pltpu.make_async_copy(
                    down_grad.at[block], near.at[place], out_sems.at[block]
                ).start()

            @pl.when(place >= half_parts)
            def _():
                pltpu.make_async_copy(
                    down_grad.at[block], far.at[place - half_parts], out_sems.at[block]
                ).start()

    wait_all(slope_copies)
    for block in range(parts):
        pltpu.make_async_copy(down_grad.at[block], near.at[0], out_sems.at[block]).wait()


def feed_forward(position, vectors, tokens, cotangent, groups, weights, up_at, relative):
    rows = tokens.shape[0]
    parts = weights[0].shape[0]
    share = D // parts
    anywhere = pl.BlockSpec(memory_space=pl.ANY)
    vmem = pl.BlockSpec(memory_space=pltpu.VMEM)
    return call(
        functools.partial(feed_forward_kernel, len(groups), share, up_at, relative),
        50,
        in_specs=[pl.BlockSpec(memory_space=pltpu.SMEM)] + [vmem] * (3 + len(groups)) + [anywhere] * 2,
        out_specs=[vmem, anywhere, anywhere, vmem, anywhere] + [vmem] * 4,
        out_shape=[
            jax.ShapeDtypeStruct((rows, D), BF),
            jax.ShapeDtypeStruct((parts // 2, 4 * share, D), BF),
            jax.ShapeDtypeStruct((parts // 2, 4 * share, D), BF),
            jax.ShapeDtypeStruct((rows, D), BF),
            jax.ShapeDtypeStruct((4, rows, D), BF),
            jax.ShapeDtypeStruct((rows, D), F32),
            jax.ShapeDtypeStruct((rows, LANES), F32),
            jax.ShapeDtypeStruct((rows, D), F32),
            jax.ShapeDtypeStruct((8, D), F32),
        ],
        scratch_shapes=[
            pltpu.VMEM((parts, share, D), BF),
            pltpu.VMEM((4, parts, share, D), BF),
            pltpu.VMEM((parts, 4 * share, D), BF),
            pltpu.VMEM((4, rows, D), BF),
            pltpu.VMEM((4, rows, D), BF),
            pltpu.VMEM((rows, D), F32),
            pltpu.VMEM((rows, D), F32),
            pltpu.VMEM((rows, D), BF),
            pltpu.VMEM((parts, 4 * share, D), BF),
            pltpu.SemaphoreType.DMA((6,)),
            pltpu.SemaphoreType.DMA((parts,)),
            pltpu.SemaphoreType.DMA((4,)),
        ],
        name="feed_forward",
        cost_estimate=pl.CostEstimate(
            flops=12_000_000_000, transcendentals=4800000, bytes_accessed=40_000_000
        ),
    )(position, vectors, tokens, cotangent, *groups, *weights)


def feed_back_kernel(
    group_count, share, up_at, vectors, sums_before, hidden_low, normed, inverse, residual_grad, *refs
):
    mixed_groups = refs[:group_count]
    slopes_in, mixing_up, down_shards, grads_out, stream_grad, sums = refs[group_count : group_count + 6]
    refs = refs[group_count + 6 :]
    grad_groups = refs[:group_count]
    (
        mixing, up, down, slopes, hidden_turned, pre_grad, low_grad, back, up_grad, mixing_grad,
        sums_low, in_sems, out_sems, slope_sems,
    ) = refs[group_count:]
    rows = hidden_low.shape[0]
    block = rows // 3
    parts = mixing.shape[0]
    chunk = parts // 4
    mixing_copy, up_copies, down_copy = weight_copies(
        share, up_at, mixing_up, down_shards, mixing, up, down, in_sems
    )
    slope_copies = [
        pltpu.make_async_copy(slopes_in.at[quarter], slopes.at[quarter], slope_sems.at[quarter])
        for quarter in range(4)
    ]
    down_copy.start()
    for quarter in range(4):
        slope_copies[quarter].start()
        up_copies[quarter].start()
    mixing_copy.start()
    add_sum = make_adder(sums)

    def vector(index):
        return vectors[index : index + 1, :]

    sums[7:8, :] = jnp.zeros((1, D), F32)
    low_grad[...] = residual_grad[...].astype(BF)
    hidden_turned[...] = hidden_low[...].T
    down_copy.wait()
    grad_copies = []
    for quarter in range(4):
        slope_copies[quarter].wait()
        up_copies[quarter].wait()
        up_part = up[quarter].reshape(D, D)
        down_part = down[quarter * chunk : (quarter + 1) * chunk].reshape(D, D)
        for index in range(3):
            at = pl.ds(index * block, block)
            part = (dot_rt(low_grad[at, :], down_part) * slopes[quarter, at, :].astype(F32)).astype(BF)
            pre_grad[quarter % 2, at, :] = part
            add_sum(3 + quarter, part.astype(F32), index == 0)
            back_part = dot_rt(part, up_part)
            if quarter == 0:
                back[at, :] = back_part
            else:
                back[at, :] += back_part
        grad = dot(hidden_turned[...], pre_grad[quarter % 2])
        up_grad[quarter] = grad.astype(BF).reshape(parts, share, D)
        grad_copies.append(
            pltpu.make_async_copy(
                up_grad.at[quarter],
                grads_out.at[:, pl.ds((1 + quarter) * share, share)],
                out_sems.at[quarter],
            )
        )
        grad_copies[-1].start()
    mixing_copy.wait()
    for index in range(3):
        at = pl.ds(index * block, block)
        hidden_grad = residual_grad[at, :] + back[at, :]
        norm = normed[at, :]
        scaled = hidden_grad * vector(1)
        inner = (
            scaled
            - jnp.mean(scaled, axis=-1, keepdims=True)
            - norm * jnp.mean(scaled * norm, axis=-1, keepdims=True)
        ) * inverse[at, 0:1]
        stream_grad[at, :] = inner
        rounded = inner.astype(BF)
        low_grad[at, :] = rounded
        add_sum(0, hidden_grad * norm, index == 0)
        add_sum(1, hidden_grad, index == 0)
        add_sum(2, rounded.astype(F32), index == 0)
        mixed_grad = dot_rt(rounded, mixing[...].reshape(D, D)).astype(BF)
        start = 0
        for group in grad_groups:
            width = group.shape[1]
            group[at, :] = mixed_grad[:, start : start + width]
            start += width
    start = 0
    for group in mixed_groups:
        width = group.shape[1]
        back[start : start + width, :] = dot_lt(group[...], low_grad[...])
        start += width
    mixing_grad[...] = back[...].astype(BF).reshape(parts, share, D)
    grad_copies.append(
        pltpu.make_async_copy(mixing_grad, grads_out.at[:, pl.ds(0, share)], out_sems.at[4])
    )
    grad_copies[-1].start()
    both_sums = jnp.concatenate([sums_before[...], sums[...]], axis=0).astype(BF)
    sums_low[...] = jnp.broadcast_to(both_sums[None], sums_low.shape)
    grad_copies.append(
        pltpu.make_async_copy(sums_low, grads_out.at[:, pl.ds(5 * share, SUM_ROWS)], out_sems.at[5])
    )
    grad_copies[-1].start()
    wait_all(grad_copies)


def feed_back(vectors, sums_before, saved, groups, weights, up_at):
    hidden_low, slopes, normed, inverse, residual_grad = saved
    rows = hidden_low.shape[0]
    parts = weights[0].shape[0]
    share = D // parts
    anywhere = pl.BlockSpec(memory_space=pl.ANY)
    vmem = pl.BlockSpec(memory_space=pltpu.VMEM)
    return call(
        functools.partial(feed_back_kernel, len(groups), share, up_at),
        50,
        in_specs=[vmem] * (6 + len(groups)) + [anywhere] * 3,
        out_specs=[anywhere] + [vmem] * (2 + len(groups)),
        out_shape=[
            jax.ShapeDtypeStruct((parts, 5 * share + SUM_ROWS, D), BF),
            jax.ShapeDtypeStruct((rows, D), F32),
            jax.ShapeDtypeStruct((8, D), F32),
        ]
        + [jax.ShapeDtypeStruct(group.shape, BF) for group in groups],
        scratch_shapes=[
            pltpu.VMEM((parts, share, D), BF),
            pltpu.VMEM((4, parts, share, D), BF),
            pltpu.VMEM((parts, 4 * share, D), BF),
            pltpu.VMEM((4, rows, D), BF),
            pltpu.VMEM((D, rows), BF),
            pltpu.VMEM((2, rows, D), BF),
            pltpu.VMEM((rows, D), BF),
            pltpu.VMEM((rows, D), F32),
            pltpu.VMEM((4, parts, share, D), BF),
            pltpu.VMEM((parts, share, D), BF),
            pltpu.VMEM((parts, SUM_ROWS, D), BF),
            pltpu.SemaphoreType.DMA((6,)),
            pltpu.SemaphoreType.DMA((6,)),
            pltpu.SemaphoreType.DMA((4,)),
        ],
        name="feed_back",
        cost_estimate=pl.CostEstimate(
            flops=13_000_000_000, transcendentals=0, bytes_accessed=40_000_000
        ),
    )(vectors, sums_before, hidden_low, normed, inverse, residual_grad, *groups, slopes, *weights)


def swap(value, bit, axis="dp"):
    size = lax.axis_size(axis)
    return lax.ppermute(value, axis, [(index, index ^ bit) for index in range(size)])


def relative_offsets(size):
    offsets = [0]
    bit = size // 2
    while bit:
        offsets += [offset ^ bit for offset in offsets]
        bit //= 2
    return offsets


tie = lax.optimization_barrier


def join(*values):
    return jnp.concatenate(values, axis=1)


def scatter_start(near, far):
    return near, swap(far, 1)


def scatter_next(kept, received, bit, axis="dp"):
    half = kept.shape[1] // 2
    first = kept[:, :half] + received[:, :half]
    second = kept[:, half:] + received[:, half:]
    return first, swap(second, bit, axis)


def local(
    tokens,
    entity_flags,
    query_weight,
    key_weight,
    value_weight,
    mixing_weight,
    mixing_bias,
    first_gain,
    first_bias,
    up_weight,
    up_bias,
    down_weight,
    down_bias,
    second_gain,
    second_bias,
    cotangent,
):
    parts = lax.axis_size("dp")
    me = lax.axis_index("dp")
    share = D // parts
    rows = tokens.shape[0]
    by_swaps = share % 16 == 0 and parts & (parts - 1) == 0 and parts > 8

    six = jnp.concatenate([query_weight, key_weight[None], value_weight[None]], axis=0)
    pairs = jnp.transpose(six.reshape(6, share, PAIRS, LANES), (2, 1, 0, 3)).reshape(PAIRS, share, D)
    up_shard = jnp.transpose(up_weight.reshape(share, 4, D), (1, 0, 2)).reshape(4 * share, D)
    small = (mixing_bias, first_gain, first_bias, down_bias, second_gain, second_bias)
    vector_shard = jnp.concatenate([jnp.stack(small), up_bias.reshape(4, share)], axis=0)

    offsets = relative_offsets(parts) if by_swaps else list(range(parts))
    order = me ^ jnp.array(offsets, jnp.int32) if by_swaps else jnp.array(offsets, jnp.int32)
    column_of = (order[:, None] * share + jnp.arange(share, dtype=jnp.int32)[None, :]).reshape(D)
    choose = (lax.broadcasted_iota(jnp.int32, (D, D), 0) == column_of[None, :]).astype(BF)
    entity = entity_flags.astype(F32)
    tokens_other = swap(tokens, 1, "seq")
    entity_other = swap(entity, 1, "seq")

    shards = []
    start = 0
    for count in FORWARD_GROUPS:
        shards.append(pairs[start : start + count])
        start += count
    count = len(shards)
    vector_rows = 16
    own = dot(tokens, choose).astype(BF)
    if by_swaps:
        padded = jnp.zeros((vector_rows, D), BF).at[0, : 10 * share].set(vector_shard.reshape(-1))
        middle_shard = jnp.concatenate([mixing_weight, padded, up_shard, down_weight], axis=0)
        up_at, down_at = share + vector_rows, 5 * share + vector_rows
    else:
        groups = []
        for shard in shards:
            full = lax.all_gather(shard, "dp", axis=1, tiled=True)
            groups.append([full.reshape(full.shape[0], 1, D, D)])
        mixing_full, up_full, down_full = (
            lax.all_gather(weight, "dp", axis=0, tiled=True)
            for weight in (mixing_weight, up_weight, down_weight)
        )
        quarter = D // 4
        up_quarters = jnp.transpose(up_full.reshape(4, quarter, 4, D), (0, 2, 1, 3)).reshape(4, D, D)
        mixing_up = jnp.concatenate([mixing_full.reshape(4, quarter, D), up_quarters], axis=1)
        down_shards = down_full.reshape(4, D, D)
        up_at, down_at = quarter, 0
        vectors = lax.all_gather(vector_shard, "dp", axis=0)
    own_entity = jnp.broadcast_to(entity[:, None], (rows, LANES))

    def partner():
        return dot(tokens_other, choose).astype(BF), jnp.broadcast_to(entity_other[:, None], (rows, LANES))

    saved = [None] * count
    if by_swaps:
        side = lax.axis_index("seq")
        groups = [None] * count
        held = [jnp.expand_dims(shard, 1) for shard in shards]
        for g in range(1, count):
            held[g] = lax.dynamic_slice_in_dim(held[g], side * (D // 2), D // 2, 3)
        beside = [None] * count
        bits = [1 << k for k in reversed(range(parts.bit_length() - 1))]
        plans = [[("dp", bit) for bit in bits]] + [
            [("dp", bit) for bit in bits[:-1]] + [("seq", 1), ("dp", 1)] for _ in range(count - 1)
        ]

        def whole_columns(mine, theirs):
            first = side == 0
            return jnp.concatenate([jnp.where(first, mine, theirs), jnp.where(first, theirs, mine)], axis=3)

        other, other_entity = None, None
        for step in range(max(len(plan) + g for g, plan in enumerate(plans))):
            active = [g for g in range(count) if 0 <= step - g < len(plans[g])]
            moved = {}
            for g in active:
                axis, bit = plans[g][step - g]
                both_parts = axis == "seq" or bit == 1
                moved[g] = (swap(held[g], bit, axis),) + ((swap(beside[g], bit, axis),) if both_parts else ())
            done = None
            for g in active:
                if plans[g][step - g] == ("dp", 1):
                    groups[g] = [held[g], beside[g], *moved.pop(g)]
                    if g == 0:
                        other, other_entity = partner()
                        both = (own, other, own_entity, other_entity)
                    saved[g] = attention_forward(*both, groups[g])
                    done = g
            waiting = sorted(moved)
            later = [held[g] for g in range(step + 1, min(step + 2, count))]
            tied = tie((
                tuple(moved[g] for g in waiting), None if done is None else saved[done][0], later, middle_shard
            ))
            if step == MIDDLE_STEP:
                gathered = lax.all_gather(tied[3], "dp", axis=0)
            if done is not None:
                saved[done] = (tied[1], *saved[done][1:])
            for g, value in zip(range(step + 1, min(step + 2, count)), tied[2]):
                held[g] = value
            for g, value in zip(waiting, tied[0]):
                axis, bit = plans[g][step - g]
                if axis == "seq":
                    held[g], beside[g] = whole_columns(held[g], value[0]), whole_columns(beside[g], value[1])
                elif bit == 2:
                    beside[g] = value[0]
                else:
                    held[g] = join(held[g], value[0])
        mixing_up = down_shards = gathered
        vectors = gathered[:, share, : 10 * share].reshape(parts, 10, share)
    else:
        other, other_entity = partner()
        both = (own, other, own_entity, other_entity)
        saved = [attention_forward(*both, pieces) for pieces in groups]
    up_vector = vectors[:, 6:].reshape(parts * 4 * share).reshape(4, D)
    vectors = jnp.concatenate(
        [jnp.transpose(vectors[:, :6], (1, 0, 2)).reshape(6, D), up_vector, jnp.zeros((6, D), BF)], axis=0
    ).astype(F32)
    middle = (mixing_up, down_shards)
    mixed = [item[0] for item in saved]
    position = (me if by_swaps else jnp.int32(0)).astype(jnp.int32).reshape(1)
    (
        layer_out, down_near, down_far, hidden_low, slopes, normed, inverse, residual_grad, sums_one,
    ) = feed_forward(position, vectors, tokens, cotangent, mixed, middle, (up_at, down_at), by_swaps)

    def over_pieces(value):
        return value.astype(F32) + swap(value, 1, "seq").astype(F32)

    def next_bit(item):
        return parts // item[0].shape[1]

    if by_swaps:
        down_state = scatter_start(down_near[None], down_far[None])
    middle_grad, stream_grad, sums_two, *mixed_grads = feed_back(
        vectors, sums_one, (hidden_low, slopes, normed, inverse, residual_grad), mixed, middle,
        (up_at, down_at),
    )

    joined, received, near, far = ([None] * count for _ in range(4))
    state = []

    def advance(items):
        return [scatter_next(*item, next_bit(item)) if next_bit(item) < parts else item for item in items]

    def start_group(index):
        shape = (near[index].shape[0], parts // 2, share, D)
        return scatter_start(near[index].reshape(shape), far[index].reshape(shape))

    for index in reversed(range(count)):
        if by_swaps:
            after = near[index + 1] if index + 1 < count else None
            tied = tie((mixed_grads[index], down_state, state, after))
            mixed_grads[index], down_state, state, after = tied
            (down_state,) = advance([down_state])
            state = advance(state)
            if after is not None:
                near[index + 1] = after
                state.append(start_group(index + 1))
        near[index], far[index], joined[index], joined_other = attention_backward(
            *both, saved[index], mixed_grads[index]
        )
        received[index] = swap(joined_other, 1, "seq")
    before = None

    if by_swaps:
        middle_sum = lax.psum_scatter(middle_grad, "dp", scatter_dimension=0, tiled=True)[0]
        near[0], far[0], down_state, state = tie((near[0], far[0], down_state, state))
        state = advance(state) + [start_group(0)]
        ends = [None] * count

        def settle(items):
            for k, item in enumerate(items):
                if next_bit(item) == parts and ends[k] is None:
                    ends[k] = over_pieces((item[0] + item[1])[:, 0])
            return advance(items)

        for index in reversed(range(count)):
            finish = (choose, stream_grad) if index == 0 else None
            before = token_gradient(groups[index], joined[index], received[index], before, finish)
            before, state, down_state, middle_sum = tie((before, state, down_state, middle_sum))
            state = settle(state)
            if index == count - 1:
                down_sum = (down_state[0] + down_state[1])[0, 0]
                outer = over_pieces(jnp.concatenate([middle_sum, down_sum], axis=0))
        tokens_grad = before
        while any(end is None for end in ends):
            state = settle(tie(state))
        mixing_sum = outer[:share]
        up_sum = outer[share : 5 * share].reshape(4, share, D)
        sums = outer[5 * share : 5 * share + SUM_ROWS]
        down_sum = outer[5 * share + SUM_ROWS :]
        pair_sum = jnp.concatenate(list(reversed(ends)), axis=0)
    else:
        for index in reversed(range(1, count)):
            before = token_gradient(groups[index], joined[index], received[index], before)
        tokens_grad = token_gradient(groups[0], joined[0], received[0], before, (choose, stream_grad))
        sums = lax.psum(jnp.concatenate([sums_one, sums_two], axis=0), ("dp", "seq"))

        def reduced(value, axis):
            piece = lax.psum_scatter(value, "dp", scatter_dimension=axis, tiled=True)
            return lax.psum(piece, "seq").astype(F32)

        down_sum = reduced(jnp.concatenate([down_near, down_far], axis=0).reshape(-1, D), 0)
        mixing_sum = reduced(middle_grad[:, :quarter].reshape(D, D), 0)
        up_quarters = middle_grad[:, quarter : 5 * quarter].reshape(4, 4, quarter, D)
        up_sum = reduced(jnp.transpose(up_quarters, (1, 0, 2, 3)).reshape(4, D, D), 1)
        pair_sum = jnp.concatenate(
            [reduced(jnp.concatenate([a, b], axis=1), 1) for a, b in zip(near, far)], axis=0
        )

    six_sum = jnp.transpose(pair_sum.reshape(PAIRS, share, 6, LANES), (2, 1, 0, 3)).reshape(6, share, D)
    up_out = jnp.transpose(up_sum, (1, 0, 2)).reshape(share, 4 * D)

    def shard(row, width=1):
        return lax.dynamic_slice(sums[row : row + width].reshape(-1), (me * share * width,), (share * width,))

    token_count = rows * parts * lax.axis_size("seq")
    stream_rms = jnp.sqrt(jnp.sum(sums[0:3], axis=1) / (token_count * D))
    return (
        layer_out,
        tokens_grad,
        six_sum[0:4],
        six_sum[4],
        six_sum[5],
        mixing_sum,
        shard(10),
        shard(8),
        shard(9),
        up_out,
        shard(11, 4),
        down_sum,
        shard(5),
        shard(3),
        shard(4),
        stream_rms,
    )


def solution(mesh):
    rows = P(("dp", "seq"), None)
    vector = P("dp")
    matrix = P("dp", None)
    stacked = P(None, "dp", None)
    in_specs = (
        rows, P(("dp", "seq")), stacked, matrix, matrix, matrix, vector, vector, vector, matrix,
        vector, matrix, vector, vector, vector, rows,
    )
    out_specs = (
        rows, rows, stacked, matrix, matrix, matrix, vector, vector, vector, matrix, vector,
        matrix, vector, vector, vector, P(),
    )
    return jax.shard_map(local, mesh=mesh, in_specs=in_specs, out_specs=out_specs, check_vma=False)
```

```python
import functools

import jax
import jax.numpy as jnp
from jax import lax
from jax.experimental import pallas as pl
from jax.experimental.pallas import tpu as pltpu
from jax.sharding import PartitionSpec as P

D = 768
HEADS = 12
HD = 64
PAIRS = HEADS // 2
LANES = 2 * HD
F32 = jnp.float32
BF = jnp.bfloat16
EPSILON = 1e-05
LN2 = 0.6931471805599453
QUERY_SCALE = HD**-0.5 / LN2
FORWARD_GROUPS = (1, 2, 3)
SUM_ROWS = 16
MIDDLE_STEP = 0
MIB = 1024 * 1024


def dot(left, right):
    return jnp.dot(left, right, preferred_element_type=F32)


def dot_rt(left, right):
    return lax.dot_general(left, right, (((1,), (1,)), ((), ())), preferred_element_type=F32)


def dot_lt(left, right):
    return lax.dot_general(left, right, (((0,), (0,)), ((), ())), preferred_element_type=F32)


def call(kernel, mebibytes, **kwargs):
    return pl.pallas_call(
        kernel, compiler_params=pltpu.CompilerParams(vmem_limit_bytes=mebibytes * MIB), **kwargs
    )


def whole_block(shape):
    return pl.BlockSpec(shape, lambda step: (0,) * len(shape))


def pair_block(shape):
    return pl.BlockSpec((1,) + shape, lambda step: (step,) + (0,) * len(shape))


def attention_forward_kernel(piece_count, own, other, own_entity, other_entity, *refs):
    pieces = refs[:piece_count]
    mixed, queries, keys, values, weights, totals, key_masked, value_ones, packed = refs[piece_count:]
    rows = own.shape[0]
    block = rows // 2
    lane = lax.broadcasted_iota(jnp.int32, (rows, LANES), 1)
    low = lane < HD
    at = 0
    for piece in pieces:
        part = piece[0].reshape(-1, D)
        packed[at : at + part.shape[0], :] = part
        at += part.shape[0]
    is_own = own_entity[...]
    is_other = other_entity[...]
    projected = dot(own[...], packed[...])
    entity_row = is_own > 0.5
    to_word = jnp.where(entity_row, projected[:, 256:384], projected[:, 0:128]) * QUERY_SCALE
    to_entity = jnp.where(entity_row, projected[:, 384:512], projected[:, 128:256]) * QUERY_SCALE
    queries[0, :, 0:LANES] = jnp.where(low, to_word, pltpu.roll(to_entity, HD, 1)).astype(BF)
    queries[0, :, LANES:] = jnp.where(low, pltpu.roll(to_word, HD, 1), to_entity).astype(BF)
    projected_other = dot(other[...], packed[:, 512:768])
    halves = (
        (projected[:, 512:640], projected[:, 640:768], is_own),
        (projected_other[:, 0:128], projected_other[:, 128:256], is_other),
    )
    for half, (key, value, entity) in enumerate(halves):
        at = pl.ds(half * rows, rows)
        keys[0, at, :] = key.astype(BF)
        values[0, at, :] = value.astype(BF)
        mask = jnp.where(low, 1.0 - entity, entity)
        turned = pltpu.roll(key, HD, 1)
        key_masked[at, 0:LANES] = (jnp.where(low, key, turned) * mask).astype(BF)
        key_masked[at, LANES:] = (jnp.where(low, turned, key) * mask).astype(BF)
        ones = jnp.ones_like(value)
        value_ones[at, 0:LANES] = jnp.where(low, value, ones).astype(BF)
        value_ones[at, LANES:] = jnp.where(low, ones, value).astype(BF)
    items = [(index, head) for index in range(rows // block) for head in range(2)]

    def scores_of(item):
        index, head = item
        columns = pl.ds(head * LANES, LANES)
        return dot_rt(queries[0, pl.ds(index * block, block), columns], key_masked[:, columns])

    ahead = scores_of(items[0])
    sums = []
    for number, (index, head) in enumerate(items):
        scores = ahead
        if number + 1 < len(items):
            ahead = scores_of(items[number + 1])
        at = pl.ds(index * block, block)
        highest = jnp.max(scores, axis=-1, keepdims=True)
        weight = jnp.exp2(scores - highest).astype(BF)
        weights[0, head, at, :] = weight
        sums.append(dot(weight, value_ones[:, pl.ds(head * LANES, LANES)]))
        if head:
            upper = jnp.where(low[:block], sums[0], sums[1])
            total = pltpu.roll(jnp.where(low[:block], sums[1], sums[0]), HD, 1)
            mixed[at, :] = (upper / total).astype(BF)
            totals[0, at, :] = total
            sums = []


def piece_blocks(pieces):
    return [pair_block(piece.shape[1:]) for piece in pieces]


def attention_forward(own, other, own_entity, other_entity, pieces):
    count = pieces[0].shape[0]
    rows = own.shape[0]
    length = 2 * rows
    return call(
        functools.partial(attention_forward_kernel, len(pieces)),
        30,
        grid=(count,),
        in_specs=[whole_block((rows, D))] * 2 + [whole_block((rows, LANES))] * 2 + piece_blocks(pieces),
        out_specs=[
            pl.BlockSpec((rows, LANES), lambda step: (0, step)),
            pair_block((rows, 2 * LANES)),
            pair_block((length, LANES)),
            pair_block((length, LANES)),
            pair_block((2, rows, length)),
            pair_block((rows, LANES)),
        ],
        out_shape=[
            jax.ShapeDtypeStruct((rows, LANES * count), BF),
            pltpu.HBM((count, rows, 2 * LANES), BF),
            pltpu.HBM((count, length, LANES), BF),
            pltpu.HBM((count, length, LANES), BF),
            pltpu.HBM((count, 2, rows, length), BF),
            pltpu.HBM((count, rows, LANES), F32),
        ],
        scratch_shapes=[
            pltpu.VMEM((length, 2 * LANES), BF),
            pltpu.VMEM((length, 2 * LANES), BF),
            pltpu.VMEM((D, D), BF),
        ],
        name="attention_forward",
        cost_estimate=pl.CostEstimate(
            flops=count * 7_000_000_000, transcendentals=count * 2400000, bytes_accessed=count * 8_000_000
        ),
    )(own, other, own_entity, other_entity, *pieces)


def attention_backward_kernel(own, other, own_entity, other_entity, *refs):
    queries, keys, values, weights, totals, mixed, grad = refs[:7]
    near, far, joined, joined_other = refs[7:11]
    key_masked, value_ones, grad_wide, query_grad, key_grad, value_grad = refs[11:]
    rows = own.shape[0]
    block = rows // 3
    lane = lax.broadcasted_iota(jnp.int32, (rows, LANES), 1)
    low = lane < HD
    is_own = own_entity[...]
    is_other = other_entity[...]
    for half, entity in enumerate((is_own, is_other)):
        at = pl.ds(half * rows, rows)
        key = keys[0, at, :].astype(F32)
        turned = pltpu.roll(key, HD, 1)
        mask = jnp.where(low, 1.0 - entity, entity)
        key_masked[at, 0:LANES] = (jnp.where(low, key, turned) * mask).astype(BF)
        key_masked[at, LANES:] = (jnp.where(low, turned, key) * mask).astype(BF)
        value = values[0, at, :].astype(F32)
        ones = jnp.where(lane % HD < 2, 1.0, 0.0)
        value_ones[at, 0:LANES] = jnp.where(low, value, ones).astype(BF)
        value_ones[at, LANES:] = jnp.where(low, ones, value).astype(BF)
    scaled = grad[...].astype(F32) / totals[0]
    inner = scaled * mixed[...].astype(F32)

    def correction(inner_sum):
        upper = inner_sum.astype(BF).astype(F32)
        return jnp.where(
            lane % HD == 0, -upper, jnp.where(lane % HD == 1, upper - inner_sum, 0.0)
        )

    first_inner = jnp.sum(jnp.where(low, inner, 0.0), axis=-1, keepdims=True)
    second_inner = jnp.sum(jnp.where(low, 0.0, inner), axis=-1, keepdims=True)
    grad_wide[:, 0:LANES] = jnp.where(low, scaled, correction(first_inner)).astype(BF)
    grad_wide[:, LANES:] = jnp.where(low, correction(second_inner), scaled).astype(BF)
    for head in range(2):
        columns = pl.ds(head * LANES, LANES)
        for index in range(rows // block):
            at = pl.ds(index * block, block)
            grad_block = grad_wide[at, columns]
            weight = weights[0, head, at, :]
            score_grad = (weight.astype(F32) * dot_rt(grad_block, value_ones[:, columns])).astype(BF)
            query_grad[at, columns] = dot(score_grad, key_masked[:, columns]) * HD**-0.5
            query_turned = queries[0, at, columns].astype(F32).T.astype(BF)
            grad_turned = grad_block.astype(F32).T[head * HD : (head + 1) * HD].astype(BF)
            key_part = dot(query_turned, score_grad)
            value_part = dot(grad_turned, weight)
            key_at = pl.ds(head * LANES, LANES)
            value_at = pl.ds(head * HD, HD)
            if index == 0:
                key_grad[key_at, :] = key_part
                value_grad[value_at, :] = value_part
            else:
                key_grad[key_at, :] += key_part
                value_grad[value_at, :] += value_part
    query_a = query_grad[:, 0:LANES]
    query_b = query_grad[:, LANES:]
    word_grad = jnp.where(low, query_a, pltpu.roll(query_b, HD, 1))
    entity_grad = jnp.where(low, pltpu.roll(query_a, HD, 1), query_b)
    is_word = 1.0 - is_own
    joined[0, :, 0:128] = (is_word * word_grad).astype(BF)
    joined[0, :, 128:256] = (is_word * entity_grad).astype(BF)
    joined[0, :, 256:384] = (is_own * word_grad).astype(BF)
    joined[0, :, 384:512] = (is_own * entity_grad).astype(BF)
    key_back = key_grad[...].T
    value_back = value_grad[...].T
    for half, entity in enumerate((is_own, is_other)):
        at = slice(half * rows, half * rows + rows)
        key_a = key_back[at, 0:LANES]
        key_b = key_back[at, LANES:]
        key_word = jnp.where(low, key_a, pltpu.roll(key_b, HD, 1))
        key_entity = jnp.where(low, pltpu.roll(key_a, HD, 1), key_b)
        key_part = (jnp.where(entity > 0.5, key_entity, key_word) * LN2).astype(BF)
        value_part = value_back[at].astype(BF)
        if half == 0:
            joined[0, :, 512:640] = key_part
            joined[0, :, 640:768] = value_part
        else:
            joined_other[0, :, 0:128] = key_part
            joined_other[0, :, 128:256] = value_part
    here = dot_lt(own[...], joined[0])
    there = dot_lt(other[...], joined_other[0])
    for target, at in ((near, slice(0, D // 2)), (far, slice(D // 2, D))):
        target[0, :, 0:512] = here[at, 0:512].astype(BF)
        target[0, :, 512:768] = (here[at, 512:768] + there[at]).astype(BF)


def attention_backward(own, other, own_entity, other_entity, saved, grad, mebibytes):
    mixed, queries, keys, values, weights, totals = saved
    count = queries.shape[0]
    rows = own.shape[0]
    length = 2 * rows
    column = pl.BlockSpec((rows, LANES), lambda step: (0, step))
    return call(
        attention_backward_kernel,
        mebibytes,
        grid=(count,),
        in_specs=[whole_block((rows, D))] * 2
        + [whole_block((rows, LANES))] * 2
        + [
            pair_block((rows, 2 * LANES)),
            pair_block((length, LANES)),
            pair_block((length, LANES)),
            pair_block((2, rows, length)),
            pair_block((rows, LANES)),
            column,
            column,
        ],
        out_specs=[pair_block((D // 2, D))] * 2 + [pair_block((rows, D)), pair_block((rows, 2 * LANES))],
        out_shape=[jax.ShapeDtypeStruct((count, D // 2, D), BF)] * 2
        + [
            jax.ShapeDtypeStruct((count, rows, D), BF),
            jax.ShapeDtypeStruct((count, rows, 2 * LANES), BF),
        ],
        scratch_shapes=[
            pltpu.VMEM((length, 2 * LANES), BF),
            pltpu.VMEM((length, 2 * LANES), BF),
            pltpu.VMEM((rows, 2 * LANES), BF),
            pltpu.VMEM((rows, 2 * LANES), F32),
            pltpu.VMEM((2 * LANES, length), F32),
            pltpu.VMEM((LANES, length), F32),
        ],
        name="attention_backward",
        cost_estimate=pl.CostEstimate(
            flops=count * 10_000_000_000, transcendentals=0, bytes_accessed=count * 12_000_000
        ),
    )(own, other, own_entity, other_entity, queries, keys, values, weights, totals, mixed, grad)


def token_gradient_kernel(piece_count, first, *refs):
    pieces = refs[:piece_count]
    refs = refs[piece_count:]
    joined, joined_other = refs[:2]
    refs = refs[2:]
    before = ()
    if not first:
        before, refs = refs[:2], refs[2:]
    *totals, packed = refs
    at = 0
    for piece in pieces:
        part = piece[0].reshape(-1, D)
        packed[at : at + part.shape[0], :] = part
        at += part.shape[0]
    step = pl.program_id(0)
    parts = (dot_rt(joined[0], packed[...]), dot_rt(joined_other[0], packed[:, 512:768]))
    for index, (total, part) in enumerate(zip(totals, parts)):

        @pl.when(step == 0)
        def _():
            total[...] = part if first else before[index][...] + part

        @pl.when(step > 0)
        def _():
            total[...] += part


def token_gradient(pieces, joined, joined_other, before):
    count, rows, _ = joined.shape
    first = before is None
    return call(
        functools.partial(token_gradient_kernel, len(pieces), first),
        16,
        grid=(count,),
        in_specs=piece_blocks(pieces)
        + [pair_block((rows, D)), pair_block((rows, 2 * LANES))]
        + [whole_block((rows, D))] * (0 if first else 2),
        out_specs=[whole_block((rows, D))] * 2,
        out_shape=[jax.ShapeDtypeStruct((rows, D), F32)] * 2,
        scratch_shapes=[pltpu.VMEM((D, D), BF)],
        name="token_gradient",
        cost_estimate=pl.CostEstimate(
            flops=count * 1_200_000_000, transcendentals=0, bytes_accessed=count * 4_000_000
        ),
    )(*pieces, joined, joined_other, *(before or ()))


def finish_kernel(own, received, choose, stream_grad, out):
    value = own[...] + received[...].astype(F32)
    upper = value.astype(BF)
    lower = (value - upper.astype(F32)).astype(BF)
    out[...] = (stream_grad[...] + dot_rt(upper, choose[...]) + dot_rt(lower, choose[...])).astype(BF)


def finish_tokens(own, received, choose, stream_grad):
    return call(
        finish_kernel,
        16,
        in_specs=[pl.BlockSpec(memory_space=pltpu.VMEM)] * 4,
        out_specs=pl.BlockSpec(memory_space=pltpu.VMEM),
        out_shape=jax.ShapeDtypeStruct(own.shape, BF),
        name="finish_tokens",
        cost_estimate=pl.CostEstimate(flops=2_000_000_000, transcendentals=0, bytes_accessed=8_000_000),
    )(own, received, choose, stream_grad)


def error_function(value):
    value = jnp.clip(value, -3.7439211627767994, 3.7439211627767994)
    square = value * value
    upper = jnp.float32(0.00022905065861350646)
    for term in (
        0.0034082910107109506, 0.050955695062380861, 0.18520832239976145, 1.128379143519084,
    ):
        upper = upper * square + term
    lower = jnp.float32(-1.1791602954361697e-7)
    for term in (
        0.000023547966471313185, 0.0010179625278914885, 0.014070470171167667,
        0.11098505178285362, 0.49746925110067538, 1.0,
    ):
        lower = lower * square + term
    return value * upper / lower


def wait_all(copies):
    for copy in copies:
        copy.wait()


def weight_copies(share, starts, mixing_up, down_shards, mixing, up, down, sems):
    return (
        pltpu.make_async_copy(mixing_up.at[:, pl.ds(0, share)], mixing, sems.at[0]),
        [
            pltpu.make_async_copy(
                mixing_up.at[:, pl.ds(starts[0] + quarter * share, share)], up.at[quarter], sems.at[1 + quarter]
            )
            for quarter in range(4)
        ],
        pltpu.make_async_copy(down_shards.at[:, pl.ds(starts[1], 4 * share)], down, sems.at[5]),
    )


def arrivals(pairs, sems):
    return [
        pltpu.make_async_copy(source, target, sems.at[index]) for index, (source, target) in enumerate(pairs)
    ]


def side_by_side(groups, target):
    pairs = []
    start = 0
    for group in groups:
        width = group.shape[1]
        pairs.append((group, target.at[:, pl.ds(start, width)]))
        start += width
    return pairs


def make_adder(sums):
    def add_sum(index, value, start):
        part = jnp.sum(value, axis=0, keepdims=True)
        if start:
            sums[index : index + 1, :] = part
        else:
            sums[index : index + 1, :] += part

    return add_sum


def halving_bits(parts):
    return [1 << k for k in range(parts.bit_length() - 1)]


def relative_place(block, me, parts, relative):
    if not relative:
        return jnp.int32(block)
    offset = me ^ block
    place = 0
    for bit in halving_bits(parts):
        place = 2 * place + jnp.where(offset & bit, 1, 0)
    return place


def feed_forward_kernel(group_count, share, up_at, relative, position, vectors, tokens_in, cotangent_in, *refs):
    mixed_groups = refs[:group_count]
    (
        mixing_up, down_shards, layer_out, near, far, hidden_low, slopes_out, normed_out, inverse_out,
        residual_grad, sums, mixing, up, down, active, slopes, total, hidden, low_grad, down_grad,
        in_sems, out_sems, slope_sems, mixed, tokens, cotangent, row_sems,
    ) = refs[group_count:]
    rows = tokens.shape[0]
    block = rows // 3
    row_copies = arrivals(
        [*side_by_side(mixed_groups, mixed), (tokens_in, tokens), (cotangent_in, cotangent)], row_sems
    )
    chunk = down.shape[0] // 4
    mixing_copy, up_copies, down_copy = weight_copies(
        share, up_at, mixing_up, down_shards, mixing, up, down, in_sems
    )
    mixing_copy.start()
    for copy in row_copies:
        copy.start()
    for copy in up_copies:
        copy.start()
    down_copy.start()
    add_sum = make_adder(sums)

    def vector(index):
        return vectors[index : index + 1, :]

    sums[6:8, :] = jnp.zeros((2, D), F32)
    mixing_copy.wait()
    wait_all(row_copies[:-1])
    for index in range(3):
        at = pl.ds(index * block, block)
        attended = dot(mixed[at, :], mixing[...].reshape(D, D)) + vector(0)
        stream = tokens[at, :].astype(F32) + attended
        add_sum(0, stream * stream, index == 0)
        add_sum(1, attended * attended, index == 0)
        center = stream - jnp.mean(stream, axis=-1, keepdims=True)
        inverse = lax.rsqrt(jnp.mean(center * center, axis=-1, keepdims=True) + EPSILON)
        normed = center * inverse
        normed_out[at, :] = normed
        inverse_out[at, :] = jnp.broadcast_to(inverse, (block, LANES))
        value = normed * vector(1) + vector(2)
        hidden[at, :] = value
        hidden_low[at, :] = value.astype(BF)
    down_copy.wait()
    slope_copies = []
    for quarter in range(4):
        up_copies[quarter].wait()
        up_part = up[quarter].reshape(D, D)
        down_part = down[quarter * chunk : (quarter + 1) * chunk].reshape(D, D)
        for index in range(3):
            at = pl.ds(index * block, block)
            before = dot(hidden_low[at, :], up_part) + vector(6 + quarter)
            half = 0.5 * (1.0 + error_function(before * 0.7071067811865476))
            act = (before * half).astype(BF)
            active[quarter, at, :] = act
            slope = half + before * jnp.exp(-0.5 * before * before) * 0.3989422804014327
            slopes[quarter, at, :] = slope.astype(BF)
            part = dot(act, down_part)
            if quarter == 0:
                total[at, :] = part
            else:
                total[at, :] += part
        slope_copies.append(
            pltpu.make_async_copy(slopes.at[quarter], slopes_out.at[quarter], slope_sems.at[quarter])
        )
        slope_copies[-1].start()
    row_copies[-1].wait()
    for index in range(3):
        at = pl.ds(index * block, block)
        forward_out = total[at, :] + vector(3)
        add_sum(2, forward_out * forward_out, index == 0)
        value = hidden[at, :] + forward_out
        center = value - jnp.mean(value, axis=-1, keepdims=True)
        inverse = lax.rsqrt(jnp.mean(center * center, axis=-1, keepdims=True) + EPSILON)
        normed = center * inverse
        layer_out[at, :] = (normed * vector(4) + vector(5)).astype(BF)
        upstream = cotangent[at, :].astype(F32)
        scaled = upstream * vector(4)
        inner = (
            scaled
            - jnp.mean(scaled, axis=-1, keepdims=True)
            - normed * jnp.mean(scaled * normed, axis=-1, keepdims=True)
        ) * inverse
        residual_grad[at, :] = inner
        rounded = inner.astype(BF)
        low_grad[at, :] = rounded
        add_sum(3, upstream * normed, index == 0)
        add_sum(4, upstream, index == 0)
        add_sum(5, rounded.astype(F32), index == 0)
    parts = down.shape[0]
    half_parts = parts // 2
    for quarter in range(4):
        grad = dot_lt(active[quarter], low_grad[...])
        at = pl.ds(quarter * chunk, chunk)
        down_grad[at] = grad.astype(BF).reshape(chunk, -1, D)
        for block in range(quarter * chunk, (quarter + 1) * chunk):
            place = relative_place(block, position[0], parts, relative)

            @pl.when(place < half_parts)
            def _():
                pltpu.make_async_copy(
                    down_grad.at[block], near.at[place], out_sems.at[block]
                ).start()

            @pl.when(place >= half_parts)
            def _():
                pltpu.make_async_copy(
                    down_grad.at[block], far.at[place - half_parts], out_sems.at[block]
                ).start()

    wait_all(slope_copies)
    for block in range(parts):
        pltpu.make_async_copy(down_grad.at[block], near.at[0], out_sems.at[block]).wait()


def feed_forward(position, vectors, tokens, cotangent, groups, weights, up_at, relative):
    rows = tokens.shape[0]
    parts = weights[0].shape[0]
    share = D // parts
    anywhere = pl.BlockSpec(memory_space=pltpu.HBM)
    vmem = pl.BlockSpec(memory_space=pltpu.VMEM)
    return call(
        functools.partial(feed_forward_kernel, len(groups), share, up_at, relative),
        50,
        in_specs=[pl.BlockSpec(memory_space=pltpu.SMEM), vmem] + [anywhere] * (4 + len(groups)),
        out_specs=[vmem, anywhere, anywhere, vmem, anywhere] + [vmem] * 4,
        out_shape=[
            jax.ShapeDtypeStruct((rows, D), BF),
            jax.ShapeDtypeStruct((parts // 2, 4 * share, D), BF),
            jax.ShapeDtypeStruct((parts // 2, 4 * share, D), BF),
            jax.ShapeDtypeStruct((rows, D), BF),
            jax.ShapeDtypeStruct((4, rows, D), BF),
            jax.ShapeDtypeStruct((rows, D), F32),
            jax.ShapeDtypeStruct((rows, LANES), F32),
            jax.ShapeDtypeStruct((rows, D), F32),
            jax.ShapeDtypeStruct((8, D), F32),
        ],
        scratch_shapes=[
            pltpu.VMEM((parts, share, D), BF),
            pltpu.VMEM((4, parts, share, D), BF),
            pltpu.VMEM((parts, 4 * share, D), BF),
            pltpu.VMEM((4, rows, D), BF),
            pltpu.VMEM((4, rows, D), BF),
            pltpu.VMEM((rows, D), F32),
            pltpu.VMEM((rows, D), F32),
            pltpu.VMEM((rows, D), BF),
            pltpu.VMEM((parts, 4 * share, D), BF),
            pltpu.SemaphoreType.DMA((6,)),
            pltpu.SemaphoreType.DMA((parts,)),
            pltpu.SemaphoreType.DMA((4,)),
            pltpu.VMEM((rows, D), BF),
            pltpu.VMEM((rows, D), BF),
            pltpu.VMEM((rows, D), BF),
            pltpu.SemaphoreType.DMA((2 + len(groups),)),
        ],
        name="feed_forward",
        cost_estimate=pl.CostEstimate(
            flops=12_000_000_000, transcendentals=4800000, bytes_accessed=40_000_000
        ),
    )(position, vectors, tokens, cotangent, *groups, *weights)


def feed_back_kernel(
    group_count, share, up_at, vectors, sums_before, hidden_in, normed_in, inverse_in, residual_in, *refs
):
    mixed_groups = refs[:group_count]
    slopes_in, mixing_up, down_shards, grads_out, stream_grad, sums = refs[group_count : group_count + 6]
    refs = refs[group_count + 6 :]
    grad_groups = refs[:group_count]
    (
        mixing, up, down, slopes, hidden_turned, pre_grad, low_grad, back, up_grad, mixing_grad,
        sums_low, in_sems, out_sems, slope_sems, mixed, hidden_low, normed, inverse, residual_grad, row_sems,
    ) = refs[group_count:]
    rows = hidden_low.shape[0]
    block = rows // 3
    row_copies = arrivals(
        [
            (residual_in, residual_grad),
            (hidden_in, hidden_low),
            *side_by_side(mixed_groups, mixed),
            (normed_in, normed),
            (inverse_in, inverse),
        ],
        row_sems,
    )
    for copy in row_copies[:2]:
        copy.start()
    parts = mixing.shape[0]
    chunk = parts // 4
    mixing_copy, up_copies, down_copy = weight_copies(
        share, up_at, mixing_up, down_shards, mixing, up, down, in_sems
    )
    slope_copies = [
        pltpu.make_async_copy(slopes_in.at[quarter], slopes.at[quarter], slope_sems.at[quarter])
        for quarter in range(4)
    ]
    down_copy.start()
    for quarter in range(4):
        slope_copies[quarter].start()
        up_copies[quarter].start()
    mixing_copy.start()
    for copy in row_copies[2:]:
        copy.start()
    add_sum = make_adder(sums)

    def vector(index):
        return vectors[index : index + 1, :]

    sums[7:8, :] = jnp.zeros((1, D), F32)
    wait_all(row_copies[:2])
    low_grad[...] = residual_grad[...].astype(BF)
    hidden_turned[...] = hidden_low[...].T
    down_copy.wait()
    grad_copies = []
    for quarter in range(4):
        slope_copies[quarter].wait()
        up_copies[quarter].wait()
        up_part = up[quarter].reshape(D, D)
        down_part = down[quarter * chunk : (quarter + 1) * chunk].reshape(D, D)
        for index in range(3):
            at = pl.ds(index * block, block)
            part = (dot_rt(low_grad[at, :], down_part) * slopes[quarter, at, :].astype(F32)).astype(BF)
            pre_grad[quarter % 2, at, :] = part
            add_sum(3 + quarter, part.astype(F32), index == 0)
            back_part = dot_rt(part, up_part)
            if quarter == 0:
                back[at, :] = back_part
            else:
                back[at, :] += back_part
        grad = dot(hidden_turned[...], pre_grad[quarter % 2])
        up_grad[quarter] = grad.astype(BF).reshape(parts, share, D)
        grad_copies.append(
            pltpu.make_async_copy(
                up_grad.at[quarter],
                grads_out.at[:, pl.ds((1 + quarter) * share, share)],
                out_sems.at[quarter],
            )
        )
        grad_copies[-1].start()
    mixing_copy.wait()
    wait_all(row_copies[2:])
    for index in range(3):
        at = pl.ds(index * block, block)
        hidden_grad = residual_grad[at, :] + back[at, :]
        norm = normed[at, :]
        scaled = hidden_grad * vector(1)
        inner = (
            scaled
            - jnp.mean(scaled, axis=-1, keepdims=True)
            - norm * jnp.mean(scaled * norm, axis=-1, keepdims=True)
        ) * inverse[at, 0:1]
        stream_grad[at, :] = inner
        rounded = inner.astype(BF)
        low_grad[at, :] = rounded
        add_sum(0, hidden_grad * norm, index == 0)
        add_sum(1, hidden_grad, index == 0)
        add_sum(2, rounded.astype(F32), index == 0)
        mixed_grad = dot_rt(rounded, mixing[...].reshape(D, D)).astype(BF)
        start = 0
        for group in grad_groups:
            width = group.shape[1]
            group[at, :] = mixed_grad[:, start : start + width]
            start += width
    back[...] = dot_lt(mixed[...], low_grad[...])
    mixing_grad[...] = back[...].astype(BF).reshape(parts, share, D)
    grad_copies.append(
        pltpu.make_async_copy(mixing_grad, grads_out.at[:, pl.ds(0, share)], out_sems.at[4])
    )
    grad_copies[-1].start()
    both_sums = jnp.concatenate([sums_before[...], sums[...]], axis=0).astype(BF)
    sums_low[...] = jnp.broadcast_to(both_sums[None], sums_low.shape)
    grad_copies.append(
        pltpu.make_async_copy(sums_low, grads_out.at[:, pl.ds(5 * share, SUM_ROWS)], out_sems.at[5])
    )
    grad_copies[-1].start()
    wait_all(grad_copies)


def feed_back(vectors, sums_before, saved, groups, weights, up_at):
    hidden_low, slopes, normed, inverse, residual_grad = saved
    rows = hidden_low.shape[0]
    parts = weights[0].shape[0]
    share = D // parts
    anywhere = pl.BlockSpec(memory_space=pltpu.HBM)
    vmem = pl.BlockSpec(memory_space=pltpu.VMEM)
    return call(
        functools.partial(feed_back_kernel, len(groups), share, up_at),
        50,
        in_specs=[vmem] * 2 + [anywhere] * (7 + len(groups)),
        out_specs=[anywhere] + [vmem] * (2 + len(groups)),
        out_shape=[
            jax.ShapeDtypeStruct((parts, 5 * share + SUM_ROWS, D), BF),
            jax.ShapeDtypeStruct((rows, D), F32),
            jax.ShapeDtypeStruct((8, D), F32),
        ]
        + [jax.ShapeDtypeStruct(group.shape, BF) for group in groups],
        scratch_shapes=[
            pltpu.VMEM((parts, share, D), BF),
            pltpu.VMEM((4, parts, share, D), BF),
            pltpu.VMEM((parts, 4 * share, D), BF),
            pltpu.VMEM((4, rows, D), BF),
            pltpu.VMEM((D, rows), BF),
            pltpu.VMEM((2, rows, D), BF),
            pltpu.VMEM((rows, D), BF),
            pltpu.VMEM((rows, D), F32),
            pltpu.VMEM((4, parts, share, D), BF),
            pltpu.VMEM((parts, share, D), BF),
            pltpu.VMEM((parts, SUM_ROWS, D), BF),
            pltpu.SemaphoreType.DMA((6,)),
            pltpu.SemaphoreType.DMA((6,)),
            pltpu.SemaphoreType.DMA((4,)),
            pltpu.VMEM((rows, D), BF),
            pltpu.VMEM((rows, D), BF),
            pltpu.VMEM((rows, D), F32),
            pltpu.VMEM((rows, LANES), F32),
            pltpu.VMEM((rows, D), F32),
            pltpu.SemaphoreType.DMA((4 + len(groups),)),
        ],
        name="feed_back",
        cost_estimate=pl.CostEstimate(
            flops=13_000_000_000, transcendentals=0, bytes_accessed=40_000_000
        ),
    )(vectors, sums_before, hidden_low, normed, inverse, residual_grad, *groups, slopes, *weights)


def swap(value, bit, axis="dp"):
    size = lax.axis_size(axis)
    return lax.ppermute(value, axis, [(index, index ^ bit) for index in range(size)])


def relative_offsets(size):
    offsets = [0]
    bit = size // 2
    while bit:
        offsets += [offset ^ bit for offset in offsets]
        bit //= 2
    return offsets


tie = lax.optimization_barrier


def join(*values):
    return jnp.concatenate(values, axis=1)


def summed(terms, at=slice(None)):
    total = terms[0][:, at].astype(F32)
    for term in terms[1:]:
        total = total + term[:, at].astype(F32)
    return total.astype(BF)


def mover(bit, axis="dp"):
    return lambda value: swap(value, bit, axis)


def core_step(near, far):
    return near, [(far, mover(1))]


def half_step(terms, bit):
    half = terms[0].shape[1] // 2
    return summed(terms, slice(0, half)), [(summed(terms, slice(half, None)), mover(bit))]


def quarter_step(terms, high, low):
    quarter = terms[0].shape[1] // 4
    sent = [
        (summed(terms, slice(k * quarter, (k + 1) * quarter)), mover(bit))
        for k, bit in ((2, high), (3, high ^ low), (1, low))
    ]
    return summed(terms, slice(0, quarter)), sent


def last_step(terms, bit):
    size = lax.axis_size("dp")
    mine, theirs = summed(terms, slice(0, 1)), summed(terms, slice(1, 2))
    across = [
        (2 * dp + seq, 2 * (dp ^ bit) + (1 - seq)) for dp in range(size) for seq in range(2)
    ]
    return mine, [
        (theirs, lambda value: lax.ppermute(value, ("dp", "seq"), across)),
        (theirs, mover(bit)),
        (mine, mover(1, "seq")),
    ]


def send(steps, ahead_of):
    ahead_of, values = tie((ahead_of, [[value for value, _ in sent] for _, sent in steps]))
    terms = [
        [kept] + [move(value) for value, (_, move) in zip(row, sent)]
        for row, (kept, sent) in zip(values, steps)
    ]
    return terms, ahead_of


def full_sum(terms):
    total = terms[0].astype(F32)
    for term in terms[1:]:
        total = total + term.astype(F32)
    return total[:, 0]


def local(
    tokens,
    entity_flags,
    query_weight,
    key_weight,
    value_weight,
    mixing_weight,
    mixing_bias,
    first_gain,
    first_bias,
    up_weight,
    up_bias,
    down_weight,
    down_bias,
    second_gain,
    second_bias,
    cotangent,
):
    parts = lax.axis_size("dp")
    me = lax.axis_index("dp")
    share = D // parts
    rows = tokens.shape[0]
    by_swaps = share % 16 == 0 and parts & (parts - 1) == 0 and parts > 8

    six = jnp.concatenate([query_weight, key_weight[None], value_weight[None]], axis=0)
    pairs = jnp.transpose(six.reshape(6, share, PAIRS, LANES), (2, 1, 0, 3)).reshape(PAIRS, share, D)
    up_shard = jnp.transpose(up_weight.reshape(share, 4, D), (1, 0, 2)).reshape(4 * share, D)
    small = (mixing_bias, first_gain, first_bias, down_bias, second_gain, second_bias)
    vector_shard = jnp.concatenate([jnp.stack(small), up_bias.reshape(4, share)], axis=0)

    offsets = relative_offsets(parts) if by_swaps else list(range(parts))
    order = me ^ jnp.array(offsets, jnp.int32) if by_swaps else jnp.array(offsets, jnp.int32)
    column_of = (order[:, None] * share + jnp.arange(share, dtype=jnp.int32)[None, :]).reshape(D)
    choose = (lax.broadcasted_iota(jnp.int32, (D, D), 0) == column_of[None, :]).astype(BF)
    entity = entity_flags.astype(F32)
    tokens_other = swap(tokens, 1, "seq")
    entity_other = swap(entity, 1, "seq")

    shards = []
    start = 0
    for count in FORWARD_GROUPS:
        shards.append(pairs[start : start + count])
        start += count
    count = len(shards)
    vector_rows = 16
    own = dot(tokens, choose).astype(BF)
    if by_swaps:
        where = lax.broadcasted_iota(jnp.int32, (share, D), 0) + me * share
        spread = (lax.broadcasted_iota(jnp.int32, (share, D), 1) == where).astype(BF)
        placed = dot(jnp.stack(small), spread).astype(BF)
        place = me * 4 * share + lax.broadcasted_iota(jnp.int32, (4 * share, D), 0)
        spread = (lax.broadcasted_iota(jnp.int32, (4 * share, D), 1) == place % D).astype(BF)
        quarter_of = me * 4 * share + lax.broadcasted_iota(jnp.int32, (4, 4 * share), 1)
        mine = quarter_of // D == lax.broadcasted_iota(jnp.int32, (4, 4 * share), 0)
        up_placed = dot(jnp.where(mine, up_bias[None, :], 0).astype(BF), spread).astype(BF)
        padded = tie(jnp.concatenate([placed, up_placed, jnp.zeros((6, D), BF)], axis=0))
        middle_shard = jnp.concatenate([mixing_weight, padded, up_shard, down_weight], axis=0)
        up_at, down_at = share + vector_rows, 5 * share + vector_rows
    else:
        groups = []
        for shard in shards:
            full = lax.all_gather(shard, "dp", axis=1, tiled=True)
            groups.append([full.reshape(full.shape[0], 1, D, D)])
        mixing_full, up_full, down_full = (
            lax.all_gather(weight, "dp", axis=0, tiled=True)
            for weight in (mixing_weight, up_weight, down_weight)
        )
        quarter = D // 4
        up_quarters = jnp.transpose(up_full.reshape(4, quarter, 4, D), (0, 2, 1, 3)).reshape(4, D, D)
        mixing_up = jnp.concatenate([mixing_full.reshape(4, quarter, D), up_quarters], axis=1)
        down_shards = down_full.reshape(4, D, D)
        up_at, down_at = quarter, 0
        vectors = lax.all_gather(vector_shard, "dp", axis=0)
        up_vector = vectors[:, 6:].reshape(parts * 4 * share).reshape(4, D)
        vectors = jnp.concatenate(
            [jnp.transpose(vectors[:, :6], (1, 0, 2)).reshape(6, D), up_vector, jnp.zeros((6, D), BF)], axis=0
        ).astype(F32)
    own_entity = jnp.broadcast_to(entity[:, None], (rows, LANES))

    def partner():
        return dot(tokens_other, choose).astype(BF), jnp.broadcast_to(entity_other[:, None], (rows, LANES))

    saved = [None] * count
    if by_swaps:
        side = lax.axis_index("seq")
        groups = [None] * count
        held = [jnp.expand_dims(shard, 1) for shard in shards]
        for g in range(1, count):
            held[g] = lax.dynamic_slice_in_dim(held[g], side * (D // 2), D // 2, 3)
        beside = [None] * count
        bits = [1 << k for k in reversed(range(parts.bit_length() - 1))]
        plans = [[("dp", bit) for bit in bits]] + [
            [("dp", bit) for bit in bits[:-1]] + [("seq", 1), ("dp", 1)] for _ in range(count - 1)
        ]

        def whole_columns(mine, theirs):
            first = side == 0
            return jnp.concatenate([jnp.where(first, mine, theirs), jnp.where(first, theirs, mine)], axis=3)

        other, other_entity = None, None
        for step in range(max(len(plan) + g for g, plan in enumerate(plans))):
            active = [g for g in range(count) if 0 <= step - g < len(plans[g])]
            moved = {}
            for g in active:
                axis, bit = plans[g][step - g]
                both_parts = axis == "seq" or bit == 1
                moved[g] = (swap(held[g], bit, axis),) + ((swap(beside[g], bit, axis),) if both_parts else ())
            done = None
            for g in active:
                if plans[g][step - g] == ("dp", 1):
                    groups[g] = [held[g], beside[g], *moved.pop(g)]
                    if g == 0:
                        other, other_entity = partner()
                        both = (own, other, own_entity, other_entity)
                    saved[g] = attention_forward(*both, groups[g])
                    done = g
            waiting = sorted(moved)
            later = [held[g] for g in range(step + 1, min(step + 2, count))]
            tied = tie((
                tuple(moved[g] for g in waiting), None if done is None else saved[done][0], later, middle_shard
            ))
            if step == MIDDLE_STEP:
                gathered = lax.all_gather(tied[3], "dp", axis=0)
            if done is not None:
                saved[done] = (tied[1], *saved[done][1:])
            for g, value in zip(range(step + 1, min(step + 2, count)), tied[2]):
                held[g] = value
            for g, value in zip(waiting, tied[0]):
                axis, bit = plans[g][step - g]
                if axis == "seq":
                    held[g], beside[g] = whole_columns(held[g], value[0]), whole_columns(beside[g], value[1])
                elif bit == 2:
                    beside[g] = value[0]
                else:
                    held[g] = join(held[g], value[0])
        mixing_up = down_shards = gathered
        vectors = jnp.sum(gathered[:, share : share + vector_rows].astype(F32), axis=0)
    else:
        other, other_entity = partner()
        both = (own, other, own_entity, other_entity)
        saved = [attention_forward(*both, pieces) for pieces in groups]
    middle = (mixing_up, down_shards)
    mixed = [item[0] for item in saved]
    position = (me if by_swaps else jnp.int32(0)).astype(jnp.int32).reshape(1)
    (
        layer_out, down_near, down_far, hidden_low, slopes, normed, inverse, residual_grad, sums_one,
    ) = feed_forward(position, vectors, tokens, cotangent, mixed, middle, (up_at, down_at), by_swaps)

    def over_pieces(value):
        return value.astype(F32) + swap(value, 1, "seq").astype(F32)

    if by_swaps:
        down_bits = halving_bits(parts)[1:]
        pair_bits = [1 << k for k in range(1, parts.bit_length() - 1)]
        (down_state,), _ = send([core_step(down_near[None], down_far[None])], ())
        (down_state,), hidden_low = send([half_step(down_state, down_bits.pop(0))], hidden_low)
    middle_grad, stream_grad, sums_two, *mixed_grads = feed_back(
        vectors, sums_one, (hidden_low, slopes, normed, inverse, residual_grad), mixed, middle,
        (up_at, down_at),
    )

    def up_columns(value):
        return jnp.transpose(value, (1, 0, 2)).reshape(share, 4 * D)

    def vector_outputs(sums):
        sums = sums.astype(F32)

        def shard(row, width=1):
            return lax.dynamic_slice(
                sums[row : row + width].reshape(-1), (me * share * width,), (share * width,)
            )

        token_count = rows * parts * lax.axis_size("seq")
        stream_rms = jnp.sqrt(jnp.sum(sums[0:3], axis=1) / (token_count * D))
        return (shard(10), shard(8), shard(9), shard(11, 4), shard(5), shard(3), shard(4), stream_rms)

    joined, joined_other, near, far = ([None] * count for _ in range(4))
    before = None
    state = {}
    steps = {}

    def group_blocks(index):
        shape = (near[index].shape[0], parts // 2, share, D)
        return near[index].reshape(shape), far[index].reshape(shape)

    def next_step(index):
        steps[index] = steps.get(index, -1) + 1
        return half_step(state[index], pair_bits[steps[index]])

    for index in reversed(range(count)):
        if by_swaps:
            fresh = index + 1 if index + 1 < count else None
            inputs = mixed_grads[index]
            if fresh is not None:
                (started,), (inputs, down_state, state) = send(
                    [core_step(*group_blocks(fresh))], (inputs, down_state, state)
                )
            else:
                inputs, down_state = tie((inputs, down_state))
            order = list(state)
            if down_bits:
                down_step = half_step(down_state, down_bits.pop(0))
            else:
                mine = summed(down_state)
                down_step = (mine, [(mine, mover(1, "seq"))])
            (down_state, *sent), inputs = send([down_step] + [next_step(later) for later in order], inputs)
            state = dict(zip(order, sent))
            if fresh is not None:
                inputs, started = tie((inputs, started))
                state[fresh] = started
                (state[fresh],), inputs = send([next_step(fresh)], inputs)
            mixed_grads[index] = inputs
        near[index], far[index], joined[index], joined_other[index] = attention_backward(
            *both, saved[index], mixed_grads[index], 58 if index == count - 1 else 34
        )
        if index < count - 1:
            done = index + 1
            near[index], joined[done] = tie((near[index], joined[done]))
            before = token_gradient(groups[done], joined[done], joined_other[done], before)
            before, mixed_grads, near[index] = tie((before, mixed_grads, near[index]))
    own_grad, other_grad = token_gradient(groups[0], joined[0], joined_other[0], before)
    other_grad = other_grad.astype(BF)

    if by_swaps:
        middle_sum = lax.psum_scatter(middle_grad, "dp", scatter_dimension=0, tiled=True)[0]
        (started, exchanged), (down_state, state) = send(
            [core_step(*group_blocks(0)), (None, [(other_grad, mover(1, "seq"))])], (down_state, state)
        )
        steps_now = []
        order = list(state)
        for later in order:
            left = pair_bits[steps[later] + 1 :]
            steps_now.append(half_step(state[later], *left) if len(left) == 1 else quarter_step(state[later], *left))
        sent, started = send(steps_now, started)
        down_sum = full_sum(down_state)[0]
        state = dict(zip(order, sent))
        (state[0], across), _ = send(
            [quarter_step(started, *pair_bits[:2]), (None, [(middle_sum, mover(1, "seq"))])], ()
        )
        middle_sum = middle_sum.astype(F32) + across[1].astype(F32)
        mixing_sum = middle_sum[:share]
        up_sum = middle_sum[share : 5 * share].reshape(4, share, D)
        settled = (down_sum, mixing_sum, up_columns(up_sum), vector_outputs(middle_sum[5 * share :]))
        state, settled = tie((state, settled))
        down_sum, mixing_sum, up_out, from_sums = settled
        outer = jnp.concatenate([summed(state[later])[:, 0] for later in range(1, count)], axis=0)
        (state[0], across), exchanged = send(
            [last_step(state[0], pair_bits[-1]), (None, [(outer, mover(1, "seq"))])],
            exchanged,
        )
        tokens_grad = finish_tokens(own_grad, exchanged[1], choose, stream_grad)
        outer = outer.astype(F32) + across[1].astype(F32)
        pair_sum = jnp.concatenate([full_sum(state[0]), outer], axis=0)
    else:
        tokens_grad = finish_tokens(own_grad, swap(other_grad, 1, "seq"), choose, stream_grad)
        sums = lax.psum(jnp.concatenate([sums_one, sums_two], axis=0), ("dp", "seq"))

        def reduced(value, axis):
            piece = lax.psum_scatter(value, "dp", scatter_dimension=axis, tiled=True)
            return lax.psum(piece, "seq").astype(F32)

        down_sum = reduced(jnp.concatenate([down_near, down_far], axis=0).reshape(-1, D), 0)
        mixing_sum = reduced(middle_grad[:, :quarter].reshape(D, D), 0)
        up_quarters = middle_grad[:, quarter : 5 * quarter].reshape(4, 4, quarter, D)
        up_sum = reduced(jnp.transpose(up_quarters, (1, 0, 2, 3)).reshape(4, D, D), 1)
        up_out, from_sums = up_columns(up_sum), vector_outputs(sums)
        pair_sum = jnp.concatenate(
            [reduced(jnp.concatenate([a, b], axis=1), 1) for a, b in zip(near, far)], axis=0
        )

    six_sum = jnp.transpose(pair_sum.reshape(PAIRS, share, 6, LANES), (2, 1, 0, 3)).reshape(6, share, D)
    mixing_bias_sum, gain_one, bias_one, up_bias_sum, down_bias_sum, gain_two, bias_two, stream_rms = from_sums
    return (
        layer_out,
        tokens_grad,
        six_sum[0:4],
        six_sum[4],
        six_sum[5],
        mixing_sum,
        mixing_bias_sum,
        gain_one,
        bias_one,
        up_out,
        up_bias_sum,
        down_sum,
        down_bias_sum,
        gain_two,
        bias_two,
        stream_rms,
    )


def solution(mesh):
    rows = P(("dp", "seq"), None)
    vector = P("dp")
    matrix = P("dp", None)
    stacked = P(None, "dp", None)
    in_specs = (
        rows, P(("dp", "seq")), stacked, matrix, matrix, matrix, vector, vector, vector, matrix,
        vector, matrix, vector, vector, vector, rows,
    )
    out_specs = (
        rows, rows, stacked, matrix, matrix, matrix, vector, vector, vector, matrix, vector,
        matrix, vector, vector, vector, P(),
    )
    return jax.shard_map(local, mesh=mesh, in_specs=in_specs, out_specs=out_specs, check_vma=False)
```

```python
import functools

import jax
import jax.numpy as jnp
from jax import lax
from jax.experimental import pallas as pl
from jax.experimental.pallas import tpu as pltpu
from jax.sharding import PartitionSpec as P

D = 768
HEADS = 12
HD = 64
PAIRS = HEADS // 2
LANES = 2 * HD
F32 = jnp.float32
BF = jnp.bfloat16
EPSILON = 1e-05
LN2 = 0.6931471805599453
QUERY_SCALE = HD**-0.5 / LN2
FORWARD_GROUPS = (1, 2, 3)
SUM_ROWS = 16
MIDDLE_STEP = 0
MIB = 1024 * 1024


def dot(left, right):
    return jnp.dot(left, right, preferred_element_type=F32)


def dot_rt(left, right):
    return lax.dot_general(left, right, (((1,), (1,)), ((), ())), preferred_element_type=F32)


def dot_lt(left, right):
    return lax.dot_general(left, right, (((0,), (0,)), ((), ())), preferred_element_type=F32)


def call(kernel, mebibytes, **kwargs):
    return pl.pallas_call(
        kernel, compiler_params=pltpu.CompilerParams(vmem_limit_bytes=mebibytes * MIB), **kwargs
    )


def in_hbm(*arrays):
    return [pltpu.with_memory_space_constraint(array, pltpu.HBM) for array in arrays]


def whole_block(shape):
    return pl.BlockSpec(shape, lambda step: (0,) * len(shape))


def pair_block(shape):
    return pl.BlockSpec((1,) + shape, lambda step: (step,) + (0,) * len(shape))


def attention_forward_kernel(piece_count, own, other, own_entity, other_entity, *refs):
    pieces = refs[:piece_count]
    mixed, queries, keys, values, weights, totals, key_masked, value_ones, packed = refs[piece_count:]
    rows = own.shape[0]
    block = rows // 2
    lane = lax.broadcasted_iota(jnp.int32, (rows, LANES), 1)
    low = lane < HD
    at = 0
    for piece in pieces:
        part = piece[0].reshape(-1, D)
        packed[at : at + part.shape[0], :] = part
        at += part.shape[0]
    is_own = own_entity[...]
    is_other = other_entity[...]
    projected = dot(own[...], packed[...])
    entity_row = is_own > 0.5
    to_word = jnp.where(entity_row, projected[:, 256:384], projected[:, 0:128]) * QUERY_SCALE
    to_entity = jnp.where(entity_row, projected[:, 384:512], projected[:, 128:256]) * QUERY_SCALE
    queries[0, :, 0:LANES] = jnp.where(low, to_word, pltpu.roll(to_entity, HD, 1)).astype(BF)
    queries[0, :, LANES:] = jnp.where(low, pltpu.roll(to_word, HD, 1), to_entity).astype(BF)
    projected_other = dot(other[...], packed[:, 512:768])
    halves = (
        (projected[:, 512:640], projected[:, 640:768], is_own),
        (projected_other[:, 0:128], projected_other[:, 128:256], is_other),
    )
    for half, (key, value, entity) in enumerate(halves):
        at = pl.ds(half * rows, rows)
        keys[0, at, :] = key.astype(BF)
        values[0, at, :] = value.astype(BF)
        mask = jnp.where(low, 1.0 - entity, entity)
        turned = pltpu.roll(key, HD, 1)
        key_masked[at, 0:LANES] = (jnp.where(low, key, turned) * mask).astype(BF)
        key_masked[at, LANES:] = (jnp.where(low, turned, key) * mask).astype(BF)
        ones = jnp.ones_like(value)
        value_ones[at, 0:LANES] = jnp.where(low, value, ones).astype(BF)
        value_ones[at, LANES:] = jnp.where(low, ones, value).astype(BF)
    items = [(index, head) for index in range(rows // block) for head in range(2)]

    def scores_of(item):
        index, head = item
        columns = pl.ds(head * LANES, LANES)
        return dot_rt(queries[0, pl.ds(index * block, block), columns], key_masked[:, columns])

    ahead = scores_of(items[0])
    sums = []
    for number, (index, head) in enumerate(items):
        scores = ahead
        if number + 1 < len(items):
            ahead = scores_of(items[number + 1])
        at = pl.ds(index * block, block)
        highest = jnp.max(scores, axis=-1, keepdims=True)
        weight = jnp.exp2(scores - highest).astype(BF)
        weights[0, head, at, :] = weight
        sums.append(dot(weight, value_ones[:, pl.ds(head * LANES, LANES)]))
        if head:
            upper = jnp.where(low[:block], sums[0], sums[1])
            total = pltpu.roll(jnp.where(low[:block], sums[1], sums[0]), HD, 1)
            mixed[at, :] = (upper / total).astype(BF)
            totals[0, at, :] = total
            sums = []


def piece_blocks(pieces):
    return [pair_block(piece.shape[1:]) for piece in pieces]


def attention_forward(own, other, own_entity, other_entity, pieces):
    count = pieces[0].shape[0]
    rows = own.shape[0]
    length = 2 * rows
    return call(
        functools.partial(attention_forward_kernel, len(pieces)),
        30,
        grid=(count,),
        in_specs=[whole_block((rows, D))] * 2 + [whole_block((rows, LANES))] * 2 + piece_blocks(pieces),
        out_specs=[
            pl.BlockSpec((rows, LANES), lambda step: (0, step)),
            pair_block((rows, 2 * LANES)),
            pair_block((length, LANES)),
            pair_block((length, LANES)),
            pair_block((2, rows, length)),
            pair_block((rows, LANES)),
        ],
        out_shape=[
            pltpu.HBM((rows, LANES * count), BF),
            pltpu.HBM((count, rows, 2 * LANES), BF),
            pltpu.HBM((count, length, LANES), BF),
            pltpu.HBM((count, length, LANES), BF),
            pltpu.HBM((count, 2, rows, length), BF),
            pltpu.HBM((count, rows, LANES), F32),
        ],
        scratch_shapes=[
            pltpu.VMEM((length, 2 * LANES), BF),
            pltpu.VMEM((length, 2 * LANES), BF),
            pltpu.VMEM((D, D), BF),
        ],
        name="attention_forward",
        cost_estimate=pl.CostEstimate(
            flops=count * 7_000_000_000, transcendentals=count * 2400000, bytes_accessed=count * 8_000_000
        ),
    )(own, other, own_entity, other_entity, *pieces)


def attention_backward_kernel(own, other, own_entity, other_entity, *refs):
    queries, keys, values, weights, totals, mixed, grad = refs[:7]
    near, far, joined, joined_other = refs[7:11]
    key_masked, value_ones, grad_wide, query_grad, key_grad, value_grad = refs[11:]
    rows = own.shape[0]
    block = rows // 3
    lane = lax.broadcasted_iota(jnp.int32, (rows, LANES), 1)
    low = lane < HD
    is_own = own_entity[...]
    is_other = other_entity[...]
    for half, entity in enumerate((is_own, is_other)):
        at = pl.ds(half * rows, rows)
        key = keys[0, at, :].astype(F32)
        turned = pltpu.roll(key, HD, 1)
        mask = jnp.where(low, 1.0 - entity, entity)
        key_masked[at, 0:LANES] = (jnp.where(low, key, turned) * mask).astype(BF)
        key_masked[at, LANES:] = (jnp.where(low, turned, key) * mask).astype(BF)
        value = values[0, at, :].astype(F32)
        ones = jnp.where(lane % HD < 2, 1.0, 0.0)
        value_ones[at, 0:LANES] = jnp.where(low, value, ones).astype(BF)
        value_ones[at, LANES:] = jnp.where(low, ones, value).astype(BF)
    scaled = grad[...].astype(F32) / totals[0]
    inner = scaled * mixed[...].astype(F32)

    def correction(inner_sum):
        upper = inner_sum.astype(BF).astype(F32)
        return jnp.where(
            lane % HD == 0, -upper, jnp.where(lane % HD == 1, upper - inner_sum, 0.0)
        )

    first_inner = jnp.sum(jnp.where(low, inner, 0.0), axis=-1, keepdims=True)
    second_inner = jnp.sum(jnp.where(low, 0.0, inner), axis=-1, keepdims=True)
    grad_wide[:, 0:LANES] = jnp.where(low, scaled, correction(first_inner)).astype(BF)
    grad_wide[:, LANES:] = jnp.where(low, correction(second_inner), scaled).astype(BF)
    for head in range(2):
        columns = pl.ds(head * LANES, LANES)
        for index in range(rows // block):
            at = pl.ds(index * block, block)
            grad_block = grad_wide[at, columns]
            weight = weights[0, head, at, :]
            score_grad = (weight.astype(F32) * dot_rt(grad_block, value_ones[:, columns])).astype(BF)
            query_grad[at, columns] = dot(score_grad, key_masked[:, columns]) * HD**-0.5
            query_turned = queries[0, at, columns].astype(F32).T.astype(BF)
            grad_turned = grad_block.astype(F32).T[head * HD : (head + 1) * HD].astype(BF)
            key_part = dot(query_turned, score_grad)
            value_part = dot(grad_turned, weight)
            key_at = pl.ds(head * LANES, LANES)
            value_at = pl.ds(head * HD, HD)
            if index == 0:
                key_grad[key_at, :] = key_part
                value_grad[value_at, :] = value_part
            else:
                key_grad[key_at, :] += key_part
                value_grad[value_at, :] += value_part
    query_a = query_grad[:, 0:LANES]
    query_b = query_grad[:, LANES:]
    word_grad = jnp.where(low, query_a, pltpu.roll(query_b, HD, 1))
    entity_grad = jnp.where(low, pltpu.roll(query_a, HD, 1), query_b)
    is_word = 1.0 - is_own
    joined[0, :, 0:128] = (is_word * word_grad).astype(BF)
    joined[0, :, 128:256] = (is_word * entity_grad).astype(BF)
    joined[0, :, 256:384] = (is_own * word_grad).astype(BF)
    joined[0, :, 384:512] = (is_own * entity_grad).astype(BF)
    key_back = key_grad[...].T
    value_back = value_grad[...].T
    for half, entity in enumerate((is_own, is_other)):
        at = slice(half * rows, half * rows + rows)
        key_a = key_back[at, 0:LANES]
        key_b = key_back[at, LANES:]
        key_word = jnp.where(low, key_a, pltpu.roll(key_b, HD, 1))
        key_entity = jnp.where(low, pltpu.roll(key_a, HD, 1), key_b)
        key_part = (jnp.where(entity > 0.5, key_entity, key_word) * LN2).astype(BF)
        value_part = value_back[at].astype(BF)
        if half == 0:
            joined[0, :, 512:640] = key_part
            joined[0, :, 640:768] = value_part
        else:
            joined_other[0, :, 0:128] = key_part
            joined_other[0, :, 128:256] = value_part
    here = dot_lt(own[...], joined[0])
    there = dot_lt(other[...], joined_other[0])
    for target, at in ((near, slice(0, D // 2)), (far, slice(D // 2, D))):
        blocks = (target.shape[0], target.shape[2])
        target[:, 0, :, 0:512] = here[at, 0:512].astype(BF).reshape(*blocks, 512)
        target[:, 0, :, 512:768] = (here[at, 512:768] + there[at]).astype(BF).reshape(*blocks, 256)


def attention_backward(own, other, own_entity, other_entity, saved, grad, mebibytes, blocks):
    mixed, queries, keys, values, weights, totals = saved
    count = queries.shape[0]
    rows = own.shape[0]
    length = 2 * rows
    column = pl.BlockSpec((rows, LANES), lambda step: (0, step))
    return call(
        attention_backward_kernel,
        mebibytes,
        grid=(count,),
        in_specs=[whole_block((rows, D))] * 2
        + [whole_block((rows, LANES))] * 2
        + [
            pair_block((rows, 2 * LANES)),
            pair_block((length, LANES)),
            pair_block((length, LANES)),
            pair_block((2, rows, length)),
            pair_block((rows, LANES)),
            column,
            column,
        ],
        out_specs=[pl.BlockSpec((blocks, 1, D // 2 // blocks, D), lambda step: (0, step, 0, 0))] * 2
        + [pair_block((rows, D)), pair_block((rows, 2 * LANES))],
        out_shape=[jax.ShapeDtypeStruct((blocks, count, D // 2 // blocks, D), BF)] * 2
        + [
            jax.ShapeDtypeStruct((count, rows, D), BF),
            jax.ShapeDtypeStruct((count, rows, 2 * LANES), BF),
        ],
        scratch_shapes=[
            pltpu.VMEM((length, 2 * LANES), BF),
            pltpu.VMEM((length, 2 * LANES), BF),
            pltpu.VMEM((rows, 2 * LANES), BF),
            pltpu.VMEM((rows, 2 * LANES), F32),
            pltpu.VMEM((2 * LANES, length), F32),
            pltpu.VMEM((LANES, length), F32),
        ],
        name="attention_backward",
        cost_estimate=pl.CostEstimate(
            flops=count * 10_000_000_000, transcendentals=0, bytes_accessed=count * 12_000_000
        ),
    )(own, other, own_entity, other_entity, queries, keys, values, weights, totals, mixed, grad)


def token_gradient_kernel(piece_count, first, *refs):
    pieces = refs[:piece_count]
    refs = refs[piece_count:]
    joined, joined_other = refs[:2]
    refs = refs[2:]
    before = ()
    if not first:
        before, refs = refs[:2], refs[2:]
    *totals, packed = refs
    at = 0
    for piece in pieces:
        part = piece[0].reshape(-1, D)
        packed[at : at + part.shape[0], :] = part
        at += part.shape[0]
    step = pl.program_id(0)
    parts = (dot_rt(joined[0], packed[...]), dot_rt(joined_other[0], packed[:, 512:768]))
    for index, (total, part) in enumerate(zip(totals, parts)):

        @pl.when(step == 0)
        def _():
            total[...] = (part if first else before[index][...] + part).astype(total.dtype)

        @pl.when(step > 0)
        def _():
            total[...] = (total[...] + part).astype(total.dtype)


def token_gradient(pieces, joined, joined_other, before, other_type=F32):
    count, rows, _ = joined.shape
    first = before is None
    return call(
        functools.partial(token_gradient_kernel, len(pieces), first),
        16,
        grid=(count,),
        in_specs=piece_blocks(pieces)
        + [pair_block((rows, D)), pair_block((rows, 2 * LANES))]
        + [whole_block((rows, D))] * (0 if first else 2),
        out_specs=[whole_block((rows, D))] * 2,
        out_shape=[jax.ShapeDtypeStruct((rows, D), F32), jax.ShapeDtypeStruct((rows, D), other_type)],
        scratch_shapes=[pltpu.VMEM((D, D), BF)],
        name="token_gradient",
        cost_estimate=pl.CostEstimate(
            flops=count * 1_200_000_000, transcendentals=0, bytes_accessed=count * 4_000_000
        ),
    )(*pieces, joined, joined_other, *(before or ()))


def finish_kernel(own, received, choose, stream_grad, out):
    value = own[...] + received[...].astype(F32)
    upper = value.astype(BF)
    lower = (value - upper.astype(F32)).astype(BF)
    out[...] = (stream_grad[...] + dot_rt(upper, choose[...]) + dot_rt(lower, choose[...])).astype(BF)


def finish_tokens(own, received, choose, stream_grad):
    return call(
        finish_kernel,
        16,
        in_specs=[pl.BlockSpec(memory_space=pltpu.VMEM)] * 4,
        out_specs=pl.BlockSpec(memory_space=pltpu.VMEM),
        out_shape=jax.ShapeDtypeStruct(own.shape, BF),
        name="finish_tokens",
        cost_estimate=pl.CostEstimate(flops=2_000_000_000, transcendentals=0, bytes_accessed=8_000_000),
    )(own, received, choose, stream_grad)


def error_function(value):
    value = jnp.clip(value, -3.7439211627767994, 3.7439211627767994)
    square = value * value
    upper = jnp.float32(0.00022905065861350646)
    for term in (
        0.0034082910107109506, 0.050955695062380861, 0.18520832239976145, 1.128379143519084,
    ):
        upper = upper * square + term
    lower = jnp.float32(-1.1791602954361697e-7)
    for term in (
        0.000023547966471313185, 0.0010179625278914885, 0.014070470171167667,
        0.11098505178285362, 0.49746925110067538, 1.0,
    ):
        lower = lower * square + term
    return value * upper / lower


def wait_all(copies):
    for copy in copies:
        copy.wait()


def weight_copies(share, starts, mixing_up, down_shards, mixing, up, down, sems):
    return (
        pltpu.make_async_copy(mixing_up.at[:, pl.ds(0, share)], mixing, sems.at[0]),
        [
            pltpu.make_async_copy(
                mixing_up.at[:, pl.ds(starts[0] + quarter * share, share)], up.at[quarter], sems.at[1 + quarter]
            )
            for quarter in range(4)
        ],
        pltpu.make_async_copy(down_shards.at[:, pl.ds(starts[1], 4 * share)], down, sems.at[5]),
    )


def arrivals(pairs, sems):
    return [
        pltpu.make_async_copy(source, target, sems.at[index]) for index, (source, target) in enumerate(pairs)
    ]


def side_by_side(groups, target):
    pairs = []
    start = 0
    for group in groups:
        width = group.shape[1]
        pairs.append((group, target.at[:, pl.ds(start, width)]))
        start += width
    return pairs


def make_adder(sums):
    def add_sum(index, value, start):
        part = jnp.sum(value, axis=0, keepdims=True)
        if start:
            sums[index : index + 1, :] = part
        else:
            sums[index : index + 1, :] += part

    return add_sum


def halving_bits(parts):
    return [1 << k for k in range(parts.bit_length() - 1)]


def relative_place(block, me, parts, relative):
    if not relative:
        return jnp.int32(block)
    offset = me ^ block
    place = 0
    for bit in halving_bits(parts):
        place = 2 * place + jnp.where(offset & bit, 1, 0)
    return place


def feed_forward_kernel(group_count, share, up_at, relative, position, vectors, tokens_in, cotangent_in, *refs):
    mixed_groups = refs[:group_count]
    (
        mixing_up, down_shards, layer_to, near, far, hidden_to, slopes_out, normed_to, inverse_to,
        residual_to, sums, mixing, up, down, active, slopes, total, hidden, low_grad, down_grad,
        in_sems, out_sems, slope_sems, mixed, tokens, cotangent, row_sems, layer_out, hidden_low,
        normed_out, inverse_out, residual_grad, leave_sems,
    ) = refs[group_count:]
    leaving = arrivals(
        [
            (hidden_low, hidden_to),
            (normed_out, normed_to),
            (inverse_out, inverse_to),
            (layer_out, layer_to),
            (residual_grad, residual_to),
        ],
        leave_sems,
    )
    rows = tokens.shape[0]
    block = rows // 3
    row_copies = arrivals(
        [*side_by_side(mixed_groups, mixed), (tokens_in, tokens), (cotangent_in, cotangent)], row_sems
    )
    chunk = down.shape[0] // 4
    mixing_copy, up_copies, down_copy = weight_copies(
        share, up_at, mixing_up, down_shards, mixing, up, down, in_sems
    )
    mixing_copy.start()
    for copy in row_copies:
        copy.start()
    for copy in up_copies:
        copy.start()
    down_copy.start()
    add_sum = make_adder(sums)

    def vector(index):
        return vectors[index : index + 1, :]

    sums[6:8, :] = jnp.zeros((2, D), F32)
    mixing_copy.wait()
    wait_all(row_copies[:-1])
    for index in range(3):
        at = pl.ds(index * block, block)
        attended = dot(mixed[at, :], mixing[...].reshape(D, D)) + vector(0)
        stream = tokens[at, :].astype(F32) + attended
        add_sum(0, stream * stream, index == 0)
        add_sum(1, attended * attended, index == 0)
        center = stream - jnp.mean(stream, axis=-1, keepdims=True)
        inverse = lax.rsqrt(jnp.mean(center * center, axis=-1, keepdims=True) + EPSILON)
        normed = center * inverse
        normed_out[at, :] = normed
        inverse_out[at, :] = jnp.broadcast_to(inverse, (block, LANES))
        value = normed * vector(1) + vector(2)
        hidden[at, :] = value
        hidden_low[at, :] = value.astype(BF)
    for copy in leaving[:3]:
        copy.start()
    down_copy.wait()
    slope_copies = []
    for quarter in range(4):
        up_copies[quarter].wait()
        up_part = up[quarter].reshape(D, D)
        down_part = down[quarter * chunk : (quarter + 1) * chunk].reshape(D, D)
        for index in range(3):
            at = pl.ds(index * block, block)
            before = dot(hidden_low[at, :], up_part) + vector(6 + quarter)
            half = 0.5 * (1.0 + error_function(before * 0.7071067811865476))
            act = (before * half).astype(BF)
            active[quarter, at, :] = act
            slope = half + before * jnp.exp(-0.5 * before * before) * 0.3989422804014327
            slopes[quarter, at, :] = slope.astype(BF)
            part = dot(act, down_part)
            if quarter == 0:
                total[at, :] = part
            else:
                total[at, :] += part
        slope_copies.append(
            pltpu.make_async_copy(slopes.at[quarter], slopes_out.at[quarter], slope_sems.at[quarter])
        )
        slope_copies[-1].start()
    row_copies[-1].wait()
    for index in range(3):
        at = pl.ds(index * block, block)
        forward_out = total[at, :] + vector(3)
        add_sum(2, forward_out * forward_out, index == 0)
        value = hidden[at, :] + forward_out
        center = value - jnp.mean(value, axis=-1, keepdims=True)
        inverse = lax.rsqrt(jnp.mean(center * center, axis=-1, keepdims=True) + EPSILON)
        normed = center * inverse
        layer_out[at, :] = (normed * vector(4) + vector(5)).astype(BF)
        upstream = cotangent[at, :].astype(F32)
        scaled = upstream * vector(4)
        inner = (
            scaled
            - jnp.mean(scaled, axis=-1, keepdims=True)
            - normed * jnp.mean(scaled * normed, axis=-1, keepdims=True)
        ) * inverse
        residual_grad[at, :] = inner
        rounded = inner.astype(BF)
        low_grad[at, :] = rounded
        add_sum(3, upstream * normed, index == 0)
        add_sum(4, upstream, index == 0)
        add_sum(5, rounded.astype(F32), index == 0)
    for copy in leaving[3:]:
        copy.start()
    parts = down.shape[0]
    half_parts = parts // 2
    for quarter in range(4):
        grad = dot_lt(active[quarter], low_grad[...])
        at = pl.ds(quarter * chunk, chunk)
        down_grad[at] = grad.astype(BF).reshape(chunk, -1, D)
        for block in range(quarter * chunk, (quarter + 1) * chunk):
            place = relative_place(block, position[0], parts, relative)

            @pl.when(place < half_parts)
            def _():
                pltpu.make_async_copy(
                    down_grad.at[block], near.at[place], out_sems.at[block]
                ).start()

            @pl.when(place >= half_parts)
            def _():
                pltpu.make_async_copy(
                    down_grad.at[block], far.at[place - half_parts], out_sems.at[block]
                ).start()

    wait_all(slope_copies)
    wait_all(leaving)
    for block in range(parts):
        pltpu.make_async_copy(down_grad.at[block], near.at[0], out_sems.at[block]).wait()


def feed_forward(position, vectors, tokens, cotangent, groups, weights, up_at, relative):
    rows = tokens.shape[0]
    parts = weights[0].shape[0]
    share = D // parts
    anywhere = pl.BlockSpec(memory_space=pltpu.HBM)
    vmem = pl.BlockSpec(memory_space=pltpu.VMEM)
    return call(
        functools.partial(feed_forward_kernel, len(groups), share, up_at, relative),
        50,
        in_specs=[pl.BlockSpec(memory_space=pltpu.SMEM), vmem] + [anywhere] * (4 + len(groups)),
        out_specs=[anywhere] * 8 + [vmem],
        out_shape=[
            jax.ShapeDtypeStruct((rows, D), BF),
            jax.ShapeDtypeStruct((parts // 2, 4 * share, D), BF),
            jax.ShapeDtypeStruct((parts // 2, 4 * share, D), BF),
            jax.ShapeDtypeStruct((rows, D), BF),
            jax.ShapeDtypeStruct((4, rows, D), BF),
            jax.ShapeDtypeStruct((rows, D), F32),
            jax.ShapeDtypeStruct((rows, LANES), F32),
            jax.ShapeDtypeStruct((rows, D), F32),
            jax.ShapeDtypeStruct((8, D), F32),
        ],
        scratch_shapes=[
            pltpu.VMEM((parts, share, D), BF),
            pltpu.VMEM((4, parts, share, D), BF),
            pltpu.VMEM((parts, 4 * share, D), BF),
            pltpu.VMEM((4, rows, D), BF),
            pltpu.VMEM((4, rows, D), BF),
            pltpu.VMEM((rows, D), F32),
            pltpu.VMEM((rows, D), F32),
            pltpu.VMEM((rows, D), BF),
            pltpu.VMEM((parts, 4 * share, D), BF),
            pltpu.SemaphoreType.DMA((6,)),
            pltpu.SemaphoreType.DMA((parts,)),
            pltpu.SemaphoreType.DMA((4,)),
            pltpu.VMEM((rows, D), BF),
            pltpu.VMEM((rows, D), BF),
            pltpu.VMEM((rows, D), BF),
            pltpu.SemaphoreType.DMA((2 + len(groups),)),
            pltpu.VMEM((rows, D), BF),
            pltpu.VMEM((rows, D), BF),
            pltpu.VMEM((rows, D), F32),
            pltpu.VMEM((rows, LANES), F32),
            pltpu.VMEM((rows, D), F32),
            pltpu.SemaphoreType.DMA((5,)),
        ],
        name="feed_forward",
        cost_estimate=pl.CostEstimate(
            flops=12_000_000_000, transcendentals=4800000, bytes_accessed=40_000_000
        ),
    )(position, vectors, *in_hbm(tokens, cotangent, *groups, *weights))


def feed_back_kernel(
    group_count, share, up_at, vectors, sums_before, hidden_in, normed_in, inverse_in, residual_in, *refs
):
    mixed_groups = refs[:group_count]
    slopes_in, mixing_up, down_shards, grads_out, stream_grad, sums = refs[group_count : group_count + 6]
    refs = refs[group_count + 6 :]
    grad_groups = refs[:group_count]
    (
        mixing, up, down, slopes, hidden_turned, pre_grad, low_grad, back, up_grad, mixing_grad,
        sums_low, in_sems, out_sems, slope_sems, mixed, hidden_low, normed, inverse, residual_grad, row_sems,
    ) = refs[group_count:]
    rows = hidden_low.shape[0]
    block = rows // 3
    row_copies = arrivals(
        [
            (residual_in, residual_grad),
            (hidden_in, hidden_low),
            *side_by_side(mixed_groups, mixed),
            (normed_in, normed),
            (inverse_in, inverse),
        ],
        row_sems,
    )
    for copy in row_copies[:2]:
        copy.start()
    parts = mixing.shape[0]
    chunk = parts // 4
    mixing_copy, up_copies, down_copy = weight_copies(
        share, up_at, mixing_up, down_shards, mixing, up, down, in_sems
    )
    slope_copies = [
        pltpu.make_async_copy(slopes_in.at[quarter], slopes.at[quarter], slope_sems.at[quarter])
        for quarter in range(4)
    ]
    down_copy.start()
    for quarter in range(4):
        slope_copies[quarter].start()
        up_copies[quarter].start()
    mixing_copy.start()
    for copy in row_copies[2:]:
        copy.start()
    add_sum = make_adder(sums)

    def vector(index):
        return vectors[index : index + 1, :]

    sums[7:8, :] = jnp.zeros((1, D), F32)
    wait_all(row_copies[:2])
    low_grad[...] = residual_grad[...].astype(BF)
    hidden_turned[...] = hidden_low[...].T
    down_copy.wait()
    grad_copies = []
    for quarter in range(4):
        slope_copies[quarter].wait()
        up_copies[quarter].wait()
        up_part = up[quarter].reshape(D, D)
        down_part = down[quarter * chunk : (quarter + 1) * chunk].reshape(D, D)
        for index in range(3):
            at = pl.ds(index * block, block)
            part = (dot_rt(low_grad[at, :], down_part) * slopes[quarter, at, :].astype(F32)).astype(BF)
            pre_grad[quarter % 2, at, :] = part
            add_sum(3 + quarter, part.astype(F32), index == 0)
            back_part = dot_rt(part, up_part)
            if quarter == 0:
                back[at, :] = back_part
            else:
                back[at, :] += back_part
        grad = dot(hidden_turned[...], pre_grad[quarter % 2])
        up_grad[quarter] = grad.astype(BF).reshape(parts, share, D)
        grad_copies.append(
            pltpu.make_async_copy(
                up_grad.at[quarter],
                grads_out.at[:, pl.ds((1 + quarter) * share, share)],
                out_sems.at[quarter],
            )
        )
        grad_copies[-1].start()
    mixing_copy.wait()
    wait_all(row_copies[2:])
    for index in range(3):
        at = pl.ds(index * block, block)
        hidden_grad = residual_grad[at, :] + back[at, :]
        norm = normed[at, :]
        scaled = hidden_grad * vector(1)
        inner = (
            scaled
            - jnp.mean(scaled, axis=-1, keepdims=True)
            - norm * jnp.mean(scaled * norm, axis=-1, keepdims=True)
        ) * inverse[at, 0:1]
        stream_grad[at, :] = inner
        rounded = inner.astype(BF)
        low_grad[at, :] = rounded
        add_sum(0, hidden_grad * norm, index == 0)
        add_sum(1, hidden_grad, index == 0)
        add_sum(2, rounded.astype(F32), index == 0)
        mixed_grad = dot_rt(rounded, mixing[...].reshape(D, D)).astype(BF)
        start = 0
        for group in grad_groups:
            width = group.shape[1]
            group[at, :] = mixed_grad[:, start : start + width]
            start += width
    back[...] = dot_lt(mixed[...], low_grad[...])
    mixing_grad[...] = back[...].astype(BF).reshape(parts, share, D)
    grad_copies.append(
        pltpu.make_async_copy(mixing_grad, grads_out.at[:, pl.ds(0, share)], out_sems.at[4])
    )
    grad_copies[-1].start()
    both_sums = jnp.concatenate([sums_before[...], sums[...]], axis=0).astype(BF)
    sums_low[...] = jnp.broadcast_to(both_sums[None], sums_low.shape)
    grad_copies.append(
        pltpu.make_async_copy(sums_low, grads_out.at[:, pl.ds(5 * share, SUM_ROWS)], out_sems.at[5])
    )
    grad_copies[-1].start()
    wait_all(grad_copies)


def feed_back(vectors, sums_before, saved, groups, weights, up_at):
    hidden_low, slopes, normed, inverse, residual_grad = saved
    rows = hidden_low.shape[0]
    parts = weights[0].shape[0]
    share = D // parts
    anywhere = pl.BlockSpec(memory_space=pltpu.HBM)
    vmem = pl.BlockSpec(memory_space=pltpu.VMEM)
    return call(
        functools.partial(feed_back_kernel, len(groups), share, up_at),
        50,
        in_specs=[vmem] * 2 + [anywhere] * (7 + len(groups)),
        out_specs=[anywhere] + [vmem] * (2 + len(groups)),
        out_shape=[
            jax.ShapeDtypeStruct((parts, 5 * share + SUM_ROWS, D), BF),
            jax.ShapeDtypeStruct((rows, D), F32),
            jax.ShapeDtypeStruct((8, D), F32),
        ]
        + [jax.ShapeDtypeStruct(group.shape, BF) for group in groups],
        scratch_shapes=[
            pltpu.VMEM((parts, share, D), BF),
            pltpu.VMEM((4, parts, share, D), BF),
            pltpu.VMEM((parts, 4 * share, D), BF),
            pltpu.VMEM((4, rows, D), BF),
            pltpu.VMEM((D, rows), BF),
            pltpu.VMEM((2, rows, D), BF),
            pltpu.VMEM((rows, D), BF),
            pltpu.VMEM((rows, D), F32),
            pltpu.VMEM((4, parts, share, D), BF),
            pltpu.VMEM((parts, share, D), BF),
            pltpu.VMEM((parts, SUM_ROWS, D), BF),
            pltpu.SemaphoreType.DMA((6,)),
            pltpu.SemaphoreType.DMA((6,)),
            pltpu.SemaphoreType.DMA((4,)),
            pltpu.VMEM((rows, D), BF),
            pltpu.VMEM((rows, D), BF),
            pltpu.VMEM((rows, D), F32),
            pltpu.VMEM((rows, LANES), F32),
            pltpu.VMEM((rows, D), F32),
            pltpu.SemaphoreType.DMA((4 + len(groups),)),
        ],
        name="feed_back",
        cost_estimate=pl.CostEstimate(
            flops=13_000_000_000, transcendentals=0, bytes_accessed=40_000_000
        ),
    )(vectors, sums_before, *in_hbm(hidden_low, normed, inverse, residual_grad, *groups, slopes, *weights))


def swap(value, bit, axis="dp"):
    size = lax.axis_size(axis)
    return lax.ppermute(value, axis, [(index, index ^ bit) for index in range(size)])


def relative_offsets(size):
    offsets = [0]
    bit = size // 2
    while bit:
        offsets += [offset ^ bit for offset in offsets]
        bit //= 2
    return offsets


tie = lax.optimization_barrier


def join(*values):
    return jnp.concatenate(values, axis=1)


def summed(terms, at=slice(None)):
    total = terms[0][at].astype(F32)
    for term in terms[1:]:
        total = total + term[at].astype(F32)
    return total.astype(BF)


def mover(bit, axis="dp"):
    return lambda value: swap(value, bit, axis)


def core_step(near, far):
    return near, [(far, mover(1))]


def half_step(terms, bit):
    half = terms[0].shape[0] // 2
    return summed(terms, slice(0, half)), [(summed(terms, slice(half, None)), mover(bit))]


def quarter_step(terms, high, low):
    quarter = terms[0].shape[0] // 4
    sent = [
        (summed(terms, slice(k * quarter, (k + 1) * quarter)), mover(bit))
        for k, bit in ((2, high), (3, high ^ low), (1, low))
    ]
    return summed(terms, slice(0, quarter)), sent


def last_step(terms, bit):
    size = lax.axis_size("dp")
    mine, theirs = summed(terms, slice(0, 1)), summed(terms, slice(1, 2))
    across = [
        (2 * dp + seq, 2 * (dp ^ bit) + (1 - seq)) for dp in range(size) for seq in range(2)
    ]
    return mine, [
        (theirs, lambda value: lax.ppermute(value, ("dp", "seq"), across)),
        (theirs, mover(bit)),
        (mine, mover(1, "seq")),
    ]


def send(steps, ahead_of):
    ahead_of, values = tie((ahead_of, [[value for value, _ in sent] for _, sent in steps]))
    terms = [
        [kept] + [move(value) for value, (_, move) in zip(row, sent)]
        for row, (kept, sent) in zip(values, steps)
    ]
    return terms, ahead_of


def full_sum(terms):
    total = terms[0].astype(F32)
    for term in terms[1:]:
        total = total + term.astype(F32)
    return total[0]


def local(
    tokens,
    entity_flags,
    query_weight,
    key_weight,
    value_weight,
    mixing_weight,
    mixing_bias,
    first_gain,
    first_bias,
    up_weight,
    up_bias,
    down_weight,
    down_bias,
    second_gain,
    second_bias,
    cotangent,
):
    parts = lax.axis_size("dp")
    me = lax.axis_index("dp")
    share = D // parts
    rows = tokens.shape[0]
    by_swaps = share % 16 == 0 and parts & (parts - 1) == 0 and parts > 8

    six = jnp.concatenate([query_weight, key_weight[None], value_weight[None]], axis=0)
    pairs = jnp.transpose(six.reshape(6, share, PAIRS, LANES), (2, 1, 0, 3)).reshape(PAIRS, share, D)
    up_shard = jnp.transpose(up_weight.reshape(share, 4, D), (1, 0, 2)).reshape(4 * share, D)
    small = (mixing_bias, first_gain, first_bias, down_bias, second_gain, second_bias)
    vector_shard = jnp.concatenate([jnp.stack(small), up_bias.reshape(4, share)], axis=0)

    offsets = relative_offsets(parts) if by_swaps else list(range(parts))
    order = me ^ jnp.array(offsets, jnp.int32) if by_swaps else jnp.array(offsets, jnp.int32)
    column_of = (order[:, None] * share + jnp.arange(share, dtype=jnp.int32)[None, :]).reshape(D)
    choose = (lax.broadcasted_iota(jnp.int32, (D, D), 0) == column_of[None, :]).astype(BF)
    entity = entity_flags.astype(F32)
    tokens_other = swap(tokens, 1, "seq")
    entity_other = swap(entity, 1, "seq")

    shards = []
    start = 0
    for width in FORWARD_GROUPS:
        shards.append(pairs[start : start + width])
        start += width
    count = len(shards)
    vector_rows = 16
    own = dot(tokens, choose).astype(BF)
    if by_swaps:
        where = lax.broadcasted_iota(jnp.int32, (share, D), 0) + me * share
        spread = (lax.broadcasted_iota(jnp.int32, (share, D), 1) == where).astype(BF)
        placed = dot(jnp.stack(small), spread).astype(BF)
        place = me * 4 * share + lax.broadcasted_iota(jnp.int32, (4 * share, D), 0)
        spread = (lax.broadcasted_iota(jnp.int32, (4 * share, D), 1) == place % D).astype(BF)
        quarter_of = me * 4 * share + lax.broadcasted_iota(jnp.int32, (4, 4 * share), 1)
        mine = quarter_of // D == lax.broadcasted_iota(jnp.int32, (4, 4 * share), 0)
        up_placed = dot(jnp.where(mine, up_bias[None, :], 0).astype(BF), spread).astype(BF)
        padded = tie(jnp.concatenate([placed, up_placed, jnp.zeros((6, D), BF)], axis=0))
        middle_shard = jnp.concatenate([mixing_weight, padded, up_shard, down_weight], axis=0)
        up_at, down_at = share + vector_rows, 5 * share + vector_rows
    else:
        groups = []
        for shard in shards:
            full = lax.all_gather(shard, "dp", axis=1, tiled=True)
            groups.append([full.reshape(full.shape[0], 1, D, D)])
        mixing_full, up_full, down_full = (
            lax.all_gather(weight, "dp", axis=0, tiled=True)
            for weight in (mixing_weight, up_weight, down_weight)
        )
        quarter = D // 4
        up_quarters = jnp.transpose(up_full.reshape(4, quarter, 4, D), (0, 2, 1, 3)).reshape(4, D, D)
        mixing_up = jnp.concatenate([mixing_full.reshape(4, quarter, D), up_quarters], axis=1)
        down_shards = down_full.reshape(4, D, D)
        up_at, down_at = quarter, 0
        vectors = lax.all_gather(vector_shard, "dp", axis=0)
        up_vector = vectors[:, 6:].reshape(parts * 4 * share).reshape(4, D)
        vectors = jnp.concatenate(
            [jnp.transpose(vectors[:, :6], (1, 0, 2)).reshape(6, D), up_vector, jnp.zeros((6, D), BF)], axis=0
        ).astype(F32)
    own_entity = jnp.broadcast_to(entity[:, None], (rows, LANES))

    def partner():
        return dot(tokens_other, choose).astype(BF), jnp.broadcast_to(entity_other[:, None], (rows, LANES))

    saved = [None] * count
    if by_swaps:
        side = lax.axis_index("seq")
        groups = [None] * count
        held = [jnp.expand_dims(shard, 1) for shard in shards]
        for g in range(1, count):
            held[g] = lax.dynamic_slice_in_dim(held[g], side * (D // 2), D // 2, 3)
        beside = [None] * count
        bits = [1 << k for k in reversed(range(parts.bit_length() - 1))]
        plans = [[("dp", bit) for bit in bits]] + [
            [("dp", bit) for bit in bits[:-1]] + [("seq", 1), ("dp", 1)] for _ in range(count - 1)
        ]

        def whole_columns(mine, theirs):
            first = side == 0
            return jnp.concatenate([jnp.where(first, mine, theirs), jnp.where(first, theirs, mine)], axis=3)

        other, other_entity = None, None
        for step in range(max(len(plan) + g for g, plan in enumerate(plans))):
            active = [g for g in range(count) if 0 <= step - g < len(plans[g])]
            moved = {}
            for g in active:
                axis, bit = plans[g][step - g]
                both_parts = axis == "seq" or bit == 1
                moved[g] = (swap(held[g], bit, axis),) + ((swap(beside[g], bit, axis),) if both_parts else ())
            done = None
            for g in active:
                if plans[g][step - g] == ("dp", 1):
                    groups[g] = [held[g], beside[g], *moved.pop(g)]
                    if g == 0:
                        other, other_entity = partner()
                        both = (own, other, own_entity, other_entity)
                    saved[g] = attention_forward(*both, groups[g])
                    done = g
            waiting = sorted(moved)
            later = [held[g] for g in range(step + 1, min(step + 2, count))]
            tied = tie((
                tuple(moved[g] for g in waiting), None if done is None else saved[done][0], later, middle_shard
            ))
            if step == MIDDLE_STEP:
                gathered = lax.all_gather(tied[3], "dp", axis=0)
            if done is not None:
                saved[done] = (tied[1], *saved[done][1:])
            for g, value in zip(range(step + 1, min(step + 2, count)), tied[2]):
                held[g] = value
            for g, value in zip(waiting, tied[0]):
                axis, bit = plans[g][step - g]
                if axis == "seq":
                    held[g], beside[g] = whole_columns(held[g], value[0]), whole_columns(beside[g], value[1])
                elif bit == 2:
                    beside[g] = value[0]
                else:
                    held[g] = join(held[g], value[0])
        mixing_up = down_shards = gathered
        vectors = jnp.sum(gathered[:, share : share + vector_rows].astype(F32), axis=0)
    else:
        other, other_entity = partner()
        both = (own, other, own_entity, other_entity)
        saved = [attention_forward(*both, pieces) for pieces in groups]
    middle = (mixing_up, down_shards)
    mixed = [item[0] for item in saved]
    position = (me if by_swaps else jnp.int32(0)).astype(jnp.int32).reshape(1)
    (
        layer_out, down_near, down_far, hidden_low, slopes, normed, inverse, residual_grad, sums_one,
    ) = feed_forward(position, vectors, tokens, cotangent, mixed, middle, (up_at, down_at), by_swaps)

    def over_pieces(value):
        return value.astype(F32) + swap(value, 1, "seq").astype(F32)

    if by_swaps:
        down_bits = halving_bits(parts)[1:]
        pair_bits = [1 << k for k in range(1, parts.bit_length() - 1)]
        (down_state,), _ = send([core_step(down_near[:, None], down_far[:, None])], ())
        (down_state,), hidden_low = send([half_step(down_state, down_bits.pop(0))], hidden_low)
    middle_grad, stream_grad, sums_two, *mixed_grads = feed_back(
        vectors, sums_one, (hidden_low, slopes, normed, inverse, residual_grad), mixed, middle,
        (up_at, down_at),
    )

    def up_columns(value):
        return jnp.transpose(value, (1, 0, 2)).reshape(share, 4 * D)

    def vector_outputs(sums):
        sums = sums.astype(F32)

        def shard(row, width=1):
            return lax.dynamic_slice(
                sums[row : row + width].reshape(-1), (me * share * width,), (share * width,)
            )

        token_count = rows * parts * lax.axis_size("seq")
        stream_rms = jnp.sqrt(jnp.sum(sums[0:3], axis=1) / (token_count * D))
        return (shard(10), shard(8), shard(9), shard(11, 4), shard(5), shard(3), shard(4), stream_rms)

    joined, joined_other, near, far = ([None] * count for _ in range(4))
    before = None
    state = {}
    steps = {}

    def next_step(index):
        steps[index] = steps.get(index, -1) + 1
        return half_step(state[index], pair_bits[steps[index]])

    for index in reversed(range(count)):
        if by_swaps:
            fresh = index + 1 if index + 1 < count else None
            inputs = mixed_grads[index]
            if fresh is not None:
                (started,), (inputs, down_state, state) = send(
                    [core_step(near[fresh], far[fresh])], (inputs, down_state, state)
                )
            else:
                inputs, down_state = tie((inputs, down_state))
            order = list(state)
            if down_bits:
                down_step = half_step(down_state, down_bits.pop(0))
            else:
                mine = summed(down_state)
                down_step = (mine, [(mine, mover(1, "seq"))])
            (down_state, *sent), inputs = send([down_step] + [next_step(later) for later in order], inputs)
            state = dict(zip(order, sent))
            if fresh is not None:
                inputs, started = tie((inputs, started))
                state[fresh] = started
                (state[fresh],), inputs = send([next_step(fresh)], inputs)
            mixed_grads[index] = inputs
        near[index], far[index], joined[index], joined_other[index] = attention_backward(
            *both, saved[index], mixed_grads[index], 58 if index == count - 1 else 34,
            parts // 2 if by_swaps else 1,
        )
        if index < count - 1:
            done = index + 1
            near[index], joined[done] = tie((near[index], joined[done]))
            before = token_gradient(groups[done], joined[done], joined_other[done], before)
            before, mixed_grads, near[index] = tie((before, mixed_grads, near[index]))
    own_grad, other_grad = token_gradient(groups[0], joined[0], joined_other[0], before, BF)

    if by_swaps:
        middle_sum = lax.psum_scatter(middle_grad, "dp", scatter_dimension=0, tiled=True)[0]
        (started,), (down_state, state, other_grad) = send(
            [core_step(near[0], far[0])], (down_state, state, other_grad)
        )
        steps_now = []
        order = list(state)
        for later in order:
            left = pair_bits[steps[later] + 1 :]
            steps_now.append(half_step(state[later], *left) if len(left) == 1 else quarter_step(state[later], *left))
        sent, started = send(steps_now, started)
        down_sum = full_sum(down_state)[0]
        state = dict(zip(order, sent))
        (state[0], across), _ = send(
            [quarter_step(started, *pair_bits[:2]), (None, [(middle_sum, mover(1, "seq"))])], ()
        )
        _, other_grad = tie((state[0][0], other_grad))
        exchanged = [None, swap(other_grad, 1, "seq")]
        middle_sum = middle_sum.astype(F32) + across[1].astype(F32)
        mixing_sum = middle_sum[:share]
        up_sum = middle_sum[share : 5 * share].reshape(4, share, D)
        settled = (down_sum, mixing_sum, up_columns(up_sum), vector_outputs(middle_sum[5 * share :]))
        state, settled = tie((state, settled))
        down_sum, mixing_sum, up_out, from_sums = settled
        outer = jnp.concatenate([summed(state[later])[0] for later in range(1, count)], axis=0)
        (state[0], across), exchanged = send(
            [last_step(state[0], pair_bits[-1]), (None, [(outer, mover(1, "seq"))])],
            exchanged,
        )
        tokens_grad = finish_tokens(own_grad, exchanged[1], choose, stream_grad)
        outer = outer.astype(F32) + across[1].astype(F32)
        pair_sum = jnp.concatenate([full_sum(state[0]), outer], axis=0)
    else:
        tokens_grad = finish_tokens(own_grad, swap(other_grad, 1, "seq"), choose, stream_grad)
        sums = lax.psum(jnp.concatenate([sums_one, sums_two], axis=0), ("dp", "seq"))

        def reduced(value, axis):
            piece = lax.psum_scatter(value, "dp", scatter_dimension=axis, tiled=True)
            return lax.psum(piece, "seq").astype(F32)

        down_sum = reduced(jnp.concatenate([down_near, down_far], axis=0).reshape(-1, D), 0)
        mixing_sum = reduced(middle_grad[:, :quarter].reshape(D, D), 0)
        up_quarters = middle_grad[:, quarter : 5 * quarter].reshape(4, 4, quarter, D)
        up_sum = reduced(jnp.transpose(up_quarters, (1, 0, 2, 3)).reshape(4, D, D), 1)
        up_out, from_sums = up_columns(up_sum), vector_outputs(sums)
        pair_sum = jnp.concatenate(
            [reduced(jnp.concatenate([a[0], b[0]], axis=1), 1) for a, b in zip(near, far)], axis=0
        )

    six_sum = jnp.transpose(pair_sum.reshape(PAIRS, share, 6, LANES), (2, 1, 0, 3)).reshape(6, share, D)
    mixing_bias_sum, gain_one, bias_one, up_bias_sum, down_bias_sum, gain_two, bias_two, stream_rms = from_sums
    return (
        layer_out,
        tokens_grad,
        six_sum[0:4],
        six_sum[4],
        six_sum[5],
        mixing_sum,
        mixing_bias_sum,
        gain_one,
        bias_one,
        up_out,
        up_bias_sum,
        down_sum,
        down_bias_sum,
        gain_two,
        bias_two,
        stream_rms,
    )


def solution(mesh):
    rows = P(("dp", "seq"), None)
    vector = P("dp")
    matrix = P("dp", None)
    stacked = P(None, "dp", None)
    in_specs = (
        rows, P(("dp", "seq")), stacked, matrix, matrix, matrix, vector, vector, vector, matrix,
        vector, matrix, vector, vector, vector, rows,
    )
    out_specs = (
        rows, rows, stacked, matrix, matrix, matrix, vector, vector, vector, matrix, vector,
        matrix, vector, vector, vector, P(),
    )
    return jax.shard_map(local, mesh=mesh, in_specs=in_specs, out_specs=out_specs, check_vma=False)
```

```python
import functools

import jax
import jax.numpy as jnp
from jax import lax
from jax.experimental import pallas as pl
from jax.experimental.pallas import tpu as pltpu
from jax.sharding import PartitionSpec as P

D = 768
HEADS = 12
HD = 64
PAIRS = HEADS // 2
LANES = 2 * HD
F32 = jnp.float32
BF = jnp.bfloat16
EPSILON = 1e-05
LN2 = 0.6931471805599453
QUERY_SCALE = HD**-0.5 / LN2
FORWARD_GROUPS = (1, 2, 3)
SUM_ROWS = 16
MIDDLE_STEP = 0
MIB = 1024 * 1024


def dot(left, right):
    return jnp.dot(left, right, preferred_element_type=F32)


def dot_rt(left, right):
    return lax.dot_general(left, right, (((1,), (1,)), ((), ())), preferred_element_type=F32)


def dot_lt(left, right):
    return lax.dot_general(left, right, (((0,), (0,)), ((), ())), preferred_element_type=F32)


def call(kernel, mebibytes, **kwargs):
    return pl.pallas_call(
        kernel, compiler_params=pltpu.CompilerParams(vmem_limit_bytes=mebibytes * MIB), **kwargs
    )


def in_hbm(*arrays):
    return [pltpu.with_memory_space_constraint(array, pltpu.HBM) for array in arrays]


def whole_block(shape):
    return pl.BlockSpec(shape, lambda step: (0,) * len(shape))


def pair_block(shape):
    return pl.BlockSpec((1,) + shape, lambda step: (step,) + (0,) * len(shape))


def attention_forward_kernel(piece_count, own, other, own_entity, other_entity, *refs):
    pieces = refs[:piece_count]
    mixed, queries, keys, values, weights, totals, key_masked, value_ones, packed = refs[piece_count:]
    rows = own.shape[0]
    block = rows // 2
    lane = lax.broadcasted_iota(jnp.int32, (rows, LANES), 1)
    low = lane < HD
    at = 0
    for piece in pieces:
        part = piece[0].reshape(-1, D)
        packed[at : at + part.shape[0], :] = part
        at += part.shape[0]
    is_own = own_entity[...]
    is_other = other_entity[...]
    projected = dot(own[...], packed[...])
    entity_row = is_own > 0.5
    to_word = jnp.where(entity_row, projected[:, 256:384], projected[:, 0:128]) * QUERY_SCALE
    to_entity = jnp.where(entity_row, projected[:, 384:512], projected[:, 128:256]) * QUERY_SCALE
    queries[0, :, 0:LANES] = jnp.where(low, to_word, pltpu.roll(to_entity, HD, 1)).astype(BF)
    queries[0, :, LANES:] = jnp.where(low, pltpu.roll(to_word, HD, 1), to_entity).astype(BF)
    projected_other = dot(other[...], packed[:, 512:768])
    halves = (
        (projected[:, 512:640], projected[:, 640:768], is_own),
        (projected_other[:, 0:128], projected_other[:, 128:256], is_other),
    )
    for half, (key, value, entity) in enumerate(halves):
        at = pl.ds(half * rows, rows)
        keys[0, at, :] = key.astype(BF)
        values[0, at, :] = value.astype(BF)
        mask = jnp.where(low, 1.0 - entity, entity)
        turned = pltpu.roll(key, HD, 1)
        key_masked[at, 0:LANES] = (jnp.where(low, key, turned) * mask).astype(BF)
        key_masked[at, LANES:] = (jnp.where(low, turned, key) * mask).astype(BF)
        ones = jnp.ones_like(value)
        value_ones[at, 0:LANES] = jnp.where(low, value, ones).astype(BF)
        value_ones[at, LANES:] = jnp.where(low, ones, value).astype(BF)
    items = [(index, head) for index in range(rows // block) for head in range(2)]

    def scores_of(item):
        index, head = item
        columns = pl.ds(head * LANES, LANES)
        return dot_rt(queries[0, pl.ds(index * block, block), columns], key_masked[:, columns])

    ahead = scores_of(items[0])
    sums = []
    for number, (index, head) in enumerate(items):
        scores = ahead
        if number + 1 < len(items):
            ahead = scores_of(items[number + 1])
        at = pl.ds(index * block, block)
        highest = jnp.max(scores, axis=-1, keepdims=True)
        weight = jnp.exp2(scores - highest).astype(BF)
        weights[0, head, at, :] = weight
        sums.append(dot(weight, value_ones[:, pl.ds(head * LANES, LANES)]))
        if head:
            upper = jnp.where(low[:block], sums[0], sums[1])
            total = pltpu.roll(jnp.where(low[:block], sums[1], sums[0]), HD, 1)
            mixed[at, :] = (upper / total).astype(BF)
            totals[0, at, :] = total
            sums = []


def piece_blocks(pieces):
    return [pair_block(piece.shape[1:]) for piece in pieces]


def attention_forward(own, other, own_entity, other_entity, pieces):
    count = pieces[0].shape[0]
    rows = own.shape[0]
    length = 2 * rows
    return call(
        functools.partial(attention_forward_kernel, len(pieces)),
        30,
        grid=(count,),
        in_specs=[whole_block((rows, D))] * 2 + [whole_block((rows, LANES))] * 2 + piece_blocks(pieces),
        out_specs=[
            pl.BlockSpec((rows, LANES), lambda step: (0, step)),
            pair_block((rows, 2 * LANES)),
            pair_block((length, LANES)),
            pair_block((length, LANES)),
            pair_block((2, rows, length)),
            pair_block((rows, LANES)),
        ],
        out_shape=[
            pltpu.HBM((rows, LANES * count), BF),
            pltpu.HBM((count, rows, 2 * LANES), BF),
            pltpu.HBM((count, length, LANES), BF),
            pltpu.HBM((count, length, LANES), BF),
            pltpu.HBM((count, 2, rows, length), BF),
            pltpu.HBM((count, rows, LANES), F32),
        ],
        scratch_shapes=[
            pltpu.VMEM((length, 2 * LANES), BF),
            pltpu.VMEM((length, 2 * LANES), BF),
            pltpu.VMEM((D, D), BF),
        ],
        name="attention_forward",
        cost_estimate=pl.CostEstimate(
            flops=count * 7_000_000_000, transcendentals=count * 2400000, bytes_accessed=count * 8_000_000
        ),
    )(own, other, own_entity, other_entity, *pieces)


def attention_backward_kernel(own, other, own_entity, other_entity, *refs):
    queries, keys, values, weights, totals, mixed, grad = refs[:7]
    near, far, joined, joined_other = refs[7:11]
    key_masked, value_ones, grad_wide, query_grad, key_grad, value_grad = refs[11:]
    rows = own.shape[0]
    block = rows // 3
    lane = lax.broadcasted_iota(jnp.int32, (rows, LANES), 1)
    low = lane < HD
    is_own = own_entity[...]
    is_other = other_entity[...]
    for half, entity in enumerate((is_own, is_other)):
        at = pl.ds(half * rows, rows)
        key = keys[0, at, :].astype(F32)
        turned = pltpu.roll(key, HD, 1)
        mask = jnp.where(low, 1.0 - entity, entity)
        key_masked[at, 0:LANES] = (jnp.where(low, key, turned) * mask).astype(BF)
        key_masked[at, LANES:] = (jnp.where(low, turned, key) * mask).astype(BF)
        value = values[0, at, :].astype(F32)
        ones = jnp.where(lane % HD < 2, 1.0, 0.0)
        value_ones[at, 0:LANES] = jnp.where(low, value, ones).astype(BF)
        value_ones[at, LANES:] = jnp.where(low, ones, value).astype(BF)
    scaled = grad[...].astype(F32) / totals[0]
    inner = scaled * mixed[...].astype(F32)

    def correction(inner_sum):
        upper = inner_sum.astype(BF).astype(F32)
        return jnp.where(
            lane % HD == 0, -upper, jnp.where(lane % HD == 1, upper - inner_sum, 0.0)
        )

    first_inner = jnp.sum(jnp.where(low, inner, 0.0), axis=-1, keepdims=True)
    second_inner = jnp.sum(jnp.where(low, 0.0, inner), axis=-1, keepdims=True)
    grad_wide[:, 0:LANES] = jnp.where(low, scaled, correction(first_inner)).astype(BF)
    grad_wide[:, LANES:] = jnp.where(low, correction(second_inner), scaled).astype(BF)
    for head in range(2):
        columns = pl.ds(head * LANES, LANES)
        for index in range(rows // block):
            at = pl.ds(index * block, block)
            grad_block = grad_wide[at, columns]
            weight = weights[0, head, at, :]
            score_grad = (weight.astype(F32) * dot_rt(grad_block, value_ones[:, columns])).astype(BF)
            query_grad[at, columns] = dot(score_grad, key_masked[:, columns]) * HD**-0.5
            query_turned = queries[0, at, columns].astype(F32).T.astype(BF)
            grad_turned = grad_block.astype(F32).T[head * HD : (head + 1) * HD].astype(BF)
            key_part = dot(query_turned, score_grad)
            value_part = dot(grad_turned, weight)
            key_at = pl.ds(head * LANES, LANES)
            value_at = pl.ds(head * HD, HD)
            if index == 0:
                key_grad[key_at, :] = key_part
                value_grad[value_at, :] = value_part
            else:
                key_grad[key_at, :] += key_part
                value_grad[value_at, :] += value_part
    query_a = query_grad[:, 0:LANES]
    query_b = query_grad[:, LANES:]
    word_grad = jnp.where(low, query_a, pltpu.roll(query_b, HD, 1))
    entity_grad = jnp.where(low, pltpu.roll(query_a, HD, 1), query_b)
    is_word = 1.0 - is_own
    joined[0, :, 0:128] = (is_word * word_grad).astype(BF)
    joined[0, :, 128:256] = (is_word * entity_grad).astype(BF)
    joined[0, :, 256:384] = (is_own * word_grad).astype(BF)
    joined[0, :, 384:512] = (is_own * entity_grad).astype(BF)
    key_back = key_grad[...].T
    value_back = value_grad[...].T
    for half, entity in enumerate((is_own, is_other)):
        at = slice(half * rows, half * rows + rows)
        key_a = key_back[at, 0:LANES]
        key_b = key_back[at, LANES:]
        key_word = jnp.where(low, key_a, pltpu.roll(key_b, HD, 1))
        key_entity = jnp.where(low, pltpu.roll(key_a, HD, 1), key_b)
        key_part = (jnp.where(entity > 0.5, key_entity, key_word) * LN2).astype(BF)
        value_part = value_back[at].astype(BF)
        if half == 0:
            joined[0, :, 512:640] = key_part
            joined[0, :, 640:768] = value_part
        else:
            joined_other[0, :, 0:128] = key_part
            joined_other[0, :, 128:256] = value_part
    here = dot_lt(own[...], joined[0])
    there = dot_lt(other[...], joined_other[0])
    for target, at in ((near, slice(0, D // 2)), (far, slice(D // 2, D))):
        blocks = (target.shape[0], target.shape[2])
        target[:, 0, :, 0:512] = here[at, 0:512].astype(BF).reshape(*blocks, 512)
        target[:, 0, :, 512:768] = (here[at, 512:768] + there[at]).astype(BF).reshape(*blocks, 256)


def attention_backward(own, other, own_entity, other_entity, saved, grad, mebibytes, blocks):
    mixed, queries, keys, values, weights, totals = saved
    count = queries.shape[0]
    rows = own.shape[0]
    length = 2 * rows
    column = pl.BlockSpec((rows, LANES), lambda step: (0, step))
    return call(
        attention_backward_kernel,
        mebibytes,
        grid=(count,),
        in_specs=[whole_block((rows, D))] * 2
        + [whole_block((rows, LANES))] * 2
        + [
            pair_block((rows, 2 * LANES)),
            pair_block((length, LANES)),
            pair_block((length, LANES)),
            pair_block((2, rows, length)),
            pair_block((rows, LANES)),
            column,
            column,
        ],
        out_specs=[pl.BlockSpec((blocks, 1, D // 2 // blocks, D), lambda step: (0, step, 0, 0))] * 2
        + [pair_block((rows, D)), pair_block((rows, 2 * LANES))],
        out_shape=[jax.ShapeDtypeStruct((blocks, count, D // 2 // blocks, D), BF)] * 2
        + [
            jax.ShapeDtypeStruct((count, rows, D), BF),
            jax.ShapeDtypeStruct((count, rows, 2 * LANES), BF),
        ],
        scratch_shapes=[
            pltpu.VMEM((length, 2 * LANES), BF),
            pltpu.VMEM((length, 2 * LANES), BF),
            pltpu.VMEM((rows, 2 * LANES), BF),
            pltpu.VMEM((rows, 2 * LANES), F32),
            pltpu.VMEM((2 * LANES, length), F32),
            pltpu.VMEM((LANES, length), F32),
        ],
        name="attention_backward",
        cost_estimate=pl.CostEstimate(
            flops=count * 10_000_000_000, transcendentals=0, bytes_accessed=count * 12_000_000
        ),
    )(own, other, own_entity, other_entity, queries, keys, values, weights, totals, mixed, grad)


def token_gradient_kernel(piece_count, first, *refs):
    pieces = refs[:piece_count]
    refs = refs[piece_count:]
    joined, joined_other = refs[:2]
    refs = refs[2:]
    before = ()
    if not first:
        before, refs = refs[:2], refs[2:]
    *totals, packed = refs
    at = 0
    for piece in pieces:
        part = piece[0].reshape(-1, D)
        packed[at : at + part.shape[0], :] = part
        at += part.shape[0]
    step = pl.program_id(0)
    parts = (dot_rt(joined[0], packed[...]), dot_rt(joined_other[0], packed[:, 512:768]))
    for index, (total, part) in enumerate(zip(totals, parts)):

        @pl.when(step == 0)
        def _():
            total[...] = (part if first else before[index][...] + part).astype(total.dtype)

        @pl.when(step > 0)
        def _():
            total[...] = (total[...] + part).astype(total.dtype)


def token_gradient(pieces, joined, joined_other, before, other_type=F32):
    count, rows, _ = joined.shape
    first = before is None
    return call(
        functools.partial(token_gradient_kernel, len(pieces), first),
        16,
        grid=(count,),
        in_specs=piece_blocks(pieces)
        + [pair_block((rows, D)), pair_block((rows, 2 * LANES))]
        + [whole_block((rows, D))] * (0 if first else 2),
        out_specs=[whole_block((rows, D))] * 2,
        out_shape=[jax.ShapeDtypeStruct((rows, D), F32), jax.ShapeDtypeStruct((rows, D), other_type)],
        scratch_shapes=[pltpu.VMEM((D, D), BF)],
        name="token_gradient",
        cost_estimate=pl.CostEstimate(
            flops=count * 1_200_000_000, transcendentals=0, bytes_accessed=count * 4_000_000
        ),
    )(*pieces, joined, joined_other, *(before or ()))


def finish_kernel(own, received, choose, stream_grad, out):
    value = own[...] + received[...].astype(F32)
    upper = value.astype(BF)
    lower = (value - upper.astype(F32)).astype(BF)
    out[...] = (stream_grad[...] + dot_rt(upper, choose[...]) + dot_rt(lower, choose[...])).astype(BF)


def finish_tokens(own, received, choose, stream_grad):
    return call(
        finish_kernel,
        16,
        in_specs=[pl.BlockSpec(memory_space=pltpu.VMEM)] * 4,
        out_specs=pl.BlockSpec(memory_space=pltpu.VMEM),
        out_shape=jax.ShapeDtypeStruct(own.shape, BF),
        name="finish_tokens",
        cost_estimate=pl.CostEstimate(flops=2_000_000_000, transcendentals=0, bytes_accessed=8_000_000),
    )(own, received, choose, stream_grad)


def error_function(value):
    value = jnp.clip(value, -3.7439211627767994, 3.7439211627767994)
    square = value * value
    upper = jnp.float32(0.00022905065861350646)
    for term in (
        0.0034082910107109506, 0.050955695062380861, 0.18520832239976145, 1.128379143519084,
    ):
        upper = upper * square + term
    lower = jnp.float32(-1.1791602954361697e-7)
    for term in (
        0.000023547966471313185, 0.0010179625278914885, 0.014070470171167667,
        0.11098505178285362, 0.49746925110067538, 1.0,
    ):
        lower = lower * square + term
    return value * upper / lower


def wait_all(copies):
    for copy in copies:
        copy.wait()


def weight_copies(share, starts, mixing_up, down_shards, mixing, up, down, sems):
    return (
        pltpu.make_async_copy(mixing_up.at[:, pl.ds(0, share)], mixing, sems.at[0]),
        [
            pltpu.make_async_copy(
                mixing_up.at[:, pl.ds(starts[0] + quarter * share, share)], up.at[quarter], sems.at[1 + quarter]
            )
            for quarter in range(4)
        ],
        pltpu.make_async_copy(down_shards.at[:, pl.ds(starts[1], 4 * share)], down, sems.at[5]),
    )


def arrivals(pairs, sems):
    return [
        pltpu.make_async_copy(source, target, sems.at[index]) for index, (source, target) in enumerate(pairs)
    ]


def side_by_side(groups, target):
    pairs = []
    start = 0
    for group in groups:
        width = group.shape[1]
        pairs.append((group, target.at[:, pl.ds(start, width)]))
        start += width
    return pairs


def make_adder(sums):
    def add_sum(index, value, start):
        part = jnp.sum(value, axis=0, keepdims=True)
        if start:
            sums[index : index + 1, :] = part
        else:
            sums[index : index + 1, :] += part

    return add_sum


def halving_bits(parts):
    return [1 << k for k in range(parts.bit_length() - 1)]


def relative_place(block, me, parts, relative):
    if not relative:
        return jnp.int32(block)
    offset = me ^ block
    place = 0
    for bit in halving_bits(parts):
        place = 2 * place + jnp.where(offset & bit, 1, 0)
    return place


def feed_forward_kernel(group_count, share, up_at, relative, position, vectors, tokens_in, cotangent_in, *refs):
    mixed_groups = refs[:group_count]
    (
        mixing_up, down_shards, layer_to, near, far, hidden_to, slopes_out, normed_to, inverse_to,
        residual_to, sums, mixing, up, down, active, slopes, total, hidden, low_grad, down_grad,
        in_sems, out_sems, slope_sems, mixed, tokens, cotangent, row_sems, layer_out, hidden_low,
        normed_out, inverse_out, residual_grad, leave_sems,
    ) = refs[group_count:]
    leaving = arrivals(
        [
            (hidden_low, hidden_to),
            (normed_out, normed_to),
            (inverse_out, inverse_to),
            (layer_out, layer_to),
            (residual_grad, residual_to),
        ],
        leave_sems,
    )
    rows = tokens.shape[0]
    block = rows // 3
    row_copies = arrivals(
        [*side_by_side(mixed_groups, mixed), (tokens_in, tokens), (cotangent_in, cotangent)], row_sems
    )
    chunk = down.shape[0] // 4
    mixing_copy, up_copies, down_copy = weight_copies(
        share, up_at, mixing_up, down_shards, mixing, up, down, in_sems
    )
    mixing_copy.start()
    for copy in row_copies:
        copy.start()
    for copy in up_copies:
        copy.start()
    down_copy.start()
    add_sum = make_adder(sums)

    def vector(index):
        return vectors[index : index + 1, :]

    sums[6:8, :] = jnp.zeros((2, D), F32)
    mixing_copy.wait()
    wait_all(row_copies[:-1])
    for index in range(3):
        at = pl.ds(index * block, block)
        attended = dot(mixed[at, :], mixing[...].reshape(D, D)) + vector(0)
        stream = tokens[at, :].astype(F32) + attended
        add_sum(0, stream * stream, index == 0)
        add_sum(1, attended * attended, index == 0)
        center = stream - jnp.mean(stream, axis=-1, keepdims=True)
        inverse = lax.rsqrt(jnp.mean(center * center, axis=-1, keepdims=True) + EPSILON)
        normed = center * inverse
        normed_out[at, :] = normed
        inverse_out[at, :] = jnp.broadcast_to(inverse, (block, LANES))
        value = normed * vector(1) + vector(2)
        hidden[at, :] = value
        hidden_low[at, :] = value.astype(BF)
    for copy in leaving[:3]:
        copy.start()
    down_copy.wait()
    slope_copies = []
    for quarter in range(4):
        up_copies[quarter].wait()
        up_part = up[quarter].reshape(D, D)
        down_part = down[quarter * chunk : (quarter + 1) * chunk].reshape(D, D)
        for index in range(3):
            at = pl.ds(index * block, block)
            before = dot(hidden_low[at, :], up_part) + vector(6 + quarter)
            scaled_before = before * 0.7071067811865476
            half = 0.5 + 0.5 * error_function(scaled_before)
            act = (before * half).astype(BF)
            active[quarter, at, :] = act
            bell = jnp.exp(-(scaled_before * scaled_before))
            slope = half + before * (bell * 0.3989422804014327)
            slopes[quarter, at, :] = slope.astype(BF)
            part = dot(act, down_part)
            if quarter == 0:
                total[at, :] = part
            else:
                total[at, :] += part
        slope_copies.append(
            pltpu.make_async_copy(slopes.at[quarter], slopes_out.at[quarter], slope_sems.at[quarter])
        )
        slope_copies[-1].start()
    row_copies[-1].wait()
    for index in range(3):
        at = pl.ds(index * block, block)
        forward_out = total[at, :] + vector(3)
        add_sum(2, forward_out * forward_out, index == 0)
        value = hidden[at, :] + forward_out
        center = value - jnp.mean(value, axis=-1, keepdims=True)
        inverse = lax.rsqrt(jnp.mean(center * center, axis=-1, keepdims=True) + EPSILON)
        normed = center * inverse
        layer_out[at, :] = (normed * vector(4) + vector(5)).astype(BF)
        upstream = cotangent[at, :].astype(F32)
        scaled = upstream * vector(4)
        inner = (
            scaled
            - jnp.mean(scaled, axis=-1, keepdims=True)
            - normed * jnp.mean(scaled * normed, axis=-1, keepdims=True)
        ) * inverse
        residual_grad[at, :] = inner
        rounded = inner.astype(BF)
        low_grad[at, :] = rounded
        add_sum(3, upstream * normed, index == 0)
        add_sum(4, upstream, index == 0)
        add_sum(5, rounded.astype(F32), index == 0)
    for copy in leaving[3:]:
        copy.start()
    parts = down.shape[0]
    half_parts = parts // 2
    for quarter in range(4):
        grad = dot_lt(active[quarter], low_grad[...])
        at = pl.ds(quarter * chunk, chunk)
        down_grad[at] = grad.astype(BF).reshape(chunk, -1, D)
        for block in range(quarter * chunk, (quarter + 1) * chunk):
            place = relative_place(block, position[0], parts, relative)

            @pl.when(place < half_parts)
            def _():
                pltpu.make_async_copy(
                    down_grad.at[block], near.at[place], out_sems.at[block]
                ).start()

            @pl.when(place >= half_parts)
            def _():
                pltpu.make_async_copy(
                    down_grad.at[block], far.at[place - half_parts], out_sems.at[block]
                ).start()

    wait_all(slope_copies)
    wait_all(leaving)
    for block in range(parts):
        pltpu.make_async_copy(down_grad.at[block], near.at[0], out_sems.at[block]).wait()


def feed_forward(position, vectors, tokens, cotangent, groups, weights, up_at, relative):
    rows = tokens.shape[0]
    parts = weights[0].shape[0]
    share = D // parts
    anywhere = pl.BlockSpec(memory_space=pltpu.HBM)
    vmem = pl.BlockSpec(memory_space=pltpu.VMEM)
    return call(
        functools.partial(feed_forward_kernel, len(groups), share, up_at, relative),
        50,
        in_specs=[pl.BlockSpec(memory_space=pltpu.SMEM), vmem] + [anywhere] * (4 + len(groups)),
        out_specs=[anywhere] * 8 + [vmem],
        out_shape=[
            jax.ShapeDtypeStruct((rows, D), BF),
            jax.ShapeDtypeStruct((parts // 2, 4 * share, D), BF),
            jax.ShapeDtypeStruct((parts // 2, 4 * share, D), BF),
            jax.ShapeDtypeStruct((rows, D), BF),
            jax.ShapeDtypeStruct((4, rows, D), BF),
            jax.ShapeDtypeStruct((rows, D), F32),
            jax.ShapeDtypeStruct((rows, LANES), F32),
            jax.ShapeDtypeStruct((rows, D), F32),
            jax.ShapeDtypeStruct((8, D), F32),
        ],
        scratch_shapes=[
            pltpu.VMEM((parts, share, D), BF),
            pltpu.VMEM((4, parts, share, D), BF),
            pltpu.VMEM((parts, 4 * share, D), BF),
            pltpu.VMEM((4, rows, D), BF),
            pltpu.VMEM((4, rows, D), BF),
            pltpu.VMEM((rows, D), F32),
            pltpu.VMEM((rows, D), F32),
            pltpu.VMEM((rows, D), BF),
            pltpu.VMEM((parts, 4 * share, D), BF),
            pltpu.SemaphoreType.DMA((6,)),
            pltpu.SemaphoreType.DMA((parts,)),
            pltpu.SemaphoreType.DMA((4,)),
            pltpu.VMEM((rows, D), BF),
            pltpu.VMEM((rows, D), BF),
            pltpu.VMEM((rows, D), BF),
            pltpu.SemaphoreType.DMA((2 + len(groups),)),
            pltpu.VMEM((rows, D), BF),
            pltpu.VMEM((rows, D), BF),
            pltpu.VMEM((rows, D), F32),
            pltpu.VMEM((rows, LANES), F32),
            pltpu.VMEM((rows, D), F32),
            pltpu.SemaphoreType.DMA((5,)),
        ],
        name="feed_forward",
        cost_estimate=pl.CostEstimate(
            flops=12_000_000_000, transcendentals=4800000, bytes_accessed=40_000_000
        ),
    )(position, vectors, *in_hbm(tokens, cotangent, *groups, *weights))


def feed_back_kernel(
    group_count, share, up_at, vectors, sums_before, hidden_in, normed_in, inverse_in, residual_in, *refs
):
    mixed_groups = refs[:group_count]
    slopes_in, mixing_up, down_shards, grads_out, stream_grad, sums = refs[group_count : group_count + 6]
    refs = refs[group_count + 6 :]
    grad_groups = refs[:group_count]
    (
        mixing, up, down, slopes, hidden_turned, pre_grad, low_grad, back, up_grad, mixing_grad,
        sums_low, in_sems, out_sems, slope_sems, mixed, hidden_low, normed, inverse, residual_grad, row_sems,
    ) = refs[group_count:]
    rows = hidden_low.shape[0]
    block = rows // 3
    row_copies = arrivals(
        [
            (residual_in, residual_grad),
            (hidden_in, hidden_low),
            *side_by_side(mixed_groups, mixed),
            (normed_in, normed),
            (inverse_in, inverse),
        ],
        row_sems,
    )
    for copy in row_copies[:2]:
        copy.start()
    parts = mixing.shape[0]
    chunk = parts // 4
    mixing_copy, up_copies, down_copy = weight_copies(
        share, up_at, mixing_up, down_shards, mixing, up, down, in_sems
    )
    slope_copies = [
        pltpu.make_async_copy(slopes_in.at[quarter], slopes.at[quarter], slope_sems.at[quarter])
        for quarter in range(4)
    ]
    down_copy.start()
    for quarter in range(4):
        slope_copies[quarter].start()
        up_copies[quarter].start()
    mixing_copy.start()
    for copy in row_copies[2:]:
        copy.start()
    add_sum = make_adder(sums)

    def vector(index):
        return vectors[index : index + 1, :]

    sums[7:8, :] = jnp.zeros((1, D), F32)
    wait_all(row_copies[:2])
    low_grad[...] = residual_grad[...].astype(BF)
    hidden_turned[...] = hidden_low[...].T
    down_copy.wait()
    grad_copies = []
    for quarter in range(4):
        slope_copies[quarter].wait()
        up_copies[quarter].wait()
        up_part = up[quarter].reshape(D, D)
        down_part = down[quarter * chunk : (quarter + 1) * chunk].reshape(D, D)
        for index in range(3):
            at = pl.ds(index * block, block)
            part = (dot_rt(low_grad[at, :], down_part) * slopes[quarter, at, :].astype(F32)).astype(BF)
            pre_grad[quarter % 2, at, :] = part
            add_sum(3 + quarter, part.astype(F32), index == 0)
            back_part = dot_rt(part, up_part)
            if quarter == 0:
                back[at, :] = back_part
            else:
                back[at, :] += back_part
        grad = dot(hidden_turned[...], pre_grad[quarter % 2])
        up_grad[quarter] = grad.astype(BF).reshape(parts, share, D)
        grad_copies.append(
            pltpu.make_async_copy(
                up_grad.at[quarter],
                grads_out.at[:, pl.ds((1 + quarter) * share, share)],
                out_sems.at[quarter],
            )
        )
        grad_copies[-1].start()
    mixing_copy.wait()
    wait_all(row_copies[2:])
    for index in range(3):
        at = pl.ds(index * block, block)
        hidden_grad = residual_grad[at, :] + back[at, :]
        norm = normed[at, :]
        scaled = hidden_grad * vector(1)
        inner = (
            scaled
            - jnp.mean(scaled, axis=-1, keepdims=True)
            - norm * jnp.mean(scaled * norm, axis=-1, keepdims=True)
        ) * inverse[at, 0:1]
        stream_grad[at, :] = inner
        rounded = inner.astype(BF)
        low_grad[at, :] = rounded
        add_sum(0, hidden_grad * norm, index == 0)
        add_sum(1, hidden_grad, index == 0)
        add_sum(2, rounded.astype(F32), index == 0)
        mixed_grad = dot_rt(rounded, mixing[...].reshape(D, D)).astype(BF)
        start = 0
        for group in grad_groups:
            width = group.shape[1]
            group[at, :] = mixed_grad[:, start : start + width]
            start += width
    back[...] = dot_lt(mixed[...], low_grad[...])
    mixing_grad[...] = back[...].astype(BF).reshape(parts, share, D)
    grad_copies.append(
        pltpu.make_async_copy(mixing_grad, grads_out.at[:, pl.ds(0, share)], out_sems.at[4])
    )
    grad_copies[-1].start()
    both_sums = jnp.concatenate([sums_before[...], sums[...]], axis=0).astype(BF)
    sums_low[...] = jnp.broadcast_to(both_sums[None], sums_low.shape)
    grad_copies.append(
        pltpu.make_async_copy(sums_low, grads_out.at[:, pl.ds(5 * share, SUM_ROWS)], out_sems.at[5])
    )
    grad_copies[-1].start()
    wait_all(grad_copies)


def feed_back(vectors, sums_before, saved, groups, weights, up_at):
    hidden_low, slopes, normed, inverse, residual_grad = saved
    rows = hidden_low.shape[0]
    parts = weights[0].shape[0]
    share = D // parts
    anywhere = pl.BlockSpec(memory_space=pltpu.HBM)
    vmem = pl.BlockSpec(memory_space=pltpu.VMEM)
    return call(
        functools.partial(feed_back_kernel, len(groups), share, up_at),
        50,
        in_specs=[vmem] * 2 + [anywhere] * (7 + len(groups)),
        out_specs=[anywhere] + [vmem] * (2 + len(groups)),
        out_shape=[
            jax.ShapeDtypeStruct((parts, 5 * share + SUM_ROWS, D), BF),
            jax.ShapeDtypeStruct((rows, D), F32),
            jax.ShapeDtypeStruct((8, D), F32),
        ]
        + [jax.ShapeDtypeStruct(group.shape, BF) for group in groups],
        scratch_shapes=[
            pltpu.VMEM((parts, share, D), BF),
            pltpu.VMEM((4, parts, share, D), BF),
            pltpu.VMEM((parts, 4 * share, D), BF),
            pltpu.VMEM((4, rows, D), BF),
            pltpu.VMEM((D, rows), BF),
            pltpu.VMEM((2, rows, D), BF),
            pltpu.VMEM((rows, D), BF),
            pltpu.VMEM((rows, D), F32),
            pltpu.VMEM((4, parts, share, D), BF),
            pltpu.VMEM((parts, share, D), BF),
            pltpu.VMEM((parts, SUM_ROWS, D), BF),
            pltpu.SemaphoreType.DMA((6,)),
            pltpu.SemaphoreType.DMA((6,)),
            pltpu.SemaphoreType.DMA((4,)),
            pltpu.VMEM((rows, D), BF),
            pltpu.VMEM((rows, D), BF),
            pltpu.VMEM((rows, D), F32),
            pltpu.VMEM((rows, LANES), F32),
            pltpu.VMEM((rows, D), F32),
            pltpu.SemaphoreType.DMA((4 + len(groups),)),
        ],
        name="feed_back",
        cost_estimate=pl.CostEstimate(
            flops=13_000_000_000, transcendentals=0, bytes_accessed=40_000_000
        ),
    )(vectors, sums_before, *in_hbm(hidden_low, normed, inverse, residual_grad, *groups, slopes, *weights))


def swap(value, bit, axis="dp"):
    size = lax.axis_size(axis)
    return lax.ppermute(value, axis, [(index, index ^ bit) for index in range(size)])


def relative_offsets(size):
    offsets = [0]
    bit = size // 2
    while bit:
        offsets += [offset ^ bit for offset in offsets]
        bit //= 2
    return offsets


tie = lax.optimization_barrier


def join(*values):
    return jnp.concatenate(values, axis=1)


def summed(terms, at=slice(None)):
    total = terms[0][at].astype(F32)
    for term in terms[1:]:
        total = total + term[at].astype(F32)
    return total.astype(BF)


def mover(bit, axis="dp"):
    return lambda value: swap(value, bit, axis)


def core_step(near, far):
    return near, [(far, mover(1))]


def half_step(terms, bit):
    half = terms[0].shape[0] // 2
    return summed(terms, slice(0, half)), [(summed(terms, slice(half, None)), mover(bit))]


def quarter_step(terms, high, low):
    quarter = terms[0].shape[0] // 4
    sent = [
        (summed(terms, slice(k * quarter, (k + 1) * quarter)), mover(bit))
        for k, bit in ((2, high), (3, high ^ low), (1, low))
    ]
    return summed(terms, slice(0, quarter)), sent


def last_step(terms, bit):
    size = lax.axis_size("dp")
    mine, theirs = summed(terms, slice(0, 1)), summed(terms, slice(1, 2))
    across = [
        (2 * dp + seq, 2 * (dp ^ bit) + (1 - seq)) for dp in range(size) for seq in range(2)
    ]
    return mine, [
        (theirs, lambda value: lax.ppermute(value, ("dp", "seq"), across)),
        (theirs, mover(bit)),
        (mine, mover(1, "seq")),
    ]


def send(steps, ahead_of):
    ahead_of, values = tie((ahead_of, [[value for value, _ in sent] for _, sent in steps]))
    terms = [
        [kept] + [move(value) for value, (_, move) in zip(row, sent)]
        for row, (kept, sent) in zip(values, steps)
    ]
    return terms, ahead_of


def full_sum(terms):
    total = terms[0].astype(F32)
    for term in terms[1:]:
        total = total + term.astype(F32)
    return total[0]


def local(
    tokens,
    entity_flags,
    query_weight,
    key_weight,
    value_weight,
    mixing_weight,
    mixing_bias,
    first_gain,
    first_bias,
    up_weight,
    up_bias,
    down_weight,
    down_bias,
    second_gain,
    second_bias,
    cotangent,
):
    parts = lax.axis_size("dp")
    me = lax.axis_index("dp")
    share = D // parts
    rows = tokens.shape[0]
    by_swaps = share % 16 == 0 and parts & (parts - 1) == 0 and parts > 8

    six = jnp.concatenate([query_weight, key_weight[None], value_weight[None]], axis=0)
    pairs = jnp.transpose(six.reshape(6, share, PAIRS, LANES), (2, 1, 0, 3)).reshape(PAIRS, share, D)
    up_shard = jnp.transpose(up_weight.reshape(share, 4, D), (1, 0, 2)).reshape(4 * share, D)
    small = (mixing_bias, first_gain, first_bias, down_bias, second_gain, second_bias)
    vector_shard = jnp.concatenate([jnp.stack(small), up_bias.reshape(4, share)], axis=0)

    offsets = relative_offsets(parts) if by_swaps else list(range(parts))
    order = me ^ jnp.array(offsets, jnp.int32) if by_swaps else jnp.array(offsets, jnp.int32)
    column_of = (order[:, None] * share + jnp.arange(share, dtype=jnp.int32)[None, :]).reshape(D)
    choose = (lax.broadcasted_iota(jnp.int32, (D, D), 0) == column_of[None, :]).astype(BF)
    entity = entity_flags.astype(F32)
    tokens_other = swap(tokens, 1, "seq")
    entity_other = swap(entity, 1, "seq")

    shards = []
    start = 0
    for width in FORWARD_GROUPS:
        shards.append(pairs[start : start + width])
        start += width
    count = len(shards)
    vector_rows = 16
    own = dot(tokens, choose).astype(BF)
    if by_swaps:
        where = lax.broadcasted_iota(jnp.int32, (share, D), 0) + me * share
        spread = (lax.broadcasted_iota(jnp.int32, (share, D), 1) == where).astype(BF)
        placed = dot(jnp.stack(small), spread).astype(BF)
        place = me * 4 * share + lax.broadcasted_iota(jnp.int32, (4 * share, D), 0)
        spread = (lax.broadcasted_iota(jnp.int32, (4 * share, D), 1) == place % D).astype(BF)
        quarter_of = me * 4 * share + lax.broadcasted_iota(jnp.int32, (4, 4 * share), 1)
        mine = quarter_of // D == lax.broadcasted_iota(jnp.int32, (4, 4 * share), 0)
        up_placed = dot(jnp.where(mine, up_bias[None, :], 0).astype(BF), spread).astype(BF)
        padded = tie(jnp.concatenate([placed, up_placed, jnp.zeros((6, D), BF)], axis=0))
        middle_shard = jnp.concatenate([mixing_weight, padded, up_shard, down_weight], axis=0)
        up_at, down_at = share + vector_rows, 5 * share + vector_rows
    else:
        groups = []
        for shard in shards:
            full = lax.all_gather(shard, "dp", axis=1, tiled=True)
            groups.append([full.reshape(full.shape[0], 1, D, D)])
        mixing_full, up_full, down_full = (
            lax.all_gather(weight, "dp", axis=0, tiled=True)
            for weight in (mixing_weight, up_weight, down_weight)
        )
        quarter = D // 4
        up_quarters = jnp.transpose(up_full.reshape(4, quarter, 4, D), (0, 2, 1, 3)).reshape(4, D, D)
        mixing_up = jnp.concatenate([mixing_full.reshape(4, quarter, D), up_quarters], axis=1)
        down_shards = down_full.reshape(4, D, D)
        up_at, down_at = quarter, 0
        vectors = lax.all_gather(vector_shard, "dp", axis=0)
        up_vector = vectors[:, 6:].reshape(parts * 4 * share).reshape(4, D)
        vectors = jnp.concatenate(
            [jnp.transpose(vectors[:, :6], (1, 0, 2)).reshape(6, D), up_vector, jnp.zeros((6, D), BF)], axis=0
        ).astype(F32)
    own_entity = jnp.broadcast_to(entity[:, None], (rows, LANES))

    def partner():
        return dot(tokens_other, choose).astype(BF), jnp.broadcast_to(entity_other[:, None], (rows, LANES))

    saved = [None] * count
    if by_swaps:
        side = lax.axis_index("seq")
        groups = [None] * count
        held = [jnp.expand_dims(shard, 1) for shard in shards]
        for g in range(1, count):
            held[g] = lax.dynamic_slice_in_dim(held[g], side * (D // 2), D // 2, 3)
        beside = [None] * count
        bits = [1 << k for k in reversed(range(parts.bit_length() - 1))]
        plans = [[("dp", bit) for bit in bits]] + [
            [("dp", bit) for bit in bits[:-1]] + [("seq", 1), ("dp", 1)] for _ in range(count - 1)
        ]

        def whole_columns(mine, theirs):
            first = side == 0
            return jnp.concatenate([jnp.where(first, mine, theirs), jnp.where(first, theirs, mine)], axis=3)

        other, other_entity = None, None
        for step in range(max(len(plan) + g for g, plan in enumerate(plans))):
            active = [g for g in range(count) if 0 <= step - g < len(plans[g])]
            moved = {}
            for g in active:
                axis, bit = plans[g][step - g]
                both_parts = axis == "seq" or bit == 1
                moved[g] = (swap(held[g], bit, axis),) + ((swap(beside[g], bit, axis),) if both_parts else ())
            done = None
            for g in active:
                if plans[g][step - g] == ("dp", 1):
                    groups[g] = [held[g], beside[g], *moved.pop(g)]
                    if g == 0:
                        other, other_entity = partner()
                        both = (own, other, own_entity, other_entity)
                    saved[g] = attention_forward(*both, groups[g])
                    done = g
            waiting = sorted(moved)
            later = [held[g] for g in range(step + 1, min(step + 2, count))]
            tied = tie((
                tuple(moved[g] for g in waiting), None if done is None else saved[done][0], later, middle_shard
            ))
            if step == MIDDLE_STEP:
                gathered = lax.all_gather(tied[3], "dp", axis=0)
            if done is not None:
                saved[done] = (tied[1], *saved[done][1:])
            for g, value in zip(range(step + 1, min(step + 2, count)), tied[2]):
                held[g] = value
            for g, value in zip(waiting, tied[0]):
                axis, bit = plans[g][step - g]
                if axis == "seq":
                    held[g], beside[g] = whole_columns(held[g], value[0]), whole_columns(beside[g], value[1])
                elif bit == 2:
                    beside[g] = value[0]
                else:
                    held[g] = join(held[g], value[0])
        mixing_up = down_shards = gathered
        vectors = jnp.sum(gathered[:, share : share + vector_rows].astype(F32), axis=0)
    else:
        other, other_entity = partner()
        both = (own, other, own_entity, other_entity)
        saved = [attention_forward(*both, pieces) for pieces in groups]
    middle = (mixing_up, down_shards)
    mixed = [item[0] for item in saved]
    position = (me if by_swaps else jnp.int32(0)).astype(jnp.int32).reshape(1)
    (
        layer_out, down_near, down_far, hidden_low, slopes, normed, inverse, residual_grad, sums_one,
    ) = feed_forward(position, vectors, tokens, cotangent, mixed, middle, (up_at, down_at), by_swaps)

    def over_pieces(value):
        return value.astype(F32) + swap(value, 1, "seq").astype(F32)

    if by_swaps:
        down_bits = halving_bits(parts)[1:]
        pair_bits = [1 << k for k in range(1, parts.bit_length() - 1)]
        (down_state,), _ = send([core_step(down_near[:, None], down_far[:, None])], ())
        (down_state,), hidden_low = send([half_step(down_state, down_bits.pop(0))], hidden_low)
    middle_grad, stream_grad, sums_two, *mixed_grads = feed_back(
        vectors, sums_one, (hidden_low, slopes, normed, inverse, residual_grad), mixed, middle,
        (up_at, down_at),
    )

    def up_columns(value):
        return jnp.transpose(value, (1, 0, 2)).reshape(share, 4 * D)

    def vector_outputs(sums):
        sums = sums.astype(F32)

        def shard(row, width=1):
            return lax.dynamic_slice(
                sums[row : row + width].reshape(-1), (me * share * width,), (share * width,)
            )

        token_count = rows * parts * lax.axis_size("seq")
        stream_rms = jnp.sqrt(jnp.sum(sums[0:3], axis=1) / (token_count * D))
        return (shard(10), shard(8), shard(9), shard(11, 4), shard(5), shard(3), shard(4), stream_rms)

    joined, joined_other, near, far = ([None] * count for _ in range(4))
    before = None
    state = {}
    steps = {}

    def next_step(index):
        steps[index] = steps.get(index, -1) + 1
        return half_step(state[index], pair_bits[steps[index]])

    for index in reversed(range(count)):
        if by_swaps:
            fresh = index + 1 if index + 1 < count else None
            inputs = mixed_grads[index]
            if fresh is not None:
                (started,), (inputs, down_state, state) = send(
                    [core_step(near[fresh], far[fresh])], (inputs, down_state, state)
                )
            else:
                inputs, down_state = tie((inputs, down_state))
            order = list(state)
            if down_bits:
                down_step = half_step(down_state, down_bits.pop(0))
            else:
                mine = summed(down_state)
                down_step = (mine, [(mine, mover(1, "seq"))])
            (down_state, *sent), inputs = send([down_step] + [next_step(later) for later in order], inputs)
            state = dict(zip(order, sent))
            if fresh is not None:
                inputs, started = tie((inputs, started))
                state[fresh] = started
                (state[fresh],), inputs = send([next_step(fresh)], inputs)
            mixed_grads[index] = inputs
        near[index], far[index], joined[index], joined_other[index] = attention_backward(
            *both, saved[index], mixed_grads[index], 58 if index == count - 1 else 34,
            parts // 2 if by_swaps else 1,
        )
        if index < count - 1:
            done = index + 1
            near[index], joined[done] = tie((near[index], joined[done]))
            before = token_gradient(groups[done], joined[done], joined_other[done], before)
            before, mixed_grads, near[index] = tie((before, mixed_grads, near[index]))
    own_grad, other_grad = token_gradient(groups[0], joined[0], joined_other[0], before, BF)

    if by_swaps:
        middle_sum = lax.psum_scatter(middle_grad, "dp", scatter_dimension=0, tiled=True)[0]
        (started,), (down_state, state, other_grad) = send(
            [core_step(near[0], far[0])], (down_state, state, other_grad)
        )
        steps_now = []
        order = list(state)
        for later in order:
            left = pair_bits[steps[later] + 1 :]
            steps_now.append(half_step(state[later], *left) if len(left) == 1 else quarter_step(state[later], *left))
        sent, started = send(steps_now, started)
        down_sum = full_sum(down_state)[0]
        state = dict(zip(order, sent))
        (state[0], across), _ = send(
            [quarter_step(started, *pair_bits[:2]), (None, [(middle_sum, mover(1, "seq"))])], ()
        )
        _, other_grad = tie((state[0][0], other_grad))
        exchanged = [None, swap(other_grad, 1, "seq")]
        middle_sum = middle_sum.astype(F32) + across[1].astype(F32)
        mixing_sum = middle_sum[:share]
        up_sum = middle_sum[share : 5 * share].reshape(4, share, D)
        settled = (down_sum, mixing_sum, up_columns(up_sum), vector_outputs(middle_sum[5 * share :]))
        state, settled = tie((state, settled))
        down_sum, mixing_sum, up_out, from_sums = settled
        outer = jnp.concatenate([summed(state[later])[0] for later in range(1, count)], axis=0)
        (state[0], across), exchanged = send(
            [last_step(state[0], pair_bits[-1]), (None, [(outer, mover(1, "seq"))])],
            exchanged,
        )
        tokens_grad = finish_tokens(own_grad, exchanged[1], choose, stream_grad)
        outer = outer.astype(F32) + across[1].astype(F32)
        pair_sum = jnp.concatenate([full_sum(state[0]), outer], axis=0)
    else:
        tokens_grad = finish_tokens(own_grad, swap(other_grad, 1, "seq"), choose, stream_grad)
        sums = lax.psum(jnp.concatenate([sums_one, sums_two], axis=0), ("dp", "seq"))

        def reduced(value, axis):
            piece = lax.psum_scatter(value, "dp", scatter_dimension=axis, tiled=True)
            return lax.psum(piece, "seq").astype(F32)

        down_sum = reduced(jnp.concatenate([down_near, down_far], axis=0).reshape(-1, D), 0)
        mixing_sum = reduced(middle_grad[:, :quarter].reshape(D, D), 0)
        up_quarters = middle_grad[:, quarter : 5 * quarter].reshape(4, 4, quarter, D)
        up_sum = reduced(jnp.transpose(up_quarters, (1, 0, 2, 3)).reshape(4, D, D), 1)
        up_out, from_sums = up_columns(up_sum), vector_outputs(sums)
        pair_sum = jnp.concatenate(
            [reduced(jnp.concatenate([a[0], b[0]], axis=1), 1) for a, b in zip(near, far)], axis=0
        )

    six_sum = jnp.transpose(pair_sum.reshape(PAIRS, share, 6, LANES), (2, 1, 0, 3)).reshape(6, share, D)
    mixing_bias_sum, gain_one, bias_one, up_bias_sum, down_bias_sum, gain_two, bias_two, stream_rms = from_sums
    return (
        layer_out,
        tokens_grad,
        six_sum[0:4],
        six_sum[4],
        six_sum[5],
        mixing_sum,
        mixing_bias_sum,
        gain_one,
        bias_one,
        up_out,
        up_bias_sum,
        down_sum,
        down_bias_sum,
        gain_two,
        bias_two,
        stream_rms,
    )


def solution(mesh):
    rows = P(("dp", "seq"), None)
    vector = P("dp")
    matrix = P("dp", None)
    stacked = P(None, "dp", None)
    in_specs = (
        rows, P(("dp", "seq")), stacked, matrix, matrix, matrix, vector, vector, vector, matrix,
        vector, matrix, vector, vector, vector, rows,
    )
    out_specs = (
        rows, rows, stacked, matrix, matrix, matrix, vector, vector, vector, matrix, vector,
        matrix, vector, vector, vector, P(),
    )
    return jax.shard_map(local, mesh=mesh, in_specs=in_specs, out_specs=out_specs, check_vma=False)
```
